256 devices in a mesh: img: 64 (over x, z, core), proto: 4 (over y).
Axes of the slice: x: 4, y: 4, z: 8, core: 2. Of those that a mesh axis runs over, the one named last changes fastest.
Arguments:
- student_feats: bfloat16 [64, 128, 384], P('img'), may hold values from -1 to 1
- teacher_feats: bfloat16 [64, 128, 384], P('img'), may hold values from -1 to 1
- student_weight: bfloat16 [384, 131072], P(None, ('img', 'proto')), may hold values from -1 to 1
- teacher_weight: bfloat16 [384, 131072], P(None, ('img', 'proto')), may hold values from -1 to 1
- patch_masks: int32 [64, 128], P('img'), may hold values from 0 to 1, as said below
Outputs:
- patch_loss: float32 [], replicated
- grad_weight: float32 [384, 131072], P(None, ('img', 'proto'))
- grad_rows: float32 [4096, 384], P(('img', 'proto'))
The draws below stay inside these ranges and needn't reach their ends.
Inputs may be any that keep to these rules, and one draw needn't show every extreme that they name: `patch_masks`: exactly 32 images have masked patches, chosen at random; a quarter of these each have 128 / 8, 32, 48 and 64 masked patches at random positions, so 1280 patches are masked in all.
All inputs are finite; a program needn't handle non-finite values.
Results may differ from the reference program's by a relative error of at most 0.0085.
Values may be sent and summed in bfloat16 or wider, within the bound.
A program may use at most 64 MiB of HBM per device.

```python
import math
import jax
import jax.numpy as jnp
from jax import lax

E = 384
P_SIZE = 131072
PATCH = 128
ITERS = 3
IMAGES = 64
ROWS = 1280
DEVICES = 256


def shared_directions(key):
    return jax.random.normal(jax.random.fold_in(key, 101), (8, E), jnp.float32)


def image_directions(key):
    return jax.random.normal(jax.random.fold_in(key, 102), (IMAGES, E), jnp.float32)


def head_columns(key, salt_value, tilted, mode):
    folded = jax.random.fold_in(key, salt_value)
    first_key, second_key, third_key = jax.random.split(folded, 3)
    mixing = jax.random.normal(first_key, (8, P_SIZE), jnp.float32) / math.sqrt(8.0)
    position = jnp.arange(P_SIZE, dtype=jnp.float32) / P_SIZE
    growth = 0.3 + 1.5 * position
    jitter = 0.6 * jax.random.normal(second_key, (E, P_SIZE), jnp.float32)
    tilt = 2.5 - 5.0 * position
    directions = shared_directions(key)
    base = jnp.dot(directions.T, mixing) * growth[None, :] + jitter
    if tilted:
        base = base + directions[0][:, None] * tilt[None, :]
    column_ids = jnp.arange(P_SIZE, dtype=jnp.int32)
    if mode == 1:
        owner = (column_ids * IMAGES // P_SIZE + IMAGES // 2) % IMAGES
        base = base + 2.5 * image_directions(key)[owner].T
    if mode == 2:
        block_width = max(P_SIZE // DEVICES, 1)
        owner = column_ids // block_width % IMAGES
        base = base + 2.5 * image_directions(key)[owner].T
    spread = jnp.exp(jax.random.uniform(third_key, (1, P_SIZE), jnp.float32, math.log(0.1), 0.0))
    columns = base * spread / math.sqrt(E)
    return jnp.clip(columns, -1.0, 1.0).astype(jnp.bfloat16)


def patch_features(key, salt_value, aligned):
    folded = jax.random.fold_in(key, salt_value)
    first_key, second_key, third_key = jax.random.split(folded, 3)
    mixing = jax.random.normal(first_key, (IMAGES, PATCH, 8), jnp.float32) / math.sqrt(8.0)
    directions = shared_directions(key)
    anchor = jnp.einsum('ipa,ae->ipe', mixing, directions) + 1.5 * directions[0][None, None, :]
    if aligned:
        anchor = anchor + 2.5 * image_directions(key)[:, None, :]
    jitter = 0.5 * jax.random.normal(second_key, (IMAGES, PATCH, E), jnp.float32)
    spread = jnp.exp(jax.random.uniform(third_key, (IMAGES, PATCH, 1), jnp.float32, math.log(0.03), math.log(0.3)))
    values = (anchor + jitter) * spread / math.sqrt(E)
    return jnp.clip(values, -1.0, 1.0).astype(jnp.bfloat16)


def draw_student_feats(key, part):
    return patch_features(key, 201, True)


def draw_teacher_feats(key, part):
    return patch_features(key, 202, True)


def draw_student_weight(key, part):
    return head_columns(key, 211, True, 1)


def draw_teacher_weight(key, part):
    return head_columns(key, 212, False, 2)


def draw_patch_masks(key, part):
    folded = jax.random.fold_in(key, 301)
    shuffled = jax.random.permutation(jax.random.fold_in(folded, 1), IMAGES)
    rank_of = jnp.argsort(shuffled).astype(jnp.int32)
    counts = jnp.where(rank_of < IMAGES // 2, PATCH // 8 * (1 + rank_of % 4), 0)
    image_keys = jax.random.split(jax.random.fold_in(folded, 2), IMAGES)

    def patch_order(image_key):
        return jnp.argsort(jax.random.permutation(image_key, PATCH)).astype(jnp.int32)
    places = jax.vmap(patch_order)(image_keys)
    return (places < counts[:, None]).astype(jnp.int32)


def setup_inputs(seed: int = 0) -> dict:
    seeds = jax.random.split(jax.random.key(seed), 6)
    return {
        "student_feats": draw_student_feats(jax.random.fold_in(seeds[5], 71), 0),
        "teacher_feats": draw_teacher_feats(jax.random.fold_in(seeds[5], 71), 0),
        "student_weight": draw_student_weight(jax.random.fold_in(seeds[5], 71), 0),
        "teacher_weight": draw_teacher_weight(jax.random.fold_in(seeds[5], 71), 0),
        "patch_masks": draw_patch_masks(jax.random.fold_in(seeds[5], 71), 0),
    }


TEACHER_TEMP = 0.07
STUDENT_TEMP = 0.1
NORM_EPS = 1e-06

def slot_rows(features, mask_rows, slot_count):
    rank_of = jnp.cumsum(mask_rows, axis=1) - 1
    slot_ids = jnp.arange(slot_count, dtype=jnp.int32)
    select = ((mask_rows[:, None, :] == 1) & (rank_of[:, None, :] == slot_ids[None, :, None])).astype(jnp.float32)
    return jnp.einsum('isp,ipe->ise', select, features.astype(jnp.float32))

def unit_rows(slot_data):
    norm_rows = jnp.sqrt(lax.optimization_barrier(jnp.sum(slot_data * slot_data, axis=-1)) + NORM_EPS)
    return ((slot_data / norm_rows[..., None]).astype(jnp.bfloat16), norm_rows)

def unit_columns(weight):
    w_float = weight.astype(jnp.float32)
    norm_cols = jnp.sqrt(lax.optimization_barrier(jnp.sum(w_float * w_float, axis=0)) + NORM_EPS)
    return ((w_float / norm_cols[None, :]).astype(jnp.bfloat16), norm_cols)

def reference(student_feats, teacher_feats, student_weight, teacher_weight, patch_masks):
    slot_count = PATCH // 2
    counts = lax.optimization_barrier(jnp.sum(patch_masks, axis=1))
    valid_slot = (jnp.arange(slot_count, dtype=jnp.int32)[None, :] < counts[:, None]).reshape(-1)
    packed_ids = jnp.nonzero(valid_slot, size=ROWS)[0].astype(jnp.int32)
    stu_unit, stu_norm = unit_rows(slot_rows(student_feats, patch_masks, slot_count).reshape(-1, E)[packed_ids])
    tea_unit, _ = unit_rows(slot_rows(teacher_feats, patch_masks, slot_count).reshape(-1, E)[packed_ids])
    count_f = counts.astype(jnp.float32)
    masked_images = jnp.sum((counts > 0).astype(jnp.float32))
    row_weight = 1.0 / (jnp.repeat(jnp.maximum(count_f, 1.0), slot_count)[packed_ids] * masked_images)
    w_unit, w_norm = unit_columns(student_weight)
    tea_w_unit, _ = unit_columns(teacher_weight)
    block_width = min(P_SIZE, 8192)
    blocks = P_SIZE // block_width
    stu_blocks = w_unit.reshape(E, blocks, block_width).transpose(1, 0, 2)
    tea_blocks = tea_w_unit.reshape(E, blocks, block_width).transpose(1, 0, 2)

    def kernel_block(w_block):
        return jnp.exp(jnp.dot(tea_unit, w_block, preferred_element_type=jnp.float32) / TEACHER_TEMP)

    def total_block(w_block):
        logits = jnp.dot(stu_unit, w_block, preferred_element_type=jnp.float32) / STUDENT_TEMP
        return lax.optimization_barrier(jnp.sum(jnp.exp(logits), axis=1))
    kernel = lax.map(kernel_block, tea_blocks)
    partition = lax.optimization_barrier(jnp.sum(lax.map(total_block, stu_blocks), axis=0))
    row_scale = jnp.ones((ROWS,), jnp.float32)
    col_scale = jnp.ones((blocks, block_width), jnp.float32)
    for sweep_idx in range(ITERS):
        col_scale = 1.0 / jnp.einsum('r,nrb->nb', row_scale, kernel, precision=lax.Precision.HIGHEST)
        row_scale = 1.0 / jnp.einsum('nrb,nb->r', kernel, col_scale, precision=lax.Precision.HIGHEST)
    log_part = jnp.log(partition)
    scaled_weight = row_weight * ROWS

    def final_block(running, pieces):
        w_block, k_block, c_block = pieces
        logits = jnp.dot(stu_unit, w_block, preferred_element_type=jnp.float32) / STUDENT_TEMP
        targets = row_scale[:, None] * k_block * c_block[None, :]
        loss_piece = jnp.sum(row_weight * lax.optimization_barrier(jnp.sum(targets * (log_part[:, None] - logits), axis=1)))
        probability = jnp.exp(logits) / partition[:, None]
        grad_logits = (scaled_weight[:, None] * (probability - targets) / STUDENT_TEMP).astype(jnp.bfloat16)
        grad_unit_w = lax.dot_general(stu_unit, grad_logits, (((0,), (0,)), ((), ())), preferred_element_type=jnp.float32)
        grad_unit_x = lax.dot_general(grad_logits, w_block, (((1,), (1,)), ((), ())), preferred_element_type=jnp.float32)
        return ((running[0] + loss_piece, running[1] + grad_unit_x), grad_unit_w)
    start_carry = (jnp.zeros((), jnp.float32), jnp.zeros((ROWS, E), jnp.float32))
    (patch_loss, grad_unit_x), grad_w_blocks = lax.scan(final_block, start_carry, (stu_blocks, kernel, col_scale))
    grad_unit_w = grad_w_blocks.transpose(1, 0, 2).reshape(E, P_SIZE)
    w_float = w_unit.astype(jnp.float32)
    grad_weight = P_SIZE / 128.0 * (grad_unit_w - w_float * lax.optimization_barrier(jnp.sum(w_float * grad_unit_w, axis=0))[None, :]) / w_norm[None, :]
    unit_float = stu_unit.astype(jnp.float32)
    grad_x = (grad_unit_x - unit_float * lax.optimization_barrier(jnp.sum(unit_float * grad_unit_x, axis=1))[:, None]) / stu_norm[:, None]
    grad_rows = jnp.zeros((IMAGES * slot_count, E), jnp.float32).at[packed_ids].set(grad_x)
    return (patch_loss, grad_weight, grad_rows)
```

```python
import jax
import jax.numpy as jnp
from jax import lax
from jax.experimental import pallas as pl
from jax.experimental.pallas import tpu as pltpu
from jax.sharding import PartitionSpec as P

MESH = pl.DeviceIdType.MESH
F32, BF16 = jnp.float32, jnp.bfloat16
TEACHER_TEMP = 0.07
STUDENT_TEMP = 0.1
NORM_EPS = 1e-06
ROWS, COLS, E, ITERS = 1280, 512, 384, 3
BLK = 64
GROUPS = [(b, m) for b in range(4) for m in range(b + 1, 5)]
ROW_W = [1.0 / (16.0 * m * 32.0) for _, m in GROUPS]


def square_at(s):
    return 4 * (s % 4) + s // 4 if s < 16 else s


def split_square(o):
    kp = lax.div(o, 3)
    f = lax.rem(o, 3)
    b = lax.div(kp + 4, 8) + lax.div(kp + 1, 8) + lax.div(kp, 9)
    first = 4 * b - lax.div(b * (b - 1), 2)
    return kp, f, b, kp - first, kp - first + b + 1


def dot(a, b):
    return jnp.dot(a, b, preferred_element_type=F32)


def dot_nt(a, b):
    return lax.dot_general(a, b, (((1,), (1,)), ((), ())), preferred_element_type=F32)


def fold8(v):
    return jnp.sum(v.reshape(v.shape[0] // 8, 8, v.shape[1]), axis=0)


def kernel(
    sf, tf, sw, tw, mask,
    loss_ref, gw_ref, gr_ref,
    units, unit_f, norm_f, cnt, raw, rawc, sel, grid, tea, stu,
    w_unit, w_t, tw_t, w_norm, kt, lg, ex, gb, csum,
    a0, b0, c0, a1, b1, c1, a2, b2, c2,
    pt, core_in, summed, in_a0, in_a1, half0, half1, in_b0, in_b1, quart, in_z,
    scale, tiles, back,
    s_raw, s_cnt, r_raw, r_cnt, s_z, r_z, s_2, r_2, s_3, r_3, s_ex, r_ex,
    s_ar, r_ar, s_core, r_core, s_ra, r_ra, s_rb, r_rb, s_rz, r_rz, s_back, r_back,
):
    img = lax.axis_index("img")
    y = lax.axis_index("proto")
    c = lax.rem(img, 2)
    z = lax.rem(lax.div(img, 2), 8)
    x = lax.div(img, 16)
    is_owner = lax.rem(z, 4) == x
    h_me = lax.div(z, 4)
    o_me = 16 * h_me + 4 * x + y
    s_me = jnp.where(h_me == 0, 4 * y + x, o_me)

    def at(px, py, pz, pc):
        return ((px * 8 + pz) * 2 + pc, py)

    def x_peer(j):
        return at(lax.rem(x + j, 4), y, z, c)

    def y_peer(j):
        return at(x, lax.rem(y + j, 4), z, c)

    def z_peer(j):
        return at(x, y, lax.rem(z + j, 8), c)

    def cy_peer(j):
        g = lax.rem(c * 4 + y + j, 8)
        return at(x, lax.rem(g, 4), z, lax.div(g, 4))

    partner = at(x, y, z, 1 - c)

    def remote(src, dst, s, r, dev):
        return pltpu.make_async_remote_copy(
            src_ref=src, dst_ref=dst, send_sem=s, recv_sem=r, device_id=dev, device_id_type=MESH
        )

    bar = pltpu.get_barrier_semaphore()

    def greet(dev):
        pl.semaphore_signal(bar, inc=1, device_id=dev, device_id_type=MESH)

    for j in range(1, 4):
        greet(x_peer(j))
    for j in range(1, 8):
        greet(z_peer(j))
        greet(cy_peer(j))

    @pl.when(is_owner)
    def _():
        @pl.loop(0, 64)
        def _(i):
            @pl.when(i != img)
            def _():
                greet((i, y))

    mrow = mask[...].astype(F32)
    upper = (
        lax.broadcasted_iota(jnp.int32, (128, 128), 0) <= lax.broadcasted_iota(jnp.int32, (128, 128), 1)
    ).astype(BF16)
    mrow8 = jnp.broadcast_to(mrow, (8, 128))
    rank = dot(mrow8.astype(BF16), upper)
    cnt[...] = jnp.broadcast_to(jnp.sum(mrow, axis=1, keepdims=True), (1, 128))
    want = lax.broadcasted_iota(jnp.int32, (64, 128), 0).astype(F32)
    pick = jnp.where(
        (jnp.broadcast_to(rank[:1], (64, 128)) - 1.0 == want)
        & (jnp.broadcast_to(mrow, (64, 128)) > 0.5), 1.0, 0.0
    ).astype(BF16)

    def unit_rows(kind, feats):
        rows = dot(pick, feats[0])
        norm = jnp.sqrt(jnp.sum(rows * rows, axis=1, keepdims=True) + NORM_EPS)
        unit = (rows / norm).astype(BF16)
        for b in range(4):
            for f in range(3):
                units[kind, b, f] = unit[16 * b:16 * b + 16, 128 * f:128 * f + 128]
        return unit, norm

    s_unit, s_norm = unit_rows(0, sf)
    unit_rows(1, tf)
    for b in range(4):
        unit_f[b] = s_unit[16 * b:16 * b + 16].astype(F32)
        norm_f[b] = jnp.broadcast_to(s_norm[16 * b:16 * b + 16], (16, 128))

    @pl.when(is_owner)
    def _():
        pl.semaphore_wait(bar, 17 + 15)

    @pl.when(jnp.logical_not(is_owner))
    def _():
        pl.semaphore_wait(bar, 17 + 16)

    def each_owner(remote_fn, local_fn):
        for h in range(2):
            for px in range(4):
                for pc in range(2):
                    t = (h * 4 + px) * 2 + pc
                    to = (px * 8 + px + 4 * h) * 2 + pc
                    _, f, b, _, _ = split_square(16 * h + 4 * px + y)

                    @pl.when(img != to)
                    def _():
                        remote_fn(t, to, pc, b, f)

                    if local_fn is not None:
                        @pl.when(img == to)
                        def _():
                            local_fn(pc, b, f)

    def raw_copies(t, to, pc, b, f):
        return (
            remote(cnt, rawc.at[img], s_cnt.at[t], r_cnt, (to, y)),
            remote(units.at[pc, b, f], raw.at[img], s_raw.at[t], r_raw, (to, y)),
        )

    def raw_start(*a):
        for cp in raw_copies(*a):
            cp.start()

    def raw_done(*a):
        for cp in raw_copies(*a):
            cp.wait_send()

    def raw_local(pc, b, f):
        pltpu.make_async_copy(cnt, rawc.at[img], r_cnt).start()
        pltpu.make_async_copy(units.at[pc, b, f], raw.at[img], r_raw).start()

    each_owner(raw_start, raw_local)

    def unit_columns(w_ref):
        w = w_ref[...].astype(F32)
        norm = jnp.sqrt(jnp.sum(w * w, axis=0, keepdims=True) + NORM_EPS)
        return w / norm, norm

    tw_u, _ = unit_columns(tw)
    tw_t[...] = tw_u.T.astype(BF16)
    sw_u, sw_n = unit_columns(sw)
    w_norm[...] = sw_n
    w_unit[...] = sw_u.astype(BF16)
    w_t[...] = sw_u.T.astype(BF16)

    kp_me, f_me, b_me, k_me, m_me = split_square(o_me)

    def z_copy(j):
        return remote(grid.at[c, s_me], grid.at[c, s_me], s_z.at[j - 1], r_z.at[h_me], z_peer(j))

    @pl.when(is_owner)
    def _():
        pltpu.make_async_copy(rawc, rawc, r_cnt).wait()
        counts = rawc[:, 0, :]
        match = jnp.where(counts == (16 * m_me).astype(F32), 1.0, 0.0)
        lower = (
            lax.broadcasted_iota(jnp.int32, (64, 64), 1) < lax.broadcasted_iota(jnp.int32, (64, 64), 0)
        ).astype(BF16)
        place = jnp.where(match > 0.5, dot(lower, match.astype(BF16)), -1.0)
        lane_block = lax.shift_right_logical(lax.broadcasted_iota(jnp.int32, (64, 128), 1), 4)
        block_sel = jnp.where(place == lane_block.astype(F32), 1.0, 0.0).astype(BF16)
        spread = (
            lax.shift_right_logical(lax.broadcasted_iota(jnp.int32, (1024, 64), 0), 4)
            == lax.broadcasted_iota(jnp.int32, (1024, 64), 1)
        ).astype(BF16)
        same_row = (
            lax.bitwise_and(lax.broadcasted_iota(jnp.int32, (1024, 128), 0), 15)
            == lax.bitwise_and(lax.broadcasted_iota(jnp.int32, (1024, 128), 1), 15)
        )
        sel_f = jnp.where(same_row, dot(spread, block_sel), 0.0)
        sel[...] = sel_f
        sel_t = sel_f.T.astype(BF16)
        pltpu.make_async_copy(raw, raw, r_raw).wait()
        grid[c, s_me] = dot(sel_t, raw[...].reshape(1024, 128)).astype(BF16)
        for j in range(1, 8):
            z_copy(j).start()

    for h in range(2):
        spot = 4 * y + x if h == 0 else 16 + 4 * x + y

        @pl.when(z != x + 4 * h)
        def _():
            remote(grid.at[c, spot], grid.at[c, spot], s_z.at[0], r_z.at[h], partner).wait_recv()

    def copy2(h, j, back_j=0):
        if h == 0:
            spot = 4 * y + lax.rem(x + back_j, 4)
            dev = x_peer(j)
        else:
            spot = 16 + 4 * x + lax.rem(y + back_j, 4)
            dev = y_peer(j)
        return remote(grid.at[c, spot], grid.at[c, spot], s_2.at[h, j - 1], r_2.at[h, j - 1], dev)

    def run4(h, off):
        return pl.ds(4 * lax.rem(y + off, 4), 4) if h == 0 else pl.ds(16 + 4 * lax.rem(x + off, 4), 4)

    def copy3(h, j, back_j=0):
        run = run4(h, back_j)
        dev = y_peer(j) if h == 0 else x_peer(j)
        return remote(grid.at[c, run], grid.at[c, run], s_3.at[h, j - 1], r_3.at[h, j - 1], dev)

    def copy_ex(h, j, kind):
        run = run4(h, (4 - j) % 4)
        return remote(grid.at[kind, run], grid.at[kind, run], s_ex.at[h, j], r_ex.at[h, j], partner)

    for j in range(1, 4):
        copy2(0, j).start()
        copy2(1, j).start()
    for h in range(2):
        for j in range(1, 4):
            copy2(h, j, 4 - j).wait_recv()
        for j in range(1, 4):
            copy3(h, j).start()
    copy_ex(0, 0, c).start()
    copy_ex(1, 0, c).start()
    for j in range(1, 4):
        for h in range(2):
            copy3(h, j, 4 - j).wait_recv()
            copy_ex(h, j, c).start()
    for h in range(2):
        for j in range(4):
            copy_ex(h, j, 1 - c).wait_recv()

    for kind, feats in ((1, tea), (0, stu)):
        for s in range(30):
            o = square_at(s)
            kp, f = o // 3, o % 3
            feats[128 * kp:128 * kp + 128, 128 * f:128 * f + 128] = grid[kind, s]

    for n in range(5):
        cols = slice(256 * n, 256 * n + 256)
        k_blk = jnp.exp(dot_nt(tw_t[...], tea[cols, :]) * (1.0 / TEACHER_TEMP))
        kt[:, cols] = k_blk
        part = k_blk[:, :128] + k_blk[:, 128:]
        csum[...] = part if n == 0 else csum[...] + part
    zero8 = jnp.zeros((8, ROWS), F32)

    def first_sweep(i, acc):
        rows = pl.ds(pl.multiple_of(i * BLK, BLK), BLK)
        col = 1.0 / jnp.sum(csum[rows, :], axis=1, keepdims=True)
        return acc + fold8(kt[rows, :] * col)

    def fold1(acc):
        return jnp.sum(acc, axis=0, keepdims=True)

    tot = fold1(lax.fori_loop(0, COLS // BLK, first_sweep, zero8))

    stages = ((a0, b0, c0), (a1, b1, c1), (a2, b2, c2))
    spots = (c * 4 + y, x, z)
    sizes = (8, 4, 8)
    sem_at = (0, 7, 10)

    def ar_copy(it, st, j):
        ref = stages[it][st]
        peer = (cy_peer, x_peer, z_peer)[st](j)
        n = sem_at[st] + j - 1
        return remote(ref.at[spots[st]], ref.at[spots[st]], s_ar.at[it, n], r_ar.at[it, n], peer)

    def all_sum(it, v, fillers):
        for st in range(3):
            ref = stages[it][st]
            ref[spots[st]] = v
            for j in range(1, sizes[st]):
                ar_copy(it, st, j).start()
            fillers[st]()
            for j in range(1, sizes[st]):
                ar_copy(it, st, j).wait_recv()
            v = ref[0]
            for k in range(1, sizes[st]):
                v = v + ref[k]
        return v

    def all_sum_sent(it):
        for st in range(3):
            for j in range(1, sizes[st]):
                ar_copy(it, st, j).wait_send()

    parts = []

    def student(ns):
        for n in ns:
            cols = slice(256 * n, 256 * n + 256)
            l_blk = dot_nt(w_t[...], stu[cols, :]) * (1.0 / STUDENT_TEMP)
            lg[:, cols] = l_blk
            e_blk = jnp.exp(l_blk)
            ex[:, cols] = e_blk
            parts.append(jnp.sum(e_blk, axis=0, keepdims=True))

    def products(kind, src):
        for n in range(5):
            cols = slice(256 * n, 256 * n + 256)
            p_blk = dot(w_unit[...], src[:, cols].astype(BF16)).astype(BF16)
            for s in range(30):
                o = square_at(s)
                kp, f = o // 3, o % 3
                if kp // 2 == n:
                    lo = 128 * (kp % 2)
                    pt[kind, s] = p_blk[128 * f:128 * f + 128, lo:lo + 128]

    total = all_sum(
        0, tot, (lambda: student((0, 1)), lambda: student((2,)), lambda: student((3, 4)))
    )
    row = 1.0 / total

    def sweep(i, acc):
        rows = pl.ds(pl.multiple_of(i * BLK, BLK), BLK)
        k_blk = kt[rows, :]
        col = 1.0 / jnp.sum(k_blk * row, axis=1, keepdims=True)
        return acc + fold8(k_blk * col)

    tot = fold1(lax.fori_loop(0, COLS // BLK, sweep, zero8))
    part_mine = jnp.concatenate(parts, axis=1)

    def empty_squares():
        for kind in range(2):
            for s in (30, 31):
                pt[kind, s] = jnp.zeros((128, 128), BF16)

    total = all_sum(
        1, jnp.concatenate([tot, part_mine], axis=1),
        (lambda: products(0, ex), empty_squares, lambda: None),
    )
    row = 1.0 / total[:, :ROWS]
    partition = total[:, ROWS:]

    def last_sweep(i, acc):
        rows = pl.ds(pl.multiple_of(i * BLK, BLK), BLK)
        k_blk = kt[rows, :]
        col = 1.0 / jnp.sum(k_blk * row, axis=1, keepdims=True)
        k_blk = k_blk * col
        kt[rows, :] = k_blk
        return acc[0] + fold8(k_blk), acc[1] + fold8(k_blk * lg[rows, :])

    acc_k, acc_l = lax.fori_loop(0, COLS // BLK, last_sweep, (zero8, zero8))

    core_copy = remote(pt.at[1 - c], core_in, s_core, r_core, partner)

    def copy_ra(h, j):
        run = run4(h, j)
        dst = (in_a0, in_a1)[h]
        dev = y_peer(j) if h == 0 else x_peer(j)
        return remote(summed.at[run], dst.at[j - 1], s_ra.at[h, j - 1], r_ra.at[h, j - 1], dev)

    def copy_rb(h, j):
        src = (half0, half1)[h]
        dst = (in_b0, in_b1)[h]
        dev = x_peer(j) if h == 0 else y_peer(j)
        spot = lax.rem((x if h == 0 else y) + j, 4)
        return remote(src.at[spot], dst.at[j - 1], s_rb.at[h, j - 1], r_rb.at[h, j - 1], dev)

    def copy_rz(h):
        away = lax.rem(x + 4 * h - z + 8, 8)
        slot = jnp.maximum(away - 1, 0)
        return remote(
            quart.at[h], in_z.at[slot], s_rz.at[h], r_rz.at[slot], at(x, y, x + 4 * h, c)
        )

    def teacher_products():
        products(1, kt)
        core_copy.start()

    def core_sum():
        core_copy.wait_recv()

        @pl.loop(0, 32)
        def _(s):
            summed[s] = (pt[c, s].astype(F32) + core_in[s].astype(F32)).astype(BF16)

        for j in range(1, 4):
            copy_ra(0, j).start()
            copy_ra(1, j).start()

    total = all_sum(
        2, jnp.concatenate([fold1(acc_k), fold1(acc_l)], axis=1),
        (teacher_products, core_sum, lambda: None),
    )
    row = 1.0 / total[:, :ROWS]
    row_w = jnp.concatenate([jnp.full((1, 128), w, F32) for w in ROW_W], axis=1)
    loss = jnp.sum(
        row_w * (jnp.log(partition) - row * total[:, ROWS:]), axis=1, keepdims=True
    )
    loss_ref[...] = loss
    lead = row_w * (ROWS / STUDENT_TEMP)
    scale_p = lead / partition
    scale_t = lead * row
    for kp in range(10):
        scale[0, kp] = scale_p[:, 128 * kp:128 * kp + 128]
        scale[1, kp] = -scale_t[:, 128 * kp:128 * kp + 128]
    scale[0, 10] = jnp.zeros((1, 128), F32)
    scale[1, 10] = jnp.zeros((1, 128), F32)

    for h in range(2):
        for j in range(1, 4):
            copy_ra(h, j).wait_recv()
        own = run4(h, 0)
        got = (in_a0, in_a1)[h]
        v = summed[own].astype(F32)
        for j in range(3):
            v = v + got[j].astype(F32)
        (half0, half1)[h][...] = v.astype(BF16)
        for j in range(1, 4):
            copy_rb(h, j).start()

    @pl.loop(0, COLS // BLK)
    def _(i):
        rows = pl.ds(pl.multiple_of(i * BLK, BLK), BLK)
        gb[rows, :] = (ex[rows, :] * scale_p - kt[rows, :] * scale_t).astype(BF16)

    for h in range(2):
        for j in range(1, 4):
            copy_rb(h, j).wait_recv()
        own = x if h == 0 else y
        got = (in_b0, in_b1)[h]
        v = (half0, half1)[h][own].astype(F32)
        for j in range(3):
            v = v + got[j].astype(F32)
        quart[h] = v.astype(BF16)

        @pl.when(z != x + 4 * h)
        def _():
            copy_rz(h).start()

    gu = dot(gb[...], stu[...]).T
    w_f = w_unit[...].astype(F32)
    gw_ref[...] = (
        1024.0 * (gu - w_f * jnp.sum(w_f * gu, axis=0, keepdims=True)) / w_norm[...]
    )

    sends_back = is_owner & (o_me < 30)

    def copy_back(i):
        return remote(
            tiles.at[i], back.at[k_me, f_me, c], s_back.at[i], r_back, (i, b_me)
        )

    @pl.when(is_owner)
    def _():
        for j in range(1, 8):
            remote(quart.at[0], in_z.at[j - 1], s_rz.at[0], r_rz.at[j - 1], partner).wait_recv()

    @pl.when(sends_back)
    def _():
        v = quart[h_me].astype(F32)
        for j in range(7):
            v = v + in_z[j].astype(F32)
        v = (v * scale[c, kp_me]).T
        t = jnp.dot(sel[...], v, precision=lax.Precision.HIGHEST, preferred_element_type=F32)
        tiles[...] = t.reshape(64, 16, 128)

        @pl.loop(0, 64)
        def _(i):
            mine = (i == img) & (b_me == y)

            @pl.when(jnp.logical_not(mine))
            def _():
                copy_back(i).start()

            @pl.when(mine)
            def _():
                pltpu.make_async_copy(tiles.at[i], back.at[k_me, f_me, c], r_back).start()

    for b in range(4):
        @pl.when(y == b)
        def _():
            got = back.at[pl.ds(0, 4 - b)]
            pltpu.make_async_copy(got, got, r_back).wait()
            for k in range(4 - b, 4):
                back[k] = jnp.zeros((3, 2, 16, 128), F32)

    cols = []
    for f in range(3):
        v = back[0, f, 0]
        for k in range(4):
            for kind in range(2):
                if k or kind:
                    v = v + back[k, f, kind]
        cols.append(v)
    gx = jnp.concatenate(cols, axis=1)
    u = unit_f[y]
    gr_ref[...] = (gx - u * jnp.sum(u * gx, axis=1, keepdims=True)) / norm_f[y][:, :1]

    each_owner(raw_done, None)

    @pl.when(is_owner)
    def _():
        for j in range(1, 8):
            z_copy(j).wait_send()

    for h in range(2):
        for j in range(1, 4):
            copy2(h, j).wait_send()
            copy3(h, j).wait_send()
            copy_ra(h, j).wait_send()
            copy_rb(h, j).wait_send()
        for j in range(4):
            copy_ex(h, j, c).wait_send()

        @pl.when(z != x + 4 * h)
        def _():
            copy_rz(h).wait_send()

    for it in range(3):
        all_sum_sent(it)
    core_copy.wait_send()

    @pl.when(sends_back)
    def _():
        @pl.loop(0, 64)
        def _(i):
            @pl.when(jnp.logical_not((i == img) & (b_me == y)))
            def _():
                copy_back(i).wait_send()


def shards(student_feats, teacher_feats, student_weight, teacher_weight, patch_masks):
    vmem = pl.BlockSpec(memory_space=pltpu.VMEM)
    dma = pltpu.SemaphoreType.DMA

    def sums(width):
        return [pltpu.VMEM((n, 1, width), F32) for n in (8, 4, 8)]

    scratch = [
        pltpu.VMEM((2, 4, 3, 16, 128), BF16),
        pltpu.VMEM((4, 16, E), F32),
        pltpu.VMEM((4, 16, 128), F32),
        pltpu.VMEM((1, 128), F32),
        pltpu.VMEM((64, 16, 128), BF16),
        pltpu.VMEM((64, 1, 128), F32),
        pltpu.VMEM((1024, 128), F32),
        pltpu.VMEM((2, 32, 128, 128), BF16),
        pltpu.VMEM((ROWS, E), BF16),
        pltpu.VMEM((ROWS, E), BF16),
        pltpu.VMEM((E, COLS), BF16),
        pltpu.VMEM((COLS, E), BF16),
        pltpu.VMEM((COLS, E), BF16),
        pltpu.VMEM((1, COLS), F32),
        pltpu.VMEM((COLS, ROWS), F32),
        pltpu.VMEM((COLS, ROWS), F32),
        pltpu.VMEM((COLS, ROWS), F32),
        pltpu.VMEM((COLS, ROWS), BF16),
        pltpu.VMEM((COLS, 128), F32),
        *sums(ROWS), *sums(2 * ROWS), *sums(2 * ROWS),
        pltpu.VMEM((2, 32, 128, 128), BF16),
        pltpu.VMEM((32, 128, 128), BF16),
        pltpu.VMEM((32, 128, 128), BF16),
        pltpu.VMEM((3, 4, 128, 128), BF16),
        pltpu.VMEM((3, 4, 128, 128), BF16),
        pltpu.VMEM((4, 128, 128), BF16),
        pltpu.VMEM((4, 128, 128), BF16),
        pltpu.VMEM((3, 128, 128), BF16),
        pltpu.VMEM((3, 128, 128), BF16),
        pltpu.VMEM((2, 128, 128), BF16),
        pltpu.VMEM((7, 128, 128), BF16),
        pltpu.VMEM((2, 11, 1, 128), F32),
        pltpu.VMEM((64, 16, 128), F32),
        pltpu.VMEM((4, 3, 2, 16, 128), F32),
        dma((16,)), dma((16,)), dma, dma,
        dma((7,)), dma((2,)),
        dma((2, 3)), dma((2, 3)), dma((2, 3)), dma((2, 3)), dma((2, 4)), dma((2, 4)),
        dma((3, 17)), dma((3, 17)),
        dma, dma,
        dma((2, 3)), dma((2, 3)), dma((2, 3)), dma((2, 3)), dma((2,)), dma((7,)),
        dma((64,)), dma,
    ]
    loss, grad_weight, grad_rows = pl.pallas_call(
        kernel,
        out_shape=(
            jax.ShapeDtypeStruct((1, 1), F32),
            jax.ShapeDtypeStruct((E, COLS), F32),
            jax.ShapeDtypeStruct((16, E), F32),
        ),
        in_specs=[vmem] * 5,
        out_specs=(vmem, vmem, vmem),
        scratch_shapes=scratch,
        compiler_params=pltpu.CompilerParams(collective_id=0, has_side_effects=True),
    )(student_feats, teacher_feats, student_weight, teacher_weight, patch_masks)
    return loss.reshape(()), grad_weight, grad_rows


def solution(mesh):
    placed = (
        P("img", None, None),
        P("img", None, None),
        P(None, ("img", "proto")),
        P(None, ("img", "proto")),
        P("img", None),
    )
    return jax.shard_map(
        shards,
        mesh=mesh,
        in_specs=placed,
        out_specs=(P(), P(None, ("img", "proto")), P(("img", "proto"), None)),
        check_vma=False,
    )
```

```python
import jax
import jax.numpy as jnp
from jax import lax
from jax.experimental import pallas as pl
from jax.experimental.pallas import tpu as pltpu
from jax.sharding import PartitionSpec as P

MESH = pl.DeviceIdType.MESH
F32, BF16 = jnp.float32, jnp.bfloat16
TEACHER_TEMP = 0.07
STUDENT_TEMP = 0.1
NORM_EPS = 1e-06
ROWS, COLS, E, ITERS = 1280, 512, 384, 3
BLK = 128
GROUPS = [(b, m) for b in range(4) for m in range(b + 1, 5)]
ROW_W = [1.0 / (16.0 * m * 32.0) for _, m in GROUPS]


def square_at(s):
    return 4 * (s % 4) + s // 4 if s < 16 else s


def split_square(o):
    kp = lax.div(o, 3)
    f = lax.rem(o, 3)
    b = lax.div(kp + 4, 8) + lax.div(kp + 1, 8) + lax.div(kp, 9)
    first = 4 * b - lax.div(b * (b - 1), 2)
    return kp, f, b, kp - first, kp - first + b + 1


def dot(a, b):
    return jnp.dot(a, b, preferred_element_type=F32)


def dot_nt(a, b):
    return lax.dot_general(a, b, (((1,), (1,)), ((), ())), preferred_element_type=F32)


def fold8(v):
    return jnp.sum(v.reshape(v.shape[0] // 8, 8, v.shape[1]), axis=0)


def kernel(
    sf_hbm, tf_hbm, sw_hbm, tw_hbm, mask_hbm,
    loss_hbm, gw_ref, gr_ref,
    sf, tf, sw, tw, mask, loss_ref,
    units, unit_f, norm_f, cnt, raw, rawc, sel, grid, tea, stu,
    w_unit, w_t, tw_t, w_norm, kt, lg, ex, gb, csum,
    ar_v, ar_a, ar_b, ls_a, ls_b,
    pt, core_in, summed, in_a0, in_a1, half0, half1, in_b0, in_b1, quart, in_z,
    scale, whole, tiles, back,
    s_raw, s_cnt, r_raw, r_cnt, s_z, r_z, s_2, r_2, s_3, r_3, s_ex, r_ex,
    s_ara, r_ara, s_arb, r_arb, s_lsa, r_lsa, s_lsb, r_lsb, s_core, r_core, s_ra, r_ra, s_rb, r_rb, s_rz, r_rz, s_pair, r_pair, s_back, r_back, s_in, s_loss,
):
    img = lax.axis_index("img")
    y = lax.axis_index("proto")
    c = lax.rem(img, 2)
    z = lax.rem(lax.div(img, 2), 8)
    x = lax.div(img, 16)
    is_owner = lax.rem(z, 4) == x
    h_me = lax.div(z, 4)
    o_me = 16 * h_me + 4 * x + y
    s_me = jnp.where(h_me == 0, 4 * y + x, o_me)

    def at(px, py, pz, pc):
        return ((px * 8 + pz) * 2 + pc, py)

    def x_peer(j):
        return at(lax.rem(x + j, 4), y, z, c)

    def y_peer(j):
        return at(x, lax.rem(y + j, 4), z, c)

    def z_peer(j):
        return at(x, y, lax.rem(z + j, 8), c)

    zc, xy = z * 2 + c, x * 4 + y

    def zc_peer(j):
        g = lax.rem(zc + j, 16)
        return at(x, y, lax.div(g, 2), lax.rem(g, 2)), lax.rem(g, 2)

    def xyc_peer(j):
        g = lax.rem(xy * 2 + c + j, 32)
        return at(lax.div(g, 8), lax.rem(lax.div(g, 2), 4), z, lax.rem(g, 2))

    def xy_peer(j):
        g = lax.rem(xy + j, 16)
        return at(lax.div(g, 4), lax.rem(g, 4), z, c)

    partner = at(x, y, z, 1 - c)

    def remote(src, dst, s, r, dev):
        return pltpu.make_async_remote_copy(
            src_ref=src, dst_ref=dst, send_sem=s, recv_sem=r, device_id=dev, device_id_type=MESH
        )

    loads = [
        pltpu.make_async_copy(src, dst, s_in.at[n])
        for n, (src, dst) in enumerate(
            ((mask_hbm, mask), (tf_hbm, tf), (sf_hbm, sf), (tw_hbm, tw), (sw_hbm, sw))
        )
    ]
    for load in loads:
        load.start()

    bar = pltpu.get_barrier_semaphore()

    def greet(dev):
        pl.semaphore_signal(bar, inc=1, device_id=dev, device_id_type=MESH)

    @pl.when(is_owner)
    def _():
        @pl.loop(0, 63)
        def _(i):
            n = lax.rem(i + 24, 63) + 1
            greet((lax.rem(img + n, 64), y))

    for j in range(1, 16):
        greet(zc_peer(j)[0])
    for j in range(1, 32):
        greet(xyc_peer(j))


    for load in loads[:3]:
        load.wait()
    mrow = mask[...].astype(F32)
    upper = (
        lax.broadcasted_iota(jnp.int32, (128, 128), 0) <= lax.broadcasted_iota(jnp.int32, (128, 128), 1)
    ).astype(BF16)
    mrow8 = jnp.broadcast_to(mrow, (8, 128))
    rank = dot(mrow8.astype(BF16), upper)
    cnt[...] = jnp.broadcast_to(jnp.sum(mrow, axis=1, keepdims=True), (1, 128))
    want = lax.broadcasted_iota(jnp.int32, (64, 128), 0).astype(F32)
    pick = jnp.where(
        (jnp.broadcast_to(rank[:1], (64, 128)) - 1.0 == want)
        & (jnp.broadcast_to(mrow, (64, 128)) > 0.5), 1.0, 0.0
    ).astype(BF16)

    def unit_rows(kind, feats):
        rows = dot(pick, feats[0])
        norm = jnp.sqrt(jnp.sum(rows * rows, axis=1, keepdims=True) + NORM_EPS)
        unit = (rows / norm).astype(BF16)
        for b in range(4):
            for f in range(3):
                units[kind, b, f] = unit[16 * b:16 * b + 16, 128 * f:128 * f + 128]
        return unit, norm

    s_unit, s_norm = unit_rows(0, sf)
    unit_rows(1, tf)
    for b in range(4):
        unit_f[b] = s_unit[16 * b:16 * b + 16].astype(F32)
        norm_f[b] = jnp.broadcast_to(s_norm[16 * b:16 * b + 16], (16, 128))

    @pl.when(is_owner)
    def _():
        pl.semaphore_wait(bar, 46 + 15)

    @pl.when(jnp.logical_not(is_owner))
    def _():
        pl.semaphore_wait(bar, 46 + 16)

    def each_owner(remote_fn, local_fn):
        for h in range(2):
            for px in range(4):
                for pc in range(2):
                    t = (h * 4 + px) * 2 + pc
                    to = (px * 8 + px + 4 * h) * 2 + pc
                    _, f, b, _, _ = split_square(16 * h + 4 * px + y)

                    @pl.when(img != to)
                    def _():
                        remote_fn(t, to, pc, b, f)

                    if local_fn is not None:
                        @pl.when(img == to)
                        def _():
                            local_fn(pc, b, f)

    def raw_copies(t, to, pc, b, f):
        return (
            remote(cnt, rawc.at[img], s_cnt.at[t], r_cnt, (to, y)),
            remote(units.at[pc, b, f], raw.at[img], s_raw.at[t], r_raw, (to, y)),
        )

    def raw_start(*a):
        for cp in raw_copies(*a):
            cp.start()

    def raw_done(*a):
        for cp in raw_copies(*a):
            cp.wait_send()

    def raw_local(pc, b, f):
        pltpu.make_async_copy(cnt, rawc.at[img], r_cnt).start()
        pltpu.make_async_copy(units.at[pc, b, f], raw.at[img], r_raw).start()

    each_owner(raw_start, raw_local)

    def unit_columns(w_ref):
        w = w_ref[...].astype(F32)
        norm = jnp.sqrt(jnp.sum(w * w, axis=0, keepdims=True) + NORM_EPS)
        return w / norm, norm

    loads[3].wait()
    tw_u, _ = unit_columns(tw)
    tw_t[...] = tw_u.T.astype(BF16)
    loads[4].wait()
    sw_u, sw_n = unit_columns(sw)
    w_norm[...] = sw_n
    w_unit[...] = sw_u.astype(BF16)
    w_t[...] = sw_u.T.astype(BF16)

    kp_me, f_me, b_me, k_me, m_me = split_square(o_me)

    def z_copy(j):
        return remote(grid.at[c, s_me], grid.at[c, s_me], s_z.at[j - 1], r_z.at[h_me], z_peer(j))

    @pl.when(is_owner)
    def _():
        pltpu.make_async_copy(rawc, rawc, r_cnt).wait()
        counts = rawc[:, 0, :]
        match = jnp.where(counts == (16 * m_me).astype(F32), 1.0, 0.0)
        lower = (
            lax.broadcasted_iota(jnp.int32, (64, 64), 1) < lax.broadcasted_iota(jnp.int32, (64, 64), 0)
        ).astype(BF16)
        place = jnp.where(match > 0.5, dot(lower, match.astype(BF16)), -1.0)
        lane_block = lax.shift_right_logical(lax.broadcasted_iota(jnp.int32, (64, 128), 1), 4)
        block_sel = jnp.where(place == lane_block.astype(F32), 1.0, 0.0).astype(BF16)
        spread = (
            lax.shift_right_logical(lax.broadcasted_iota(jnp.int32, (1024, 64), 0), 4)
            == lax.broadcasted_iota(jnp.int32, (1024, 64), 1)
        ).astype(BF16)
        same_row = (
            lax.bitwise_and(lax.broadcasted_iota(jnp.int32, (1024, 128), 0), 15)
            == lax.bitwise_and(lax.broadcasted_iota(jnp.int32, (1024, 128), 1), 15)
        )
        sel_f = jnp.where(same_row, dot(spread, block_sel), 0.0)
        by_core = sel_f.astype(BF16).reshape(32, 2, 16, 128)
        for core in range(2):
            sel[core] = by_core[:, core].reshape(512, 128)
        sel_t = sel_f.T.astype(BF16)
        pltpu.make_async_copy(raw, raw, r_raw).wait()
        grid[c, s_me] = dot(sel_t, raw[...].reshape(1024, 128)).astype(BF16)
        for j in range(1, 8):
            z_copy(j).start()

    for h in range(2):
        spot = 4 * y + x if h == 0 else 16 + 4 * x + y

        @pl.when(z != x + 4 * h)
        def _():
            remote(grid.at[c, spot], grid.at[c, spot], s_z.at[0], r_z.at[h], partner).wait_recv()

    def copy2(h, j, back_j=0):
        if h == 0:
            spot = 4 * y + lax.rem(x + back_j, 4)
            dev = x_peer(j)
        else:
            spot = 16 + 4 * x + lax.rem(y + back_j, 4)
            dev = y_peer(j)
        return remote(grid.at[c, spot], grid.at[c, spot], s_2.at[h, j - 1], r_2.at[h, j - 1], dev)

    def run4(h, off):
        return pl.ds(4 * lax.rem(y + off, 4), 4) if h == 0 else pl.ds(16 + 4 * lax.rem(x + off, 4), 4)

    def copy3(h, j, back_j=0):
        run = run4(h, back_j)
        dev = y_peer(j) if h == 0 else x_peer(j)
        return remote(grid.at[c, run], grid.at[c, run], s_3.at[h, j - 1], r_3.at[h, j - 1], dev)

    def copy_ex(h, j, kind):
        run = run4(h, (4 - j) % 4)
        return remote(grid.at[kind, run], grid.at[kind, run], s_ex.at[h, j], r_ex.at[h, j], partner)

    def spread_lines():
        for j in range(1, 4):
            copy2(0, j).start()
            copy2(1, j).start()

    def spread_planes(kind):
        for h in range(2):
            for j in range(1, 4):
                copy2(h, j, 4 - j).wait_recv()
            for j in range(1, 4):
                copy3(h, j).start()
        copy_ex(0, 0, kind).start()
        copy_ex(1, 0, kind).start()

    def hand_over(kind):
        for j in range(1, 4):
            for h in range(2):
                copy3(h, j, 4 - j).wait_recv()
                copy_ex(h, j, kind).start()

    def take_over(kind, js):
        for j in js:
            for h in range(2):
                copy_ex(h, j, kind).wait_recv()

    def assemble(kind, feats):
        for s in range(30):
            o = square_at(s)
            kp, f = o // 3, o % 3
            feats[128 * kp:128 * kp + 128, 128 * f:128 * f + 128] = grid[kind, s]

    @pl.when(c == 1)
    def _():
        spread_lines()
        spread_planes(1)
        hand_over(1)

    @pl.when(c == 0)
    def _():
        take_over(1, (0, 1))
        spread_lines()
        take_over(1, (2, 3))

    assemble(1, tea)

    for n in range(5):
        cols = slice(256 * n, 256 * n + 256)
        k_blk = jnp.exp(dot_nt(tw_t[...], tea[cols, :]) * (1.0 / TEACHER_TEMP))
        kt[:, cols] = k_blk
        part = k_blk[:, :128] + k_blk[:, 128:]
        csum[...] = part if n == 0 else csum[...] + part
    zero8 = jnp.zeros((8, ROWS), F32)

    def first_sweep(i, acc):
        rows = pl.ds(pl.multiple_of(i * BLK, BLK), BLK)
        col = 1.0 / jnp.sum(csum[rows, :], axis=1, keepdims=True)
        return acc + fold8(kt[rows, :] * col)

    def fold1(acc):
        return jnp.sum(acc, axis=0, keepdims=True)

    tot = fold1(lax.fori_loop(0, COLS // BLK, first_sweep, zero8))

    def ar_a_copy(k, j):
        dev, half = zc_peer(j)
        return remote(ar_v.at[k, half], ar_a.at[k, zc], s_ara.at[k], r_ara.at[k], dev)

    def ar_b_copy(k, j):
        ref = ar_b.at[k, c * 16 + xy]
        return remote(ref, ref, s_arb.at[k], r_arb.at[k], xyc_peer(j))

    def wait_bytes(ref, sem):
        pltpu.make_async_copy(ref, ref, sem).wait()

    def sum_start(k, v):
        ar_v[k, 0] = v[:, :640]
        ar_v[k, 1] = v[:, 640:]
        for j in range(1, 16):
            ar_a_copy(k, j).start()
        ar_a[k, zc] = ar_v[k, c]

    def sum_turn(k):
        wait_bytes(ar_a.at[k, pl.ds(0, 15)], r_ara.at[k])
        v = ar_a[k, 0]
        for i in range(1, 16):
            v = v + ar_a[k, i]
        ar_b[k, c * 16 + xy] = v
        for j in range(1, 32):
            ar_b_copy(k, j).start()

    def sum_end(k):
        wait_bytes(ar_b.at[k, pl.ds(0, 31)], r_arb.at[k])
        halves = []
        for half in range(2):
            v = ar_b[k, half * 16]
            for i in range(1, 16):
                v = v + ar_b[k, half * 16 + i]
            halves.append(v)
        return jnp.concatenate(halves, axis=1)

    def sum_sent(k):
        wait_bytes(ar_a.at[k, pl.ds(0, 15)], s_ara.at[k])
        wait_bytes(ar_b.at[k, pl.ds(0, 31)], s_arb.at[k])

    core_copy = remote(pt.at[1 - c], core_in, s_core, r_core, partner)

    def copy_ra(h, j):
        run = run4(h, j)
        dst = (in_a0, in_a1)[h]
        dev = y_peer(j) if h == 0 else x_peer(j)
        return remote(summed.at[run], dst.at[j - 1], s_ra.at[h, j - 1], r_ra.at[h, j - 1], dev)

    def copy_rb(h, j):
        src = (half0, half1)[h]
        dst = (in_b0, in_b1)[h]
        dev = x_peer(j) if h == 0 else y_peer(j)
        spot = lax.rem((x if h == 0 else y) + j, 4)
        return remote(src.at[spot], dst.at[j - 1], s_rb.at[h, j - 1], r_rb.at[h, j - 1], dev)

    def copy_rz(h):
        away = lax.rem(x + 4 * h - z + 8, 8)
        slot = jnp.maximum(away - 1, 0)
        return remote(
            quart.at[h], in_z.at[slot], s_rz.at[h], r_rz.at[slot], at(x, y, x + 4 * h, c)
        )

    def core_sum():
        core_copy.wait_recv()

        @pl.loop(0, 32)
        def _(s):
            summed[s] = (pt[c, s].astype(F32) + core_in[s].astype(F32)).astype(BF16)

        for j in range(1, 4):
            copy_ra(0, j).start()
            copy_ra(1, j).start()

    def line_sums():
        for h in range(2):
            for j in range(1, 4):
                copy_ra(h, j).wait_recv()
            own = run4(h, 0)
            got = (in_a0, in_a1)[h]
            v = summed[own].astype(F32)
            for j in range(3):
                v = v + got[j].astype(F32)
            (half0, half1)[h][...] = v.astype(BF16)
            for j in range(1, 4):
                copy_rb(h, j).start()

    def plane_sums():
        for h in range(2):
            for j in range(1, 4):
                copy_rb(h, j).wait_recv()
            own = x if h == 0 else y
            got = (in_b0, in_b1)[h]
            v = (half0, half1)[h][own].astype(F32)
            for j in range(3):
                v = v + got[j].astype(F32)
            quart[h] = v

            @pl.when(z != x + 4 * h)
            def _():
                copy_rz(h).start()

    pair_copy = remote(whole.at[c], whole.at[c], s_pair, r_pair, partner)

    def finish_square():
        for j in range(1, 8):
            remote(quart.at[0], in_z.at[j - 1], s_rz.at[0], r_rz.at[j - 1], partner).wait_recv()
        v = quart[h_me]
        for j in range(7):
            v = v + in_z[j]
        whole[c] = v * scale[c, kp_me]
        pair_copy.start()

    parts = []

    def student(ns):
        for n in ns:
            cols = slice(256 * n, 256 * n + 256)
            l_blk = dot_nt(w_t[...], stu[cols, :]) * (1.0 / STUDENT_TEMP)
            lg[:, cols] = l_blk
            e_blk = jnp.exp(l_blk)
            ex[:, cols] = e_blk
            parts.append(jnp.sum(e_blk, axis=0, keepdims=True))

    def products(kind, src):
        for n in range(5):
            cols = slice(256 * n, 256 * n + 256)
            p_blk = dot(w_unit[...], src[:, cols].astype(BF16)).astype(BF16)
            for s in range(30):
                o = square_at(s)
                kp, f = o // 3, o % 3
                if kp // 2 == n:
                    lo = 128 * (kp % 2)
                    pt[kind, s] = p_blk[128 * f:128 * f + 128, lo:lo + 128]

    def empty_squares():
        for kind in range(2):
            for s in (30, 31):
                pt[kind, s] = jnp.zeros((128, 128), BF16)

    sum_start(0, tot)

    @pl.when(c == 0)
    def _():
        spread_planes(0)

    sum_turn(0)

    @pl.when(c == 0)
    def _():
        hand_over(0)

    @pl.when(c == 1)
    def _():
        take_over(0, range(4))

    assemble(0, stu)
    student(range(5))
    sum_start(3, jnp.concatenate(parts, axis=1))
    products(0, ex)
    empty_squares()

    @pl.when(c == 1)
    def _():
        core_copy.start()

    row = 1.0 / sum_end(0)

    def sweep(i, acc):
        rows = pl.ds(pl.multiple_of(i * BLK, BLK), BLK)
        k_blk = kt[rows, :]
        col = 1.0 / jnp.sum(k_blk * row, axis=1, keepdims=True)
        return acc + fold8(k_blk * col)

    tot = fold1(lax.fori_loop(0, COLS // BLK, sweep, zero8))
    sum_start(1, tot)

    @pl.when(c == 0)
    def _():
        core_sum()

    sum_turn(1)
    row = 1.0 / sum_end(1)

    def last_sweep(i, acc):
        rows = pl.ds(pl.multiple_of(i * BLK, BLK), BLK)
        k_blk = kt[rows, :]
        col = 1.0 / jnp.sum(k_blk * row, axis=1, keepdims=True)
        k_blk = k_blk * col
        kt[rows, :] = k_blk
        return acc[0] + fold8(k_blk), acc[1] + fold8(k_blk * lg[rows, :])

    acc_k, acc_l = lax.fori_loop(0, COLS // BLK, last_sweep, (zero8, zero8))

    sum_start(2, fold1(acc_k))
    sum_turn(3)
    products(1, kt)

    @pl.when(c == 0)
    def _():
        core_copy.start()
        line_sums()

    @pl.when(c == 1)
    def _():
        core_sum()

    sum_turn(2)
    partition = sum_end(3)

    @pl.when(c == 0)
    def _():
        plane_sums()

    @pl.when(c == 1)
    def _():
        line_sums()

    row = 1.0 / sum_end(2)
    row_w = jnp.concatenate([jnp.full((1, 128), w, F32) for w in ROW_W], axis=1)
    log_term = jnp.sum(row_w * jnp.log(partition), axis=1, keepdims=True)
    cross = jnp.sum(row_w * row * fold1(acc_l), axis=1, keepdims=True)
    ls_a[zc] = jnp.broadcast_to(cross, (1, 128))

    def ls_a_copy(j):
        return remote(ls_a.at[zc], ls_a.at[zc], s_lsa, r_lsa, zc_peer(j)[0])

    def ls_b_copy(j):
        return remote(ls_b.at[xy], ls_b.at[xy], s_lsb, r_lsb, xy_peer(j))

    for j in range(1, 16):
        ls_a_copy(j).start()
    lead = row_w * (ROWS / STUDENT_TEMP)
    scale_p = lead / partition
    scale_t = lead * row
    for kp in range(10):
        scale[0, kp] = scale_p[:, 128 * kp:128 * kp + 128]
        scale[1, kp] = -scale_t[:, 128 * kp:128 * kp + 128]
    scale[0, 10] = jnp.zeros((1, 128), F32)
    scale[1, 10] = jnp.zeros((1, 128), F32)

    @pl.when(is_owner & (c == 0))
    def _():
        finish_square()

    @pl.loop(0, COLS // BLK)
    def _(i):
        rows = pl.ds(pl.multiple_of(i * BLK, BLK), BLK)
        gb[rows, :] = (ex[rows, :] * scale_p - kt[rows, :] * scale_t).astype(BF16)

    @pl.when(c == 1)
    def _():
        plane_sums()

    gu = dot(gb[...], stu[...]).T
    w_f = w_unit[...].astype(F32)
    gw_ref[...] = (
        1024.0 * (gu - w_f * jnp.sum(w_f * gu, axis=0, keepdims=True)) / w_norm[...]
    )
    wait_bytes(ls_a.at[pl.ds(0, 15)], r_lsa)
    v = ls_a[0]
    for i in range(1, 16):
        v = v + ls_a[i]
    ls_b[xy] = v
    for j in range(1, 16):
        ls_b_copy(j).start()

    sends_back = is_owner & (o_me < 30)

    def copy_back(i):
        return remote(
            tiles.at[i], back.at[k_me, f_me], s_back.at[i], r_back, (2 * i + c, b_me)
        )

    def stays(i):
        return (2 * i + c == img) & (b_me == y)

    @pl.when(is_owner & (c == 1))
    def _():
        finish_square()

    @pl.when(is_owner)
    def _():
        remote(whole.at[1 - c], whole.at[1 - c], s_pair, r_pair, partner).wait_recv()

    @pl.when(sends_back)
    def _():
        v = (whole[0] + whole[1]).T
        hi = v.astype(BF16)
        lo = (v - hi.astype(F32)).astype(BF16)
        tiles[...] = (dot(sel[c], hi) + dot(sel[c], lo)).reshape(32, 16, 128)

        @pl.loop(0, 32)
        def _(i):
            @pl.when(jnp.logical_not(stays(i)))
            def _():
                copy_back(i).start()

            @pl.when(stays(i))
            def _():
                pltpu.make_async_copy(tiles.at[i], back.at[k_me, f_me], r_back).start()

    for b in range(4):
        @pl.when(y == b)
        def _():
            got = back.at[pl.ds(0, 4 - b)]
            pltpu.make_async_copy(got, got, r_back).wait()
            for k in range(4 - b, 4):
                back[k] = jnp.zeros((3, 16, 128), F32)

    cols = []
    for f in range(3):
        cols.append(back[0, f] + back[1, f] + back[2, f] + back[3, f])
    gx = jnp.concatenate(cols, axis=1)
    u = unit_f[y]
    gr_ref[...] = (gx - u * jnp.sum(u * gx, axis=1, keepdims=True)) / norm_f[y][:, :1]

    wait_bytes(ls_b.at[pl.ds(0, 15)], r_lsb)
    v = ls_b[0]
    for i in range(1, 16):
        v = v + ls_b[i]
    loss_ref[...] = log_term - v[:, :1]
    store_loss = pltpu.make_async_copy(loss_ref, loss_hbm, s_loss)
    store_loss.start()

    each_owner(raw_done, None)

    @pl.when(is_owner)
    def _():
        pair_copy.wait_send()
        for j in range(1, 8):
            z_copy(j).wait_send()

    for h in range(2):
        for j in range(1, 4):
            copy2(h, j).wait_send()
            copy3(h, j).wait_send()
            copy_ra(h, j).wait_send()
            copy_rb(h, j).wait_send()
        for j in range(4):
            copy_ex(h, j, c).wait_send()

        @pl.when(z != x + 4 * h)
        def _():
            copy_rz(h).wait_send()

    for k in range(4):
        sum_sent(k)
    wait_bytes(ls_a.at[pl.ds(0, 15)], s_lsa)
    wait_bytes(ls_b.at[pl.ds(0, 15)], s_lsb)
    store_loss.wait()
    core_copy.wait_send()

    @pl.when(sends_back)
    def _():
        @pl.loop(0, 32)
        def _(i):
            @pl.when(jnp.logical_not(stays(i)))
            def _():
                copy_back(i).wait_send()


def shards(student_feats, teacher_feats, student_weight, teacher_weight, patch_masks):
    vmem = pl.BlockSpec(memory_space=pltpu.VMEM)
    hbm = pl.BlockSpec(memory_space=pltpu.HBM)
    dma = pltpu.SemaphoreType.DMA

    scratch = [
        pltpu.VMEM((1, 128, E), BF16),
        pltpu.VMEM((1, 128, E), BF16),
        pltpu.VMEM((E, COLS), BF16),
        pltpu.VMEM((E, COLS), BF16),
        pltpu.VMEM((1, 128), jnp.int32),
        pltpu.VMEM((1, 1), F32),
        pltpu.VMEM((2, 4, 3, 16, 128), BF16),
        pltpu.VMEM((4, 16, E), F32),
        pltpu.VMEM((4, 16, 128), F32),
        pltpu.VMEM((1, 128), F32),
        pltpu.VMEM((64, 16, 128), BF16),
        pltpu.VMEM((64, 1, 128), F32),
        pltpu.VMEM((2, 512, 128), BF16),
        pltpu.VMEM((2, 32, 128, 128), BF16),
        pltpu.VMEM((ROWS, E), BF16),
        pltpu.VMEM((ROWS, E), BF16),
        pltpu.VMEM((E, COLS), BF16),
        pltpu.VMEM((COLS, E), BF16),
        pltpu.VMEM((COLS, E), BF16),
        pltpu.VMEM((1, COLS), F32),
        pltpu.VMEM((COLS, ROWS), F32),
        pltpu.VMEM((COLS, ROWS), F32),
        pltpu.VMEM((COLS, ROWS), F32),
        pltpu.VMEM((COLS, ROWS), BF16),
        pltpu.VMEM((COLS, 128), F32),
        pltpu.VMEM((4, 2, 1, 640), F32),
        pltpu.VMEM((4, 16, 1, 640), F32),
        pltpu.VMEM((4, 32, 1, 640), F32),
        pltpu.VMEM((16, 1, 128), F32),
        pltpu.VMEM((16, 1, 128), F32),
        pltpu.VMEM((2, 32, 128, 128), BF16),
        pltpu.VMEM((32, 128, 128), BF16),
        pltpu.VMEM((32, 128, 128), BF16),
        pltpu.VMEM((3, 4, 128, 128), BF16),
        pltpu.VMEM((3, 4, 128, 128), BF16),
        pltpu.VMEM((4, 128, 128), BF16),
        pltpu.VMEM((4, 128, 128), BF16),
        pltpu.VMEM((3, 128, 128), BF16),
        pltpu.VMEM((3, 128, 128), BF16),
        pltpu.VMEM((2, 128, 128), F32),
        pltpu.VMEM((7, 128, 128), F32),
        pltpu.VMEM((2, 11, 1, 128), F32),
        pltpu.VMEM((2, 128, 128), F32),
        pltpu.VMEM((32, 16, 128), F32),
        pltpu.VMEM((4, 3, 16, 128), F32),
        dma((16,)), dma((16,)), dma, dma,
        dma((7,)), dma((2,)),
        dma((2, 3)), dma((2, 3)), dma((2, 3)), dma((2, 3)), dma((2, 4)), dma((2, 4)),
        dma((4,)), dma((4,)), dma((4,)), dma((4,)), dma, dma, dma, dma,
        dma, dma,
        dma((2, 3)), dma((2, 3)), dma((2, 3)), dma((2, 3)), dma((2,)), dma((7,)),
        dma, dma,
        dma((32,)), dma,
        dma((5,)), dma,
    ]
    loss, grad_weight, grad_rows = pl.pallas_call(
        kernel,
        out_shape=(
            jax.ShapeDtypeStruct((1, 1), F32),
            jax.ShapeDtypeStruct((E, COLS), F32),
            jax.ShapeDtypeStruct((16, E), F32),
        ),
        in_specs=[hbm] * 5,
        out_specs=(hbm, vmem, vmem),
        scratch_shapes=scratch,
        compiler_params=pltpu.CompilerParams(
            collective_id=0, has_side_effects=True, vmem_limit_bytes=40 * 2**20
        ),
    )(*(
        pltpu.with_memory_space_constraint(a, pltpu.HBM)
        for a in (student_feats, teacher_feats, student_weight, teacher_weight, patch_masks)
    ))
    return loss.reshape(()), grad_weight, grad_rows


def solution(mesh):
    placed = (
        P("img", None, None),
        P("img", None, None),
        P(None, ("img", "proto")),
        P(None, ("img", "proto")),
        P("img", None),
    )
    return jax.shard_map(
        shards,
        mesh=mesh,
        in_specs=placed,
        out_specs=(P(), P(None, ("img", "proto")), P(("img", "proto"), None)),
        check_vma=False,
    )
```

```python
import jax
import jax.numpy as jnp
from jax import lax
from jax.experimental import pallas as pl
from jax.experimental.pallas import tpu as pltpu
from jax.sharding import PartitionSpec as P

MESH = pl.DeviceIdType.MESH
F32, BF16 = jnp.float32, jnp.bfloat16
TEACHER_TEMP = 0.07
STUDENT_TEMP = 0.1
NORM_EPS = 1e-06
ROWS, COLS, E, ITERS = 1280, 512, 384, 3
BLK = 128
GROUPS = [(b, m) for b in range(4) for m in range(b + 1, 5)]
ROW_W = [1.0 / (16.0 * m * 32.0) for _, m in GROUPS]


def square_at(s):
    y, q = (s // 4, s % 4) if s < 16 else (s % 4, s // 4)
    if q == 7 and y >= 2:
        return 28 + y
    return q + (0, 12, 20, 8)[y] + (15 if y == 3 and q >= 4 else 0)


SPOT_OF = {square_at(s): s for s in range(32)}


def square_on(y, q):
    base = jnp.where(y == 0, 0, jnp.where(y == 1, 12, jnp.where(y == 2, 20, 8)))
    o = q + base + jnp.where((y == 3) & (q >= 4), 15, 0)
    return jnp.where((q == 7) & (y >= 2), 28 + y, o)


def split_square(o):
    kp = lax.div(o, 3)
    f = lax.rem(o, 3)
    b = lax.div(kp + 4, 8) + lax.div(kp + 1, 8) + lax.div(kp, 9)
    first = 4 * b - lax.div(b * (b - 1), 2)
    return kp, f, b, kp - first, kp - first + b + 1


def dot(a, b):
    return jnp.dot(a, b, preferred_element_type=F32)


def dot_nt(a, b):
    return lax.dot_general(a, b, (((1,), (1,)), ((), ())), preferred_element_type=F32)


def fold8(v):
    return jnp.sum(v.reshape(v.shape[0] // 8, 8, v.shape[1]), axis=0)


def kernel(
    sf_hbm, tf_hbm, sw_hbm, tw_hbm, mask_hbm,
    loss_hbm, gw_ref, gr_ref,
    sf, tf, sw, tw, mask, loss_ref,
    units, unit_f, norm_f, cnt, raw, rawc, sel, grid, tea, stu,
    w_unit, w_t, tw_t, w_norm, kt, lg, ex, gb, csum,
    ar_v, ar_a, ar_b, ls_a, ls_b,
    pt, core_in, summed, in_a0, in_a1, half0, half1, in_b0, in_b1, quart, in_z,
    scale, whole, tiles, back,
    s_raw, s_cnt, r_raw, r_cnt, s_z, r_z, s_2, r_2, s_3, r_3, s_ex, r_ex,
    s_ara, r_ara, s_arb, r_arb, s_lsa, r_lsa, s_lsb, r_lsb, s_core, r_core, s_ra, r_ra, s_rb, r_rb, s_rz, r_rz, s_pair, r_pair, s_back, r_back, s_in, s_loss, turn,
):
    img = lax.axis_index("img")
    y = lax.axis_index("proto")
    c = lax.rem(img, 2)
    z = lax.rem(lax.div(img, 2), 8)
    x = lax.div(img, 16)
    is_owner = lax.rem(z, 4) == x
    h_me = lax.div(z, 4)
    o_me = square_on(y, 4 * h_me + x)
    s_me = jnp.where(h_me == 0, 4 * y + x, 16 + 4 * x + y)

    def at(px, py, pz, pc):
        return ((px * 8 + pz) * 2 + pc, py)

    def x_peer(j):
        return at(lax.rem(x + j, 4), y, z, c)

    def y_peer(j):
        return at(x, lax.rem(y + j, 4), z, c)

    def z_peer(j):
        return at(x, y, lax.rem(z + j, 8), c)

    zc, xy = z * 2 + c, x * 4 + y

    def zc_peer(j):
        g = lax.rem(zc + j, 16)
        return at(x, y, lax.div(g, 2), lax.rem(g, 2)), lax.rem(g, 2)

    def xyc_peer(j):
        g = lax.rem(xy * 2 + c + j, 32)
        return at(lax.div(g, 8), lax.rem(lax.div(g, 2), 4), z, lax.rem(g, 2))

    def xy_peer(j):
        g = lax.rem(xy + j, 16)
        return at(lax.div(g, 4), lax.rem(g, 4), z, c)

    partner = at(x, y, z, 1 - c)

    def remote(src, dst, s, r, dev):
        return pltpu.make_async_remote_copy(
            src_ref=src, dst_ref=dst, send_sem=s, recv_sem=r, device_id=dev, device_id_type=MESH
        )

    loads = [
        pltpu.make_async_copy(src, dst, s_in.at[n])
        for n, (src, dst) in enumerate(
            ((mask_hbm, mask), (tf_hbm, tf), (sf_hbm, sf), (tw_hbm, tw), (sw_hbm, sw))
        )
    ]
    for load in loads:
        load.start()

    bar = pltpu.get_barrier_semaphore()

    def greet(dev):
        pl.semaphore_signal(bar, inc=1, device_id=dev, device_id_type=MESH)

    def hops(n):
        px, pz = n // 16, n // 2 % 8
        return min(px, 4 - px) + min(pz, 8 - pz)

    @pl.when(is_owner)
    def _():
        for n in sorted(range(1, 64), key=hops, reverse=True):
            greet((lax.bitwise_and(img + n, 63), y))

    for j in range(1, 16):
        greet(zc_peer(j)[0])
    for j in range(1, 32):
        greet(xyc_peer(j))


    for load in loads[:3]:
        load.wait()
    mrow = mask[...].astype(F32)
    upper = (
        lax.broadcasted_iota(jnp.int32, (128, 128), 0) <= lax.broadcasted_iota(jnp.int32, (128, 128), 1)
    ).astype(BF16)
    mrow8 = jnp.broadcast_to(mrow, (8, 128))
    rank = dot(mrow8.astype(BF16), upper)
    cnt[...] = jnp.broadcast_to(jnp.sum(mrow, axis=1, keepdims=True), (1, 128))
    want = lax.broadcasted_iota(jnp.int32, (64, 128), 0).astype(F32)
    pick = jnp.where(
        (jnp.broadcast_to(rank[:1], (64, 128)) - 1.0 == want)
        & (jnp.broadcast_to(mrow, (64, 128)) > 0.5), 1.0, 0.0
    ).astype(BF16)

    def unit_rows(kind, feats):
        rows = dot(pick, feats[0])
        norm = jnp.sqrt(jnp.sum(rows * rows, axis=1, keepdims=True) + NORM_EPS)
        unit = (rows / norm).astype(BF16)
        for b in range(4):
            for f in range(3):
                units[kind, b, f] = unit[16 * b:16 * b + 16, 128 * f:128 * f + 128]
        return unit, norm

    s_unit, s_norm = unit_rows(0, sf)
    unit_rows(1, tf)
    for b in range(4):
        unit_f[b] = s_unit[16 * b:16 * b + 16].astype(F32)
        norm_f[b] = jnp.broadcast_to(s_norm[16 * b:16 * b + 16], (16, 128))

    @pl.when(is_owner)
    def _():
        pl.semaphore_wait(bar, 46 + 15)

    @pl.when(jnp.logical_not(is_owner))
    def _():
        pl.semaphore_wait(bar, 46 + 16)

    def each_owner(remote_fn, local_fn, cores=(1, 0)):
        for pc in cores:
            for h in range(2):
                for px in range(4):
                    t = (h * 4 + px) * 2 + pc
                    to = (px * 8 + px + 4 * h) * 2 + pc
                    _, f, b, _, _ = split_square(square_on(y, 4 * h + px))

                    @pl.when(img != to)
                    def _():
                        remote_fn(t, to, pc, b, f)

                    if local_fn is not None:
                        @pl.when(img == to)
                        def _():
                            local_fn(pc, b, f)

    def cnt_copy(t, to, pc, b, f):
        return remote(cnt, rawc.at[img], s_cnt.at[t], r_cnt, (to, y))

    def tile_copy(t, to, pc, b, f):
        return remote(units.at[pc, b, f], raw.at[img], s_raw.at[t], r_raw, (to, y))

    def cnt_start(*a):
        cnt_copy(*a).start()

    def tile_start(*a):
        tile_copy(*a).start()

    def cnt_done(*a):
        cnt_copy(*a).wait_send()

    def tile_done(*a):
        tile_copy(*a).wait_send()

    def cnt_local(pc, b, f):
        pltpu.make_async_copy(cnt, rawc.at[img], r_cnt).start()

    def tile_local(pc, b, f):
        pltpu.make_async_copy(units.at[pc, b, f], raw.at[img], r_raw).start()

    each_owner(cnt_start, cnt_local)
    each_owner(tile_start, tile_local, (1,))

    def unit_columns(w_ref):
        w = w_ref[...].astype(F32)
        norm = jnp.sqrt(jnp.sum(w * w, axis=0, keepdims=True) + NORM_EPS)
        return w / norm, norm

    loads[3].wait()
    tw_u, _ = unit_columns(tw)
    tw_t[...] = tw_u.T.astype(BF16)
    loads[4].wait()
    sw_u, sw_n = unit_columns(sw)
    w_norm[...] = sw_n
    w_unit[...] = sw_u.astype(BF16)
    w_t[...] = sw_u.T.astype(BF16)

    each_owner(tile_done, None, (1,))
    each_owner(tile_start, tile_local, (0,))

    kp_me, f_me, b_me, k_me, m_me = split_square(o_me)

    def z_copy(j):
        return remote(grid.at[c, s_me], grid.at[c, s_me], s_z.at[j - 1], r_z.at[h_me], z_peer(j))

    @pl.when(is_owner)
    def _():
        pltpu.make_async_copy(rawc, rawc, r_cnt).wait()
        counts = rawc[:, 0, :]
        match = jnp.where(counts == (16 * m_me).astype(F32), 1.0, 0.0)
        lower = (
            lax.broadcasted_iota(jnp.int32, (64, 64), 1) < lax.broadcasted_iota(jnp.int32, (64, 64), 0)
        ).astype(BF16)
        place = jnp.where(match > 0.5, dot(lower, match.astype(BF16)), -1.0)
        lane_image = lax.shift_right_logical(lax.broadcasted_iota(jnp.int32, (64, 1024), 1), 4)
        own_image = lane_image == lax.broadcasted_iota(jnp.int32, (64, 1024), 0)
        along = jnp.where(own_image, jnp.broadcast_to(place[:, :1], (64, 1024)), 0.0)
        place_row = dot(jnp.ones((8, 64), BF16), along.astype(BF16))
        sub = lax.broadcasted_iota(jnp.int32, (128, 1024), 0)
        same_row = lax.bitwise_and(sub, 15) == lax.bitwise_and(
            lax.broadcasted_iota(jnp.int32, (128, 1024), 1), 15
        )
        slot_block = lax.shift_right_logical(sub, 4).astype(F32)
        sel_t = jnp.where(
            same_row & (jnp.broadcast_to(place_row[:1], (128, 1024)) == slot_block), 1.0, 0.0
        ).astype(BF16)
        pltpu.make_async_copy(raw, raw, r_raw).wait()
        grid[c, s_me] = dot(sel_t, raw[...].reshape(1024, 128)).astype(BF16)

        @pl.when(c == 0)
        def _():
            pl.semaphore_wait(turn, 1)

        for j in range(1, 8):
            z_copy(j).start()

        lane_block = lax.shift_right_logical(lax.broadcasted_iota(jnp.int32, (64, 128), 1), 4)
        block_sel = jnp.where(place == lane_block.astype(F32), 1.0, 0.0).astype(BF16)
        spread = (
            lax.shift_right_logical(lax.broadcasted_iota(jnp.int32, (1024, 64), 0), 4)
            == lax.broadcasted_iota(jnp.int32, (1024, 64), 1)
        ).astype(BF16)
        same_lane = (
            lax.bitwise_and(lax.broadcasted_iota(jnp.int32, (1024, 128), 0), 15)
            == lax.bitwise_and(lax.broadcasted_iota(jnp.int32, (1024, 128), 1), 15)
        )
        sel_f = jnp.where(same_lane, dot(spread, block_sel), 0.0)
        by_core = sel_f.astype(BF16).reshape(32, 2, 16, 128)
        for core in range(2):
            sel[core] = by_core[:, core].reshape(512, 128)

        @pl.when(c == 1)
        def _():
            for j in range(1, 8):
                z_copy(j).wait_send()
            pl.semaphore_signal(turn, inc=1, device_id=partner, device_id_type=MESH)

    for h in range(2):
        spot = 4 * y + x if h == 0 else 16 + 4 * x + y

        @pl.when(z != x + 4 * h)
        def _():
            remote(grid.at[c, spot], grid.at[c, spot], s_z.at[0], r_z.at[h], partner).wait_recv()

    def copy2(h, j, back_j=0):
        if h == 0:
            spot = 4 * y + lax.rem(x + back_j, 4)
            dev = x_peer(j)
        else:
            spot = 16 + 4 * x + lax.rem(y + back_j, 4)
            dev = y_peer(j)
        return remote(grid.at[c, spot], grid.at[c, spot], s_2.at[h, j - 1], r_2.at[h, j - 1], dev)

    def run4(h, off):
        return pl.ds(4 * lax.rem(y + off, 4), 4) if h == 0 else pl.ds(16 + 4 * lax.rem(x + off, 4), 4)

    def copy3(h, j, back_j=0):
        run = run4(h, back_j)
        dev = y_peer(j) if h == 0 else x_peer(j)
        return remote(grid.at[c, run], grid.at[c, run], s_3.at[h, j - 1], r_3.at[h, j - 1], dev)

    def copy_ex(h, j, kind):
        run = run4(h, (4 - j) % 4)
        return remote(grid.at[kind, run], grid.at[kind, run], s_ex.at[h, j], r_ex.at[h, j], partner)

    def spread_lines():
        for j in range(1, 4):
            copy2(0, j).start()
            copy2(1, j).start()

    def spread_planes(kind):
        for h in range(2):
            for j in range(1, 4):
                copy2(h, j, 4 - j).wait_recv()
            for j in range(1, 4):
                copy3(h, j).start()
        copy_ex(0, 0, kind).start()
        copy_ex(1, 0, kind).start()

    def hand_over(kind):
        for j in range(1, 4):
            for h in range(2):
                copy3(h, j, 4 - j).wait_recv()
                copy_ex(h, j, kind).start()

    def take_over(kind, js):
        for j in js:
            for h in range(2):
                copy_ex(h, j, kind).wait_recv()

    def assemble(kind, feats):
        for o in range(30):
            s, kp, f = SPOT_OF[o], o // 3, o % 3
            feats[128 * kp:128 * kp + 128, 128 * f:128 * f + 128] = grid[kind, s]

    @pl.when(c == 1)
    def _():
        spread_lines()
        spread_planes(1)
        hand_over(1)

    @pl.when(c == 0)
    def _():
        take_over(1, (0, 1))
        spread_lines()
        take_over(1, (2, 3))

    assemble(1, tea)

    for n in range(5):
        cols = slice(256 * n, 256 * n + 256)
        k_blk = jnp.exp(dot_nt(tw_t[...], tea[cols, :]) * (1.0 / TEACHER_TEMP))
        kt[:, cols] = k_blk
        part = k_blk[:, :128] + k_blk[:, 128:]
        csum[...] = part if n == 0 else csum[...] + part
    zero8 = jnp.zeros((8, ROWS), F32)

    def first_sweep(i, acc):
        rows = pl.ds(pl.multiple_of(i * BLK, BLK), BLK)
        col = 1.0 / jnp.sum(csum[rows, :], axis=1, keepdims=True)
        return acc + fold8(kt[rows, :] * col)

    def fold1(acc):
        return jnp.sum(acc, axis=0, keepdims=True)

    tot = fold1(lax.fori_loop(0, COLS // BLK, first_sweep, zero8))

    def ar_a_copy(k, j):
        dev, half = zc_peer(j)
        return remote(ar_v.at[k, half], ar_a.at[k, zc], s_ara.at[k], r_ara.at[k], dev)

    def ar_b_copy(k, j):
        ref = ar_b.at[k, c * 16 + xy]
        return remote(ref, ref, s_arb.at[k], r_arb.at[k], xyc_peer(j))

    def wait_bytes(ref, sem):
        pltpu.make_async_copy(ref, ref, sem).wait()

    def sum_start(k, v):
        ar_v[k, 0] = v[:, :640]
        ar_v[k, 1] = v[:, 640:]
        for j in range(1, 16):
            ar_a_copy(k, j).start()
        ar_a[k, zc] = ar_v[k, c]

    def sum_turn(k):
        wait_bytes(ar_a.at[k, pl.ds(0, 15)], r_ara.at[k])
        v = ar_a[k, 0]
        for i in range(1, 16):
            v = v + ar_a[k, i]
        ar_b[k, c * 16 + xy] = v
        for j in range(1, 32):
            ar_b_copy(k, j).start()

    def sum_end(k):
        wait_bytes(ar_b.at[k, pl.ds(0, 31)], r_arb.at[k])
        halves = []
        for half in range(2):
            v = ar_b[k, half * 16]
            for i in range(1, 16):
                v = v + ar_b[k, half * 16 + i]
            halves.append(v)
        return jnp.concatenate(halves, axis=1)

    def late_a_copy(k, j):
        half = lax.rem(xy * 2 + c + j, 2)
        return remote(
            ar_v.at[k, half], ar_b.at[k, xy * 2 + c], s_arb.at[k], r_arb.at[k], xyc_peer(j)
        )

    def late_b_copy(k, j):
        ref = ar_a.at[k, c * 8 + z]
        return remote(ref, ref, s_ara.at[k], r_ara.at[k], zc_peer(j)[0])

    def late_start(k, v):
        ar_v[k, 0] = v[:, :640]
        ar_v[k, 1] = v[:, 640:]
        for j in range(1, 32):
            late_a_copy(k, j).start()
        ar_b[k, xy * 2 + c] = ar_v[k, c]

    def late_turn(k):
        wait_bytes(ar_b.at[k, pl.ds(0, 31)], r_arb.at[k])
        v = ar_b[k, 0]
        for i in range(1, 32):
            v = v + ar_b[k, i]
        ar_a[k, c * 8 + z] = v
        for j in range(1, 16):
            late_b_copy(k, j).start()

    def late_end(k):
        wait_bytes(ar_a.at[k, pl.ds(0, 15)], r_ara.at[k])
        halves = []
        for half in range(2):
            v = ar_a[k, half * 8]
            for i in range(1, 8):
                v = v + ar_a[k, half * 8 + i]
            halves.append(v)
        return jnp.concatenate(halves, axis=1)

    def sum_sent(k):
        wait_bytes(ar_a.at[k, pl.ds(0, 15)], s_ara.at[k])
        wait_bytes(ar_b.at[k, pl.ds(0, 31)], s_arb.at[k])

    def core_piece(n):
        run = pl.ds(18 * n, 18 - 6 * n)
        return remote(pt.at[1 - c, run], core_in.at[run], s_core.at[n], r_core.at[n], partner)

    def copy_ra(h, j):
        run = run4(h, j)
        dst = (in_a0, in_a1)[h]
        dev = y_peer(j) if h == 0 else x_peer(j)
        return remote(summed.at[run], dst.at[j - 1], s_ra.at[h, j - 1], r_ra.at[h, j - 1], dev)

    def copy_rb(h, j):
        src = (half0, half1)[h]
        dst = (in_b0, in_b1)[h]
        dev = x_peer(j) if h == 0 else y_peer(j)
        spot = lax.rem((x if h == 0 else y) + j, 4)
        return remote(src.at[spot], dst.at[j - 1], s_rb.at[h, j - 1], r_rb.at[h, j - 1], dev)

    def copy_rz(h):
        away = lax.rem(x + 4 * h - z + 8, 8)
        slot = jnp.maximum(away - 1, 0)
        return remote(
            quart.at[h], in_z.at[slot], s_rz.at[h], r_rz.at[slot], at(x, y, x + 4 * h, c)
        )

    def core_sum():
        for s in (SPOT_OF[30], SPOT_OF[31]):
            summed[s] = jnp.zeros((128, 128), BF16)
        for n in range(2):
            core_piece(n).wait_recv()
            for o in range(18 * n, 18 + 12 * n):
                v = pt[c, o].astype(F32) + core_in[o].astype(F32)
                summed[SPOT_OF[o]] = v.astype(BF16)
        for j in range(1, 4):
            copy_ra(0, j).start()
            copy_ra(1, j).start()

    def line_sums():
        for h in range(2):
            for j in range(1, 4):
                copy_ra(h, j).wait_recv()
            own = run4(h, 0)
            got = (in_a0, in_a1)[h]
            v = summed[own].astype(F32)
            for j in range(3):
                v = v + got[j].astype(F32)
            (half0, half1)[h][...] = v.astype(BF16)
            for j in range(1, 4):
                copy_rb(h, j).start()

    def plane_sums():
        for h in range(2):
            for j in range(1, 4):
                copy_rb(h, j).wait_recv()
            own = x if h == 0 else y
            got = (in_b0, in_b1)[h]
            v = (half0, half1)[h][own].astype(F32)
            for j in range(3):
                v = v + got[j].astype(F32)
            quart[h] = v

            @pl.when(z != x + 4 * h)
            def _():
                copy_rz(h).start()

    pair_copy = remote(whole.at[c], whole.at[c], s_pair, r_pair, partner)

    def finish_square():
        for j in range(1, 8):
            remote(quart.at[0], in_z.at[j - 1], s_rz.at[0], r_rz.at[j - 1], partner).wait_recv()
        v = quart[h_me]
        for j in range(7):
            v = v + in_z[j]
        whole[c] = v * scale[c, kp_me]
        pair_copy.start()

    parts = []

    def student(ns):
        for n in ns:
            cols = slice(256 * n, 256 * n + 256)
            l_blk = dot_nt(w_t[...], stu[cols, :]) * (1.0 / STUDENT_TEMP)
            lg[:, cols] = l_blk
            e_blk = jnp.exp(l_blk)
            ex[:, cols] = e_blk
            parts.append(jnp.sum(e_blk, axis=0, keepdims=True))

    def products(kind, src):
        for n in range(2):
            for half in range(3 * n, 3 + 2 * n):
                cols = slice(256 * half, 256 * half + 256)
                p_blk = dot(w_unit[...], src[:, cols].astype(BF16)).astype(BF16)
                for k in range(6):
                    lo, f = 128 * (k // 3), k % 3
                    pt[kind, 6 * half + k] = p_blk[128 * f:128 * f + 128, lo:lo + 128]

            @pl.when(c != kind)
            def _():
                core_piece(n).start()

    sum_start(0, tot)

    @pl.when(c == 0)
    def _():
        spread_planes(0)

    sum_turn(0)

    @pl.when(c == 0)
    def _():
        hand_over(0)

    @pl.when(c == 1)
    def _():
        take_over(0, range(4))

    assemble(0, stu)
    student(range(5))
    sum_start(3, jnp.concatenate(parts, axis=1))
    products(0, ex)

    row = 1.0 / sum_end(0)

    def sweep(i, acc):
        rows = pl.ds(pl.multiple_of(i * BLK, BLK), BLK)
        k_blk = kt[rows, :]
        col = 1.0 / jnp.sum(k_blk * row, axis=1, keepdims=True)
        return acc + fold8(k_blk * col)

    tot = fold1(lax.fori_loop(0, COLS // BLK, sweep, zero8))
    late_start(1, tot)
    late_turn(1)
    sum_turn(3)

    @pl.when(c == 0)
    def _():
        core_sum()

    row = 1.0 / late_end(1)

    def last_sweep(i, acc):
        rows = pl.ds(pl.multiple_of(i * BLK, BLK), BLK)
        k_blk = kt[rows, :]
        col = 1.0 / jnp.sum(k_blk * row, axis=1, keepdims=True)
        k_blk = k_blk * col
        kt[rows, :] = k_blk
        return acc[0] + fold8(k_blk), acc[1] + fold8(k_blk * lg[rows, :])

    acc_k, acc_l = lax.fori_loop(0, COLS // BLK, last_sweep, (zero8, zero8))

    late_start(2, fold1(acc_k))
    products(1, kt)

    @pl.when(c == 0)
    def _():
        line_sums()

    @pl.when(c == 1)
    def _():
        core_sum()

    late_turn(2)
    partition = sum_end(3)

    @pl.when(c == 0)
    def _():
        plane_sums()

    @pl.when(c == 1)
    def _():
        line_sums()

    row = 1.0 / late_end(2)
    row_w = jnp.concatenate([jnp.full((1, 128), w, F32) for w in ROW_W], axis=1)
    log_term = jnp.sum(row_w * jnp.log(partition), axis=1, keepdims=True)
    cross = jnp.sum(row_w * row * fold1(acc_l), axis=1, keepdims=True)
    ls_a[zc] = jnp.broadcast_to(cross, (1, 128))

    def ls_a_copy(j):
        return remote(ls_a.at[zc], ls_a.at[zc], s_lsa, r_lsa, zc_peer(j)[0])

    def ls_b_copy(j):
        return remote(ls_b.at[xy], ls_b.at[xy], s_lsb, r_lsb, xy_peer(j))

    for j in range(1, 16):
        ls_a_copy(j).start()
    lead = row_w * (ROWS / STUDENT_TEMP)
    scale_p = lead / partition
    scale_t = lead * row
    for kp in range(10):
        scale[0, kp] = scale_p[:, 128 * kp:128 * kp + 128]
        scale[1, kp] = -scale_t[:, 128 * kp:128 * kp + 128]
    scale[0, 10] = jnp.zeros((1, 128), F32)
    scale[1, 10] = jnp.zeros((1, 128), F32)

    @pl.when(is_owner & (c == 0))
    def _():
        finish_square()

    @pl.loop(0, COLS // BLK)
    def _(i):
        rows = pl.ds(pl.multiple_of(i * BLK, BLK), BLK)
        gb[rows, :] = (ex[rows, :] * scale_p - kt[rows, :] * scale_t).astype(BF16)

    @pl.when(c == 1)
    def _():
        plane_sums()

    gu = dot(gb[...], stu[...]).T
    w_f = w_unit[...].astype(F32)
    gw_ref[...] = (
        1024.0 * (gu - w_f * jnp.sum(w_f * gu, axis=0, keepdims=True)) / w_norm[...]
    )
    wait_bytes(ls_a.at[pl.ds(0, 15)], r_lsa)
    v = ls_a[0]
    for i in range(1, 16):
        v = v + ls_a[i]
    ls_b[xy] = v
    for j in range(1, 16):
        ls_b_copy(j).start()

    sends_back = is_owner & (o_me < 30)

    def copy_back(i):
        return remote(
            tiles.at[i], back.at[k_me, f_me], s_back.at[i], r_back, (2 * i + c, b_me)
        )

    def stays(i):
        return (2 * i + c == img) & (b_me == y)

    @pl.when(is_owner & (c == 1))
    def _():
        finish_square()

    @pl.when(is_owner)
    def _():
        remote(whole.at[1 - c], whole.at[1 - c], s_pair, r_pair, partner).wait_recv()

    @pl.when(sends_back)
    def _():
        v = whole[0] + whole[1]
        hi = v.astype(BF16)
        lo = (v - hi.astype(F32)).astype(BF16)
        for q in range(4):
            part_sel = sel[c, 128 * q:128 * q + 128]
            t = dot_nt(part_sel, hi) + dot_nt(part_sel, lo)
            tiles[8 * q:8 * q + 8] = t.reshape(8, 16, 128)
            for i in range(8 * q, 8 * q + 8):
                @pl.when(jnp.logical_not(stays(i)))
                def _():
                    copy_back(i).start()

                @pl.when(stays(i))
                def _():
                    pltpu.make_async_copy(tiles.at[i], back.at[k_me, f_me], r_back).start()

    wait_bytes(ls_b.at[pl.ds(0, 15)], r_lsb)
    v = ls_b[0]
    for i in range(1, 16):
        v = v + ls_b[i]
    loss_ref[...] = log_term - v[:, :1]
    store_loss = pltpu.make_async_copy(loss_ref, loss_hbm, s_loss)
    store_loss.start()

    each_owner(cnt_done, None)
    each_owner(tile_done, None, (0,))

    @pl.when(is_owner)
    def _():
        pair_copy.wait_send()

        @pl.when(c == 0)
        def _():
            for j in range(1, 8):
                z_copy(j).wait_send()

    for h in range(2):
        for j in range(1, 4):
            copy2(h, j).wait_send()
            copy3(h, j).wait_send()
            copy_ra(h, j).wait_send()
            copy_rb(h, j).wait_send()
        for j in range(4):
            copy_ex(h, j, c).wait_send()

        @pl.when(z != x + 4 * h)
        def _():
            copy_rz(h).wait_send()

    for k in range(4):
        sum_sent(k)
    wait_bytes(ls_a.at[pl.ds(0, 15)], s_lsa)
    wait_bytes(ls_b.at[pl.ds(0, 15)], s_lsb)
    for n in range(2):
        core_piece(n).wait_send()

    for b in range(4):
        @pl.when(y == b)
        def _():
            got = back.at[pl.ds(0, 4 - b)]
            pltpu.make_async_copy(got, got, r_back).wait()
            for k in range(4 - b, 4):
                back[k] = jnp.zeros((3, 16, 128), F32)

    cols = []
    for f in range(3):
        cols.append(back[0, f] + back[1, f] + back[2, f] + back[3, f])
    gx = jnp.concatenate(cols, axis=1)
    u = unit_f[y]
    gr_ref[...] = (gx - u * jnp.sum(u * gx, axis=1, keepdims=True)) / norm_f[y][:, :1]
    store_loss.wait()

    @pl.when(sends_back)
    def _():
        @pl.loop(0, 32)
        def _(i):
            @pl.when(jnp.logical_not(stays(i)))
            def _():
                copy_back(i).wait_send()


def shards(student_feats, teacher_feats, student_weight, teacher_weight, patch_masks):
    vmem = pl.BlockSpec(memory_space=pltpu.VMEM)
    hbm = pl.BlockSpec(memory_space=pltpu.HBM)
    dma = pltpu.SemaphoreType.DMA

    scratch = [
        pltpu.VMEM((1, 128, E), BF16),
        pltpu.VMEM((1, 128, E), BF16),
        pltpu.VMEM((E, COLS), BF16),
        pltpu.VMEM((E, COLS), BF16),
        pltpu.VMEM((1, 128), jnp.int32),
        pltpu.VMEM((1, 1), F32),
        pltpu.VMEM((2, 4, 3, 16, 128), BF16),
        pltpu.VMEM((4, 16, E), F32),
        pltpu.VMEM((4, 16, 128), F32),
        pltpu.VMEM((1, 128), F32),
        pltpu.VMEM((64, 16, 128), BF16),
        pltpu.VMEM((64, 1, 128), F32),
        pltpu.VMEM((2, 512, 128), BF16),
        pltpu.VMEM((2, 32, 128, 128), BF16),
        pltpu.VMEM((ROWS, E), BF16),
        pltpu.VMEM((ROWS, E), BF16),
        pltpu.VMEM((E, COLS), BF16),
        pltpu.VMEM((COLS, E), BF16),
        pltpu.VMEM((COLS, E), BF16),
        pltpu.VMEM((1, COLS), F32),
        pltpu.VMEM((COLS, ROWS), F32),
        pltpu.VMEM((COLS, ROWS), F32),
        pltpu.VMEM((COLS, ROWS), F32),
        pltpu.VMEM((COLS, ROWS), BF16),
        pltpu.VMEM((COLS, 128), F32),
        pltpu.VMEM((4, 2, 1, 640), F32),
        pltpu.VMEM((4, 16, 1, 640), F32),
        pltpu.VMEM((4, 32, 1, 640), F32),
        pltpu.VMEM((16, 1, 128), F32),
        pltpu.VMEM((16, 1, 128), F32),
        pltpu.VMEM((2, 30, 128, 128), BF16),
        pltpu.VMEM((30, 128, 128), BF16),
        pltpu.VMEM((32, 128, 128), BF16),
        pltpu.VMEM((3, 4, 128, 128), BF16),
        pltpu.VMEM((3, 4, 128, 128), BF16),
        pltpu.VMEM((4, 128, 128), BF16),
        pltpu.VMEM((4, 128, 128), BF16),
        pltpu.VMEM((3, 128, 128), BF16),
        pltpu.VMEM((3, 128, 128), BF16),
        pltpu.VMEM((2, 128, 128), F32),
        pltpu.VMEM((7, 128, 128), F32),
        pltpu.VMEM((2, 11, 1, 128), F32),
        pltpu.VMEM((2, 128, 128), F32),
        pltpu.VMEM((32, 16, 128), F32),
        pltpu.VMEM((4, 3, 16, 128), F32),
        dma((16,)), dma((16,)), dma, dma,
        dma((7,)), dma((2,)),
        dma((2, 3)), dma((2, 3)), dma((2, 3)), dma((2, 3)), dma((2, 4)), dma((2, 4)),
        dma((4,)), dma((4,)), dma((4,)), dma((4,)), dma, dma, dma, dma,
        dma((2,)), dma((2,)),
        dma((2, 3)), dma((2, 3)), dma((2, 3)), dma((2, 3)), dma((2,)), dma((7,)),
        dma, dma,
        dma((32,)), dma,
        dma((5,)), dma,
        pltpu.SemaphoreType.REGULAR,
    ]
    loss, grad_weight, grad_rows = pl.pallas_call(
        kernel,
        out_shape=(
            jax.ShapeDtypeStruct((1, 1), F32),
            jax.ShapeDtypeStruct((E, COLS), F32),
            jax.ShapeDtypeStruct((16, E), F32),
        ),
        in_specs=[hbm] * 5,
        out_specs=(hbm, vmem, vmem),
        scratch_shapes=scratch,
        compiler_params=pltpu.CompilerParams(
            collective_id=0, has_side_effects=True, vmem_limit_bytes=40 * 2**20
        ),
    )(*(
        pltpu.with_memory_space_constraint(a, pltpu.HBM)
        for a in (student_feats, teacher_feats, student_weight, teacher_weight, patch_masks)
    ))
    return loss.reshape(()), grad_weight, grad_rows


def solution(mesh):
    placed = (
        P("img", None, None),
        P("img", None, None),
        P(None, ("img", "proto")),
        P(None, ("img", "proto")),
        P("img", None),
    )
    return jax.shard_map(
        shards,
        mesh=mesh,
        in_specs=placed,
        out_specs=(P(), P(None, ("img", "proto")), P(("img", "proto"), None)),
        check_vma=False,
    )
```

```python
import jax
import jax.numpy as jnp
from jax import lax
from jax.experimental import pallas as pl
from jax.experimental.pallas import tpu as pltpu
from jax.sharding import PartitionSpec as P

MESH = pl.DeviceIdType.MESH
F32, BF16 = jnp.float32, jnp.bfloat16
TEACHER_TEMP = 0.07
STUDENT_TEMP = 0.1
NORM_EPS = 1e-06
ROWS, COLS, E, ITERS = 1280, 512, 384, 3
BLK = 128
GROUPS = [(b, m) for b in range(4) for m in range(b + 1, 5)]
ROW_W = [1.0 / (16.0 * m * 32.0) for _, m in GROUPS]


def square_at(s):
    y, q = (s // 4, s % 4) if s < 16 else (s % 4, s // 4)
    if q == 7 and y >= 2:
        return 28 + y
    return q + (0, 12, 20, 8)[y] + (15 if y == 3 and q >= 4 else 0)


SPOT_OF = {square_at(s): s for s in range(32)}


def square_on(y, q):
    base = jnp.where(y == 0, 0, jnp.where(y == 1, 12, jnp.where(y == 2, 20, 8)))
    o = q + base + jnp.where((y == 3) & (q >= 4), 15, 0)
    return jnp.where((q == 7) & (y >= 2), 28 + y, o)


def split_square(o):
    kp = lax.div(o, 3)
    f = lax.rem(o, 3)
    b = lax.div(kp + 4, 8) + lax.div(kp + 1, 8) + lax.div(kp, 9)
    first = 4 * b - lax.div(b * (b - 1), 2)
    return kp, f, b, kp - first, kp - first + b + 1


def dot(a, b):
    return jnp.dot(a, b, preferred_element_type=F32)


def dot_nt(a, b):
    return lax.dot_general(a, b, (((1,), (1,)), ((), ())), preferred_element_type=F32)


def fold8(v):
    return jnp.sum(v.reshape(v.shape[0] // 8, 8, v.shape[1]), axis=0)


def kernel(
    sf_hbm, tf_hbm, sw_hbm, tw_hbm, mask_hbm,
    loss_hbm, gw_ref, gr_ref,
    sf, tf, sw, tw, mask, loss_ref,
    units, unit_f, norm_f, cnt, raw, rawc, sel, grid, tea, stu,
    w_unit, w_t, tw_t, w_norm, kt, lg, ex, gb, csum,
    ar_v, ar_a, ar_b, ls_a, ls_b,
    pt, core_in, summed, in_a0, in_a1, half0, half1, in_b0, in_b1, quart_p, quart_t, in_zp, in_zt,
    scale, whole, tiles, back,
    s_raw, s_cnt, r_raw, r_cnt, s_z, r_z, s_2, r_2, s_3, r_3, s_ex, r_ex,
    s_ara, r_ara, s_arb, r_arb, s_lsa, r_lsa, s_lsb, r_lsb, s_core, r_core, s_ra, r_ra, s_rb, r_rb, s_rz, r_rz, s_pair, r_pair, s_back, r_back, s_in, s_loss, turn,
):
    img = lax.axis_index("img")
    y = lax.axis_index("proto")
    c = lax.rem(img, 2)
    z = lax.rem(lax.div(img, 2), 8)
    x = lax.div(img, 16)
    is_owner = lax.rem(z, 4) == x
    h_me = lax.div(z, 4)
    o_me = square_on(y, 4 * h_me + x)
    s_me = jnp.where(h_me == 0, 4 * y + x, 16 + 4 * x + y)

    def at(px, py, pz, pc):
        return ((px * 8 + pz) * 2 + pc, py)

    def x_peer(j):
        return at(lax.rem(x + j, 4), y, z, c)

    def y_peer(j):
        return at(x, lax.rem(y + j, 4), z, c)

    def z_peer(j):
        return at(x, y, lax.rem(z + j, 8), c)

    zc, xy = z * 2 + c, x * 4 + y

    def zc_peer(j):
        g = lax.rem(zc + j, 16)
        return at(x, y, lax.div(g, 2), lax.rem(g, 2)), lax.rem(g, 2)

    def xyc_peer(j):
        g = lax.rem(xy * 2 + c + j, 32)
        return at(lax.div(g, 8), lax.rem(lax.div(g, 2), 4), z, lax.rem(g, 2))

    def xy_peer(j):
        g = lax.rem(xy + j, 16)
        return at(lax.div(g, 4), lax.rem(g, 4), z, c)

    partner = at(x, y, z, 1 - c)

    def remote(src, dst, s, r, dev):
        return pltpu.make_async_remote_copy(
            src_ref=src, dst_ref=dst, send_sem=s, recv_sem=r, device_id=dev, device_id_type=MESH
        )

    loads = [
        pltpu.make_async_copy(src, dst, s_in.at[n])
        for n, (src, dst) in enumerate(
            ((mask_hbm, mask), (tf_hbm, tf), (sf_hbm, sf), (tw_hbm, tw), (sw_hbm, sw))
        )
    ]
    for load in loads:
        load.start()

    bar = pltpu.get_barrier_semaphore()

    def greet(dev):
        pl.semaphore_signal(bar, inc=1, device_id=dev, device_id_type=MESH)

    def hops(n):
        px, pz = n // 16, n // 2 % 8
        return min(px, 4 - px) + min(pz, 8 - pz)

    @pl.when(is_owner)
    def _():
        for n in sorted(range(1, 64), key=hops, reverse=True):
            greet((lax.bitwise_and(img + n, 63), y))

    for j in range(1, 16):
        greet(zc_peer(j)[0])
    for j in range(1, 32):
        greet(xyc_peer(j))


    for load in loads[:3]:
        load.wait()
    mrow = mask[...].astype(F32)
    upper = (
        lax.broadcasted_iota(jnp.int32, (128, 128), 0) <= lax.broadcasted_iota(jnp.int32, (128, 128), 1)
    ).astype(BF16)
    mrow8 = jnp.broadcast_to(mrow, (8, 128))
    rank = dot(mrow8.astype(BF16), upper)
    cnt[...] = jnp.broadcast_to(jnp.sum(mrow, axis=1, keepdims=True), (1, 128))
    want = lax.broadcasted_iota(jnp.int32, (64, 128), 0).astype(F32)
    pick = jnp.where(
        (jnp.broadcast_to(rank[:1], (64, 128)) - 1.0 == want)
        & (jnp.broadcast_to(mrow, (64, 128)) > 0.5), 1.0, 0.0
    ).astype(BF16)

    def unit_rows(kind, feats):
        rows = dot(pick, feats[0])
        norm = jnp.sqrt(jnp.sum(rows * rows, axis=1, keepdims=True) + NORM_EPS)
        unit = (rows / norm).astype(BF16)
        for b in range(4):
            for f in range(3):
                units[kind, b, f] = unit[16 * b:16 * b + 16, 128 * f:128 * f + 128]
        return unit, norm

    s_unit, s_norm = unit_rows(0, sf)
    unit_rows(1, tf)
    for b in range(4):
        unit_f[b] = s_unit[16 * b:16 * b + 16].astype(F32)
        norm_f[b] = jnp.broadcast_to(s_norm[16 * b:16 * b + 16], (16, 128))

    @pl.when(is_owner)
    def _():
        pl.semaphore_wait(bar, 46 + 15)

    @pl.when(jnp.logical_not(is_owner))
    def _():
        pl.semaphore_wait(bar, 46 + 16)

    def each_owner(remote_fn, local_fn, cores=(1, 0)):
        for pc in cores:
            for h in range(2):
                for px in range(4):
                    t = (h * 4 + px) * 2 + pc
                    to = (px * 8 + px + 4 * h) * 2 + pc
                    _, f, b, _, _ = split_square(square_on(y, 4 * h + px))

                    @pl.when(img != to)
                    def _():
                        remote_fn(t, to, pc, b, f)

                    if local_fn is not None:
                        @pl.when(img == to)
                        def _():
                            local_fn(pc, b, f)

    def cnt_copy(t, to, pc, b, f):
        return remote(cnt, rawc.at[img], s_cnt.at[t], r_cnt, (to, y))

    def tile_copy(t, to, pc, b, f):
        return remote(units.at[pc, b, f], raw.at[img], s_raw.at[t], r_raw, (to, y))

    def cnt_start(*a):
        cnt_copy(*a).start()

    def tile_start(*a):
        tile_copy(*a).start()

    def cnt_done(*a):
        cnt_copy(*a).wait_send()

    def tile_done(*a):
        tile_copy(*a).wait_send()

    def cnt_local(pc, b, f):
        pltpu.make_async_copy(cnt, rawc.at[img], r_cnt).start()

    def tile_local(pc, b, f):
        pltpu.make_async_copy(units.at[pc, b, f], raw.at[img], r_raw).start()

    each_owner(cnt_start, cnt_local)
    each_owner(tile_start, tile_local, (1,))

    def unit_columns(w_ref):
        w = w_ref[...].astype(F32)
        norm = jnp.sqrt(jnp.sum(w * w, axis=0, keepdims=True) + NORM_EPS)
        return w / norm, norm

    loads[3].wait()
    tw_u, _ = unit_columns(tw)
    tw_t[...] = tw_u.T.astype(BF16)
    loads[4].wait()
    sw_u, sw_n = unit_columns(sw)
    w_norm[...] = sw_n
    w_unit[...] = sw_u.astype(BF16)
    w_t[...] = sw_u.T.astype(BF16)

    each_owner(tile_done, None, (1,))
    each_owner(tile_start, tile_local, (0,))

    kp_me, f_me, b_me, k_me, m_me = split_square(o_me)

    def z_copy(j):
        return remote(grid.at[c, s_me], grid.at[c, s_me], s_z.at[j - 1], r_z.at[h_me], z_peer(j))

    @pl.when(is_owner)
    def _():
        pltpu.make_async_copy(rawc, rawc, r_cnt).wait()
        counts = rawc[:, 0, :]
        match = jnp.where(counts == (16 * m_me).astype(F32), 1.0, 0.0)
        lower = (
            lax.broadcasted_iota(jnp.int32, (64, 64), 1) < lax.broadcasted_iota(jnp.int32, (64, 64), 0)
        ).astype(BF16)
        place = jnp.where(match > 0.5, dot(lower, match.astype(BF16)), -1.0)
        lane_image = lax.shift_right_logical(lax.broadcasted_iota(jnp.int32, (64, 1024), 1), 4)
        own_image = lane_image == lax.broadcasted_iota(jnp.int32, (64, 1024), 0)
        along = jnp.where(own_image, jnp.broadcast_to(place[:, :1], (64, 1024)), 0.0)
        place_row = dot(jnp.ones((8, 64), BF16), along.astype(BF16))
        sub = lax.broadcasted_iota(jnp.int32, (128, 1024), 0)
        same_row = lax.bitwise_and(sub, 15) == lax.bitwise_and(
            lax.broadcasted_iota(jnp.int32, (128, 1024), 1), 15
        )
        slot_block = lax.shift_right_logical(sub, 4).astype(F32)
        sel_t = jnp.where(
            same_row & (jnp.broadcast_to(place_row[:1], (128, 1024)) == slot_block), 1.0, 0.0
        ).astype(BF16)
        pltpu.make_async_copy(raw, raw, r_raw).wait()
        grid[c, s_me] = dot(sel_t, raw[...].reshape(1024, 128)).astype(BF16)

        @pl.when(c == 0)
        def _():
            pl.semaphore_wait(turn, 1)

        for j in range(1, 8):
            z_copy(j).start()

        lane_block = lax.shift_right_logical(lax.broadcasted_iota(jnp.int32, (64, 128), 1), 4)
        block_sel = jnp.where(place == lane_block.astype(F32), 1.0, 0.0).astype(BF16)
        spread = (
            lax.shift_right_logical(lax.broadcasted_iota(jnp.int32, (1024, 64), 0), 4)
            == lax.broadcasted_iota(jnp.int32, (1024, 64), 1)
        ).astype(BF16)
        same_lane = (
            lax.bitwise_and(lax.broadcasted_iota(jnp.int32, (1024, 128), 0), 15)
            == lax.bitwise_and(lax.broadcasted_iota(jnp.int32, (1024, 128), 1), 15)
        )
        sel_f = jnp.where(same_lane, dot(spread, block_sel), 0.0)
        by_core = sel_f.astype(BF16).reshape(32, 2, 16, 128)
        for core in range(2):
            sel[core] = by_core[:, core].reshape(512, 128)

        @pl.when(c == 1)
        def _():
            for j in range(1, 8):
                z_copy(j).wait_send()
            pl.semaphore_signal(turn, inc=1, device_id=partner, device_id_type=MESH)

    for h in range(2):
        spot = 4 * y + x if h == 0 else 16 + 4 * x + y

        @pl.when(z != x + 4 * h)
        def _():
            remote(grid.at[c, spot], grid.at[c, spot], s_z.at[0], r_z.at[h], partner).wait_recv()

    def copy2(h, j, back_j=0):
        if h == 0:
            spot = 4 * y + lax.rem(x + back_j, 4)
            dev = x_peer(j)
        else:
            spot = 16 + 4 * x + lax.rem(y + back_j, 4)
            dev = y_peer(j)
        return remote(grid.at[c, spot], grid.at[c, spot], s_2.at[h, j - 1], r_2.at[h, j - 1], dev)

    def run4(h, off):
        return pl.ds(4 * lax.rem(y + off, 4), 4) if h == 0 else pl.ds(16 + 4 * lax.rem(x + off, 4), 4)

    def copy3(h, j, back_j=0):
        run = run4(h, back_j)
        dev = y_peer(j) if h == 0 else x_peer(j)
        return remote(grid.at[c, run], grid.at[c, run], s_3.at[h, j - 1], r_3.at[h, j - 1], dev)

    def copy_ex(h, j, kind):
        run = run4(h, (4 - j) % 4)
        return remote(grid.at[kind, run], grid.at[kind, run], s_ex.at[h, j], r_ex.at[h, j], partner)

    def spread_lines():
        for j in range(1, 4):
            copy2(0, j).start()
            copy2(1, j).start()

    def spread_planes(kind):
        for h in range(2):
            for j in range(1, 4):
                copy2(h, j, 4 - j).wait_recv()
            for j in range(1, 4):
                copy3(h, j).start()
        copy_ex(0, 0, kind).start()
        copy_ex(1, 0, kind).start()

    def hand_over(kind):
        for j in range(1, 4):
            for h in range(2):
                copy3(h, j, 4 - j).wait_recv()
                copy_ex(h, j, kind).start()

    def take_over(kind, js):
        for j in js:
            for h in range(2):
                copy_ex(h, j, kind).wait_recv()

    def assemble(kind, feats):
        for o in range(30):
            s, kp, f = SPOT_OF[o], o // 3, o % 3
            feats[128 * kp:128 * kp + 128, 128 * f:128 * f + 128] = grid[kind, s]

    @pl.when(c == 1)
    def _():
        spread_lines()
        spread_planes(1)
        hand_over(1)

    @pl.when(c == 0)
    def _():
        take_over(1, (0, 1))
        spread_lines()
        take_over(1, (2, 3))

    assemble(1, tea)

    for n in range(5):
        cols = slice(256 * n, 256 * n + 256)
        k_blk = jnp.exp(dot_nt(tw_t[...], tea[cols, :]) * (1.0 / TEACHER_TEMP))
        kt[:, cols] = k_blk
        part = k_blk[:, :128] + k_blk[:, 128:]
        csum[...] = part if n == 0 else csum[...] + part
    zero8 = jnp.zeros((8, ROWS), F32)

    def first_sweep(i, acc):
        rows = pl.ds(pl.multiple_of(i * BLK, BLK), BLK)
        col = 1.0 / jnp.sum(csum[rows, :], axis=1, keepdims=True)
        return acc + fold8(kt[rows, :] * col)

    def fold1(acc):
        return jnp.sum(acc, axis=0, keepdims=True)

    tot = fold1(lax.fori_loop(0, COLS // BLK, first_sweep, zero8))

    def ar_a_copy(k, j):
        dev, half = zc_peer(j)
        return remote(ar_v.at[k, half], ar_a.at[k, zc], s_ara.at[k], r_ara.at[k], dev)

    def ar_b_copy(k, j):
        ref = ar_b.at[k, c * 16 + xy]
        return remote(ref, ref, s_arb.at[k], r_arb.at[k], xyc_peer(j))

    def wait_bytes(ref, sem):
        pltpu.make_async_copy(ref, ref, sem).wait()

    def sum_start(k, v):
        ar_v[k, 0] = v[:, :640]
        ar_v[k, 1] = v[:, 640:]
        for j in range(1, 16):
            ar_a_copy(k, j).start()
        ar_a[k, zc] = ar_v[k, c]

    def sum_turn(k):
        wait_bytes(ar_a.at[k, pl.ds(0, 15)], r_ara.at[k])
        v = ar_a[k, 0]
        for i in range(1, 16):
            v = v + ar_a[k, i]
        ar_b[k, c * 16 + xy] = v
        for j in range(1, 32):
            ar_b_copy(k, j).start()

    def sum_end(k):
        wait_bytes(ar_b.at[k, pl.ds(0, 31)], r_arb.at[k])
        halves = []
        for half in range(2):
            v = ar_b[k, half * 16]
            for i in range(1, 16):
                v = v + ar_b[k, half * 16 + i]
            halves.append(v)
        return jnp.concatenate(halves, axis=1)

    def late_a_copy(k, j):
        half = lax.rem(xy * 2 + c + j, 2)
        return remote(
            ar_v.at[k, half], ar_b.at[k, xy * 2 + c], s_arb.at[k], r_arb.at[k], xyc_peer(j)
        )

    def late_b_copy(k, j):
        ref = ar_a.at[k, c * 8 + z]
        return remote(ref, ref, s_ara.at[k], r_ara.at[k], zc_peer(j)[0])

    def late_start(k, v):
        ar_v[k, 0] = v[:, :640]
        ar_v[k, 1] = v[:, 640:]
        for j in range(1, 32):
            late_a_copy(k, j).start()
        ar_b[k, xy * 2 + c] = ar_v[k, c]

    def late_turn(k):
        wait_bytes(ar_b.at[k, pl.ds(0, 31)], r_arb.at[k])
        v = ar_b[k, 0]
        for i in range(1, 32):
            v = v + ar_b[k, i]
        ar_a[k, c * 8 + z] = v
        for j in range(1, 16):
            late_b_copy(k, j).start()

    def late_end(k):
        wait_bytes(ar_a.at[k, pl.ds(0, 15)], r_ara.at[k])
        halves = []
        for half in range(2):
            v = ar_a[k, half * 8]
            for i in range(1, 8):
                v = v + ar_a[k, half * 8 + i]
            halves.append(v)
        return jnp.concatenate(halves, axis=1)

    def sum_sent(k):
        wait_bytes(ar_a.at[k, pl.ds(0, 15)], s_ara.at[k])
        wait_bytes(ar_b.at[k, pl.ds(0, 31)], s_arb.at[k])

    def core_piece(n):
        run = pl.ds(18 * n, 18 - 6 * n)
        return remote(pt.at[1 - c, run], core_in.at[run], s_core.at[n], r_core.at[n], partner)

    def copy_ra(h, j):
        run = run4(h, j)
        dst = (in_a0, in_a1)[h]
        dev = y_peer(j) if h == 0 else x_peer(j)
        return remote(summed.at[run], dst.at[j - 1], s_ra.at[h, j - 1], r_ra.at[h, j - 1], dev)

    def copy_rb(h, j):
        src = (half0, half1)[h]
        dst = (in_b0, in_b1)[h]
        dev = x_peer(j) if h == 0 else y_peer(j)
        spot = lax.rem((x if h == 0 else y) + j, 4)
        return remote(src.at[spot], dst.at[j - 1], s_rb.at[h, j - 1], r_rb.at[h, j - 1], dev)

    quarts, in_zs = (quart_p, quart_t), (in_zp, in_zt)

    def copy_rz(kind, h):
        away = lax.rem(x + 4 * h - z + 8, 8)
        slot = jnp.maximum(away - 1, 0)
        return remote(
            quarts[kind].at[h], in_zs[kind].at[slot], s_rz.at[h], r_rz.at[slot],
            at(x, y, x + 4 * h, c),
        )

    def core_sum():
        for s in (SPOT_OF[30], SPOT_OF[31]):
            summed[s] = jnp.zeros((128, 128), BF16)
        for n in range(2):
            core_piece(n).wait_recv()
            for o in range(18 * n, 18 + 12 * n):
                v = pt[c, o].astype(F32) + core_in[o].astype(F32)
                summed[SPOT_OF[o]] = v.astype(BF16)
        for j in range(1, 4):
            copy_ra(0, j).start()
            copy_ra(1, j).start()

    def line_sums():
        for h in range(2):
            for j in range(1, 4):
                copy_ra(h, j).wait_recv()
            own = run4(h, 0)
            got = (in_a0, in_a1)[h]
            v = summed[own].astype(F32)
            for j in range(3):
                v = v + got[j].astype(F32)
            (half0, half1)[h][...] = v.astype(BF16)
            for j in range(1, 4):
                copy_rb(h, j).start()

    def plane_sums(kind):
        for h in range(2):
            for j in range(1, 4):
                copy_rb(h, j).wait_recv()
            own = x if h == 0 else y
            got = (in_b0, in_b1)[h]
            v = (half0, half1)[h][own].astype(F32)
            for j in range(3):
                v = v + got[j].astype(F32)
            quarts[kind][h] = v.astype(quarts[kind].dtype)

            @pl.when(z != x + 4 * h)
            def _():
                copy_rz(kind, h).start()

    pair_copy = remote(whole.at[c], whole.at[c], s_pair, r_pair, partner)

    def finish_square(kind):
        src, got = quarts[kind], in_zs[kind]
        for j in range(1, 8):
            remote(src.at[0], got.at[j - 1], s_rz.at[0], r_rz.at[j - 1], partner).wait_recv()
        v = src[h_me].astype(F32)
        for j in range(7):
            v = v + got[j].astype(F32)
        whole[c] = v * scale[c, kp_me]
        pair_copy.start()

    parts = []

    def student(ns):
        for n in ns:
            cols = slice(256 * n, 256 * n + 256)
            l_blk = dot_nt(w_t[...], stu[cols, :]) * (1.0 / STUDENT_TEMP)
            lg[:, cols] = l_blk
            e_blk = jnp.exp(l_blk)
            ex[:, cols] = e_blk
            parts.append(jnp.sum(e_blk, axis=0, keepdims=True))

    def products(kind, src):
        for n in range(2):
            for half in range(3 * n, 3 + 2 * n):
                cols = slice(256 * half, 256 * half + 256)
                p_blk = dot(w_unit[...], src[:, cols].astype(BF16)).astype(BF16)
                for k in range(6):
                    lo, f = 128 * (k // 3), k % 3
                    pt[kind, 6 * half + k] = p_blk[128 * f:128 * f + 128, lo:lo + 128]

            @pl.when(c != kind)
            def _():
                core_piece(n).start()

    sum_start(0, tot)

    @pl.when(c == 0)
    def _():
        spread_planes(0)

    sum_turn(0)

    @pl.when(c == 0)
    def _():
        hand_over(0)

    @pl.when(c == 1)
    def _():
        take_over(0, range(4))

    assemble(0, stu)
    student(range(5))
    sum_start(3, jnp.concatenate(parts, axis=1))

    row = 1.0 / sum_end(0)

    def sweep(i, acc):
        rows = pl.ds(pl.multiple_of(i * BLK, BLK), BLK)
        k_blk = kt[rows, :]
        col = 1.0 / jnp.sum(k_blk * row, axis=1, keepdims=True)
        return acc + fold8(k_blk * col)

    tot = fold1(lax.fori_loop(0, COLS // BLK, sweep, zero8))
    late_start(1, tot)
    products(0, ex)
    late_turn(1)
    sum_turn(3)

    @pl.when(c == 0)
    def _():
        core_sum()

    row = 1.0 / late_end(1)

    def last_sweep(i, acc):
        rows = pl.ds(pl.multiple_of(i * BLK, BLK), BLK)
        k_blk = kt[rows, :]
        col = 1.0 / jnp.sum(k_blk * row, axis=1, keepdims=True)
        k_blk = k_blk * col
        kt[rows, :] = k_blk
        return acc[0] + fold8(k_blk), acc[1] + fold8(k_blk * lg[rows, :])

    acc_k, acc_l = lax.fori_loop(0, COLS // BLK, last_sweep, (zero8, zero8))

    products(1, kt)
    late_start(2, fold1(acc_k))

    @pl.when(c == 0)
    def _():
        line_sums()

    @pl.when(c == 1)
    def _():
        core_sum()

    late_turn(2)
    partition = sum_end(3)

    @pl.when(c == 1)
    def _():
        line_sums()

    row = 1.0 / late_end(2)

    @pl.when(c == 0)
    def _():
        plane_sums(0)

    row_w = jnp.concatenate([jnp.full((1, 128), w, F32) for w in ROW_W], axis=1)
    log_term = jnp.sum(row_w * jnp.log(partition), axis=1, keepdims=True)
    cross = jnp.sum(row_w * row * fold1(acc_l), axis=1, keepdims=True)
    ls_a[zc] = jnp.broadcast_to(cross, (1, 128))

    def ls_a_copy(j):
        return remote(ls_a.at[zc], ls_a.at[zc], s_lsa, r_lsa, zc_peer(j)[0])

    def ls_b_copy(j):
        return remote(ls_b.at[xy], ls_b.at[xy], s_lsb, r_lsb, xy_peer(j))

    for j in range(1, 16):
        ls_a_copy(j).start()
    lead = row_w * (ROWS / STUDENT_TEMP)
    scale_p = lead / partition
    scale_t = lead * row
    for kp in range(10):
        scale[0, kp] = scale_p[:, 128 * kp:128 * kp + 128]
        scale[1, kp] = -scale_t[:, 128 * kp:128 * kp + 128]
    scale[0, 10] = jnp.zeros((1, 128), F32)
    scale[1, 10] = jnp.zeros((1, 128), F32)

    @pl.loop(0, COLS // BLK)
    def _(i):
        rows = pl.ds(pl.multiple_of(i * BLK, BLK), BLK)
        gb[rows, :] = (ex[rows, :] * scale_p - kt[rows, :] * scale_t).astype(BF16)

    @pl.when(c == 1)
    def _():
        plane_sums(1)

    gu = dot(gb[...], stu[...]).T
    w_f = w_unit[...].astype(F32)
    gw_ref[...] = (
        1024.0 * (gu - w_f * jnp.sum(w_f * gu, axis=0, keepdims=True)) / w_norm[...]
    )
    wait_bytes(ls_a.at[pl.ds(0, 15)], r_lsa)
    v = ls_a[0]
    for i in range(1, 16):
        v = v + ls_a[i]
    ls_b[xy] = v
    for j in range(1, 16):
        ls_b_copy(j).start()

    sends_back = is_owner & (o_me < 30)

    def copy_back(i):
        return remote(
            tiles.at[i], back.at[k_me, f_me], s_back, r_back, (2 * i + c, b_me)
        )

    def stays(i):
        return (2 * i + c == img) & (b_me == y)

    @pl.when(is_owner & (c == 0))
    def _():
        finish_square(0)

    @pl.when(is_owner & (c == 1))
    def _():
        finish_square(1)

    @pl.when(is_owner)
    def _():
        remote(whole.at[1 - c], whole.at[1 - c], s_pair, r_pair, partner).wait_recv()

    @pl.when(sends_back)
    def _():
        v = whole[0] + whole[1]
        hi = v.astype(BF16)
        lo = (v - hi.astype(F32)).astype(BF16)
        for q in range(4):
            part_sel = sel[c, 128 * q:128 * q + 128]
            t = dot_nt(part_sel, hi) + dot_nt(part_sel, lo)
            tiles[8 * q:8 * q + 8] = t.reshape(8, 16, 128)
            for i in range(8 * q, 8 * q + 8):
                @pl.when(jnp.logical_not(stays(i)))
                def _():
                    copy_back(i).start()

                @pl.when(stays(i))
                def _():
                    pltpu.make_async_copy(tiles.at[i], back.at[k_me, f_me], r_back).start()

    wait_bytes(ls_b.at[pl.ds(0, 15)], r_lsb)
    v = ls_b[0]
    for i in range(1, 16):
        v = v + ls_b[i]
    loss_ref[...] = log_term - v[:, :1]
    store_loss = pltpu.make_async_copy(loss_ref, loss_hbm, s_loss)
    store_loss.start()

    each_owner(cnt_done, None)
    each_owner(tile_done, None, (0,))

    @pl.when(is_owner)
    def _():
        pair_copy.wait_send()

        @pl.when(c == 0)
        def _():
            for j in range(1, 8):
                z_copy(j).wait_send()

    for h in range(2):
        for j in range(1, 4):
            copy2(h, j).wait_send()
            copy3(h, j).wait_send()
            copy_ra(h, j).wait_send()
            copy_rb(h, j).wait_send()
        for j in range(4):
            copy_ex(h, j, c).wait_send()

        for kind in range(2):
            @pl.when((z != x + 4 * h) & (c == kind))
            def _():
                copy_rz(kind, h).wait_send()

    for k in range(4):
        sum_sent(k)
    wait_bytes(ls_a.at[pl.ds(0, 15)], s_lsa)
    wait_bytes(ls_b.at[pl.ds(0, 15)], s_lsb)
    for n in range(2):
        core_piece(n).wait_send()

    @pl.when(sends_back & (b_me == y))
    def _():
        wait_bytes(tiles.at[pl.ds(0, 31)], s_back)

    @pl.when(sends_back & (b_me != y))
    def _():
        wait_bytes(tiles, s_back)

    for b in range(4):
        @pl.when(y == b)
        def _():
            got = back.at[pl.ds(0, 4 - b)]
            pltpu.make_async_copy(got, got, r_back).wait()
            for k in range(4 - b, 4):
                back[k] = jnp.zeros((3, 16, 128), F32)

    cols = []
    for f in range(3):
        cols.append(back[0, f] + back[1, f] + back[2, f] + back[3, f])
    gx = jnp.concatenate(cols, axis=1)
    u = unit_f[y]
    gr_ref[...] = (gx - u * jnp.sum(u * gx, axis=1, keepdims=True)) / norm_f[y][:, :1]
    store_loss.wait()


def shards(student_feats, teacher_feats, student_weight, teacher_weight, patch_masks):
    vmem = pl.BlockSpec(memory_space=pltpu.VMEM)
    hbm = pl.BlockSpec(memory_space=pltpu.HBM)
    dma = pltpu.SemaphoreType.DMA

    scratch = [
        pltpu.VMEM((1, 128, E), BF16),
        pltpu.VMEM((1, 128, E), BF16),
        pltpu.VMEM((E, COLS), BF16),
        pltpu.VMEM((E, COLS), BF16),
        pltpu.VMEM((1, 128), jnp.int32),
        pltpu.VMEM((1, 1), F32),
        pltpu.VMEM((2, 4, 3, 16, 128), BF16),
        pltpu.VMEM((4, 16, E), F32),
        pltpu.VMEM((4, 16, 128), F32),
        pltpu.VMEM((1, 128), F32),
        pltpu.VMEM((64, 16, 128), BF16),
        pltpu.VMEM((64, 1, 128), F32),
        pltpu.VMEM((2, 512, 128), BF16),
        pltpu.VMEM((2, 32, 128, 128), BF16),
        pltpu.VMEM((ROWS, E), BF16),
        pltpu.VMEM((ROWS, E), BF16),
        pltpu.VMEM((E, COLS), BF16),
        pltpu.VMEM((COLS, E), BF16),
        pltpu.VMEM((COLS, E), BF16),
        pltpu.VMEM((1, COLS), F32),
        pltpu.VMEM((COLS, ROWS), F32),
        pltpu.VMEM((COLS, ROWS), F32),
        pltpu.VMEM((COLS, ROWS), F32),
        pltpu.VMEM((COLS, ROWS), BF16),
        pltpu.VMEM((COLS, 128), F32),
        pltpu.VMEM((4, 2, 1, 640), F32),
        pltpu.VMEM((4, 16, 1, 640), F32),
        pltpu.VMEM((4, 32, 1, 640), F32),
        pltpu.VMEM((16, 1, 128), F32),
        pltpu.VMEM((16, 1, 128), F32),
        pltpu.VMEM((2, 30, 128, 128), BF16),
        pltpu.VMEM((30, 128, 128), BF16),
        pltpu.VMEM((32, 128, 128), BF16),
        pltpu.VMEM((3, 4, 128, 128), BF16),
        pltpu.VMEM((3, 4, 128, 128), BF16),
        pltpu.VMEM((4, 128, 128), BF16),
        pltpu.VMEM((4, 128, 128), BF16),
        pltpu.VMEM((3, 128, 128), BF16),
        pltpu.VMEM((3, 128, 128), BF16),
        pltpu.VMEM((2, 128, 128), F32),
        pltpu.VMEM((2, 128, 128), BF16),
        pltpu.VMEM((7, 128, 128), F32),
        pltpu.VMEM((7, 128, 128), BF16),
        pltpu.VMEM((2, 11, 1, 128), F32),
        pltpu.VMEM((2, 128, 128), F32),
        pltpu.VMEM((32, 16, 128), F32),
        pltpu.VMEM((4, 3, 16, 128), F32),
        dma((16,)), dma((16,)), dma, dma,
        dma((7,)), dma((2,)),
        dma((2, 3)), dma((2, 3)), dma((2, 3)), dma((2, 3)), dma((2, 4)), dma((2, 4)),
        dma((4,)), dma((4,)), dma((4,)), dma((4,)), dma, dma, dma, dma,
        dma((2,)), dma((2,)),
        dma((2, 3)), dma((2, 3)), dma((2, 3)), dma((2, 3)), dma((2,)), dma((7,)),
        dma, dma,
        dma, dma,
        dma((5,)), dma,
        pltpu.SemaphoreType.REGULAR,
    ]
    loss, grad_weight, grad_rows = pl.pallas_call(
        kernel,
        out_shape=(
            jax.ShapeDtypeStruct((1, 1), F32),
            jax.ShapeDtypeStruct((E, COLS), F32),
            jax.ShapeDtypeStruct((16, E), F32),
        ),
        in_specs=[hbm] * 5,
        out_specs=(hbm, vmem, vmem),
        scratch_shapes=scratch,
        compiler_params=pltpu.CompilerParams(
            collective_id=0, has_side_effects=True, vmem_limit_bytes=40 * 2**20
        ),
    )(*(
        pltpu.with_memory_space_constraint(a, pltpu.HBM)
        for a in (student_feats, teacher_feats, student_weight, teacher_weight, patch_masks)
    ))
    return loss.reshape(()), grad_weight, grad_rows


def solution(mesh):
    placed = (
        P("img", None, None),
        P("img", None, None),
        P(None, ("img", "proto")),
        P(None, ("img", "proto")),
        P("img", None),
    )
    return jax.shard_map(
        shards,
        mesh=mesh,
        in_specs=placed,
        out_specs=(P(), P(None, ("img", "proto")), P(("img", "proto"), None)),
        check_vma=False,
    )
```

```python
import jax
import jax.numpy as jnp
from jax import lax
from jax.experimental import pallas as pl
from jax.experimental.pallas import tpu as pltpu
from jax.sharding import PartitionSpec as P

MESH = pl.DeviceIdType.MESH
F32, BF16 = jnp.float32, jnp.bfloat16
TEACHER_TEMP = 0.07
STUDENT_TEMP = 0.1
NORM_EPS = 1e-06
ROWS, COLS, E, ITERS = 1280, 512, 384, 3
BLK = 128
GROUPS = [(b, m) for b in range(4) for m in range(b + 1, 5)]
ROW_W = [1.0 / (16.0 * m * 32.0) for _, m in GROUPS]


def square_at(s):
    y, q = (s // 4, s % 4) if s < 16 else (s % 4, s // 4)
    if q == 7 and y >= 2:
        return 28 + y
    return q + (0, 12, 20, 8)[y] + (15 if y == 3 and q >= 4 else 0)


SPOT_OF = {square_at(s): s for s in range(32)}


def square_on(y, q):
    base = jnp.where(y == 0, 0, jnp.where(y == 1, 12, jnp.where(y == 2, 20, 8)))
    o = q + base + jnp.where((y == 3) & (q >= 4), 15, 0)
    return jnp.where((q == 7) & (y >= 2), 28 + y, o)


def split_square(o):
    kp = lax.div(o, 3)
    f = lax.rem(o, 3)
    b = lax.div(kp + 4, 8) + lax.div(kp + 1, 8) + lax.div(kp, 9)
    first = 4 * b - lax.div(b * (b - 1), 2)
    return kp, f, b, kp - first, kp - first + b + 1


def dot(a, b):
    return jnp.dot(a, b, preferred_element_type=F32)


def dot_nt(a, b):
    return lax.dot_general(a, b, (((1,), (1,)), ((), ())), preferred_element_type=F32)


def fold8(v):
    return jnp.sum(v.reshape(v.shape[0] // 8, 8, v.shape[1]), axis=0)


def kernel(
    sf_hbm, tf_hbm, sw_hbm, tw_hbm, mask_hbm,
    loss_hbm, gw_ref, gr_ref,
    sf, tf, sw, tw, mask, loss_ref,
    units, unit_f, norm_f, cnt, raw, rawc, sel, grid, tea, stu,
    w_unit, w_t, tw_t, w_norm, kt, lg, ex, gb, csum,
    ar_v, ar_a, ar_b, ls_a, ls_b,
    pt, core_in, summed, in_a0, in_a1, half0, half1, in_b0, in_b1, quart_p, quart_t, in_zp, in_zt,
    scale, whole, tiles, back,
    s_raw, s_cnt, r_raw, r_cnt, s_z, r_z, s_2, r_2, s_3, r_3, s_ex, r_ex,
    s_ara, r_ara, s_arb, r_arb, s_lsa, r_lsa, s_lsb, r_lsb, s_core, r_core, s_ra, r_ra, s_rb, r_rb, s_rz, r_rz, s_pair, r_pair, s_back, r_back, s_in, s_loss, turn,
):
    img = lax.axis_index("img")
    y = lax.axis_index("proto")
    c = lax.rem(img, 2)
    z = lax.rem(lax.div(img, 2), 8)
    x = lax.div(img, 16)
    is_owner = lax.rem(z, 4) == x
    h_me = lax.div(z, 4)
    o_me = square_on(y, 4 * h_me + x)
    s_me = jnp.where(h_me == 0, 4 * y + x, 16 + 4 * x + y)

    def at(px, py, pz, pc):
        return ((px * 8 + pz) * 2 + pc, py)

    def x_peer(j):
        return at(lax.rem(x + j, 4), y, z, c)

    def y_peer(j):
        return at(x, lax.rem(y + j, 4), z, c)

    def z_peer(j):
        return at(x, y, lax.rem(z + j, 8), c)

    zc, xy = z * 2 + c, x * 4 + y

    def zc_peer(j):
        g = lax.rem(zc + j, 16)
        return at(x, y, lax.div(g, 2), lax.rem(g, 2)), lax.rem(g, 2)

    def xyc_peer(j):
        g = lax.rem(xy * 2 + c + j, 32)
        return at(lax.div(g, 8), lax.rem(lax.div(g, 2), 4), z, lax.rem(g, 2))

    def xy_peer(j):
        g = lax.rem(xy + j, 16)
        return at(lax.div(g, 4), lax.rem(g, 4), z, c)

    partner = at(x, y, z, 1 - c)

    def remote(src, dst, s, r, dev):
        return pltpu.make_async_remote_copy(
            src_ref=src, dst_ref=dst, send_sem=s, recv_sem=r, device_id=dev, device_id_type=MESH
        )

    loads = [
        pltpu.make_async_copy(src, dst, s_in.at[n])
        for n, (src, dst) in enumerate(
            ((mask_hbm, mask), (tf_hbm, tf), (sf_hbm, sf), (tw_hbm, tw), (sw_hbm, sw))
        )
    ]
    for load in loads:
        load.start()

    bar = pltpu.get_barrier_semaphore()

    def greet(dev):
        pl.semaphore_signal(bar, inc=1, device_id=dev, device_id_type=MESH)

    def hops(n):
        px, pz = n // 16, n // 2 % 8
        return min(px, 4 - px) + min(pz, 8 - pz)

    @pl.when(is_owner)
    def _():
        for n in sorted(range(1, 64), key=hops, reverse=True):
            greet((lax.bitwise_and(img + n, 63), y))

    for j in range(1, 16):
        greet(zc_peer(j)[0])
    for j in range(1, 32):
        greet(xyc_peer(j))


    for load in loads[:3]:
        load.wait()
    mrow = mask[...].astype(F32)
    upper = (
        lax.broadcasted_iota(jnp.int32, (128, 128), 0) <= lax.broadcasted_iota(jnp.int32, (128, 128), 1)
    ).astype(BF16)
    mrow8 = jnp.broadcast_to(mrow, (8, 128))
    rank = dot(mrow8.astype(BF16), upper)
    cnt[...] = jnp.broadcast_to(jnp.sum(mrow, axis=1, keepdims=True), (1, 128))
    want = lax.broadcasted_iota(jnp.int32, (64, 128), 0).astype(F32)
    pick = jnp.where(
        (jnp.broadcast_to(rank[:1], (64, 128)) - 1.0 == want)
        & (jnp.broadcast_to(mrow, (64, 128)) > 0.5), 1.0, 0.0
    ).astype(BF16)

    def unit_rows(kind, feats):
        rows = dot(pick, feats[0])
        norm = jnp.sqrt(jnp.sum(rows * rows, axis=1, keepdims=True) + NORM_EPS)
        unit = (rows / norm).astype(BF16)
        for b in range(4):
            for f in range(3):
                units[kind, b, f] = unit[16 * b:16 * b + 16, 128 * f:128 * f + 128]
        return unit, norm

    s_unit, s_norm = unit_rows(0, sf)
    unit_rows(1, tf)
    for b in range(4):
        unit_f[b] = s_unit[16 * b:16 * b + 16].astype(F32)
        norm_f[b] = jnp.broadcast_to(s_norm[16 * b:16 * b + 16], (16, 128))

    @pl.when(is_owner)
    def _():
        pl.semaphore_wait(bar, 46 + 15)

    @pl.when(jnp.logical_not(is_owner))
    def _():
        pl.semaphore_wait(bar, 46 + 16)

    def each_owner(remote_fn, local_fn, cores=(1, 0)):
        for pc in cores:
            for h in range(2):
                for px in range(4):
                    t = (h * 4 + px) * 2 + pc
                    to = (px * 8 + px + 4 * h) * 2 + pc
                    _, f, b, _, _ = split_square(square_on(y, 4 * h + px))

                    @pl.when(img != to)
                    def _():
                        remote_fn(t, to, pc, b, f)

                    if local_fn is not None:
                        @pl.when(img == to)
                        def _():
                            local_fn(pc, b, f)

    def cnt_copy(t, to, pc, b, f):
        return remote(cnt, rawc.at[img], s_cnt.at[t], r_cnt, (to, y))

    def tile_copy(t, to, pc, b, f):
        return remote(units.at[pc, b, f], raw.at[img], s_raw.at[t], r_raw, (to, y))

    def cnt_start(*a):
        cnt_copy(*a).start()

    def tile_start(*a):
        tile_copy(*a).start()

    def cnt_done(*a):
        cnt_copy(*a).wait_send()

    def tile_done(*a):
        tile_copy(*a).wait_send()

    def cnt_local(pc, b, f):
        pltpu.make_async_copy(cnt, rawc.at[img], r_cnt).start()

    def tile_local(pc, b, f):
        pltpu.make_async_copy(units.at[pc, b, f], raw.at[img], r_raw).start()

    each_owner(cnt_start, cnt_local)
    each_owner(tile_start, tile_local, (1,))

    def unit_columns(w_ref):
        w = w_ref[...].astype(F32)
        norm = jnp.sqrt(jnp.sum(w * w, axis=0, keepdims=True) + NORM_EPS)
        return w / norm, norm

    loads[3].wait()
    tw_u, _ = unit_columns(tw)
    tw_t[...] = tw_u.T.astype(BF16)
    loads[4].wait()
    sw_u, sw_n = unit_columns(sw)
    w_norm[...] = sw_n
    w_unit[...] = sw_u.astype(BF16)
    w_t[...] = sw_u.T.astype(BF16)

    each_owner(tile_done, None, (1,))
    each_owner(tile_start, tile_local, (0,))

    kp_me, f_me, b_me, k_me, m_me = split_square(o_me)

    def z_copy(j):
        return remote(grid.at[c, s_me], grid.at[c, s_me], s_z.at[j - 1], r_z.at[h_me], z_peer(j))

    @pl.when(is_owner)
    def _():
        pltpu.make_async_copy(rawc, rawc, r_cnt).wait()
        counts = rawc[:, 0, :]
        match = jnp.where(counts == (16 * m_me).astype(F32), 1.0, 0.0)
        lower = (
            lax.broadcasted_iota(jnp.int32, (64, 64), 1) < lax.broadcasted_iota(jnp.int32, (64, 64), 0)
        ).astype(BF16)
        place = jnp.where(match > 0.5, dot(lower, match.astype(BF16)), -1.0)
        lane_image = lax.shift_right_logical(lax.broadcasted_iota(jnp.int32, (64, 1024), 1), 4)
        own_image = lane_image == lax.broadcasted_iota(jnp.int32, (64, 1024), 0)
        along = jnp.where(own_image, jnp.broadcast_to(place[:, :1], (64, 1024)), 0.0)
        place_row = dot(jnp.ones((8, 64), BF16), along.astype(BF16))
        sub = lax.broadcasted_iota(jnp.int32, (128, 1024), 0)
        same_row = lax.bitwise_and(sub, 15) == lax.bitwise_and(
            lax.broadcasted_iota(jnp.int32, (128, 1024), 1), 15
        )
        slot_block = lax.shift_right_logical(sub, 4).astype(F32)
        sel_t = jnp.where(
            same_row & (jnp.broadcast_to(place_row[:1], (128, 1024)) == slot_block), 1.0, 0.0
        ).astype(BF16)
        pltpu.make_async_copy(raw, raw, r_raw).wait()
        grid[c, s_me] = dot(sel_t, raw[...].reshape(1024, 128)).astype(BF16)

        @pl.when(c == 0)
        def _():
            pl.semaphore_wait(turn, 1)

        for j in range(1, 8):
            z_copy(j).start()

        lane_block = lax.shift_right_logical(lax.broadcasted_iota(jnp.int32, (64, 128), 1), 4)
        block_sel = jnp.where(place == lane_block.astype(F32), 1.0, 0.0).astype(BF16)
        spread = (
            lax.shift_right_logical(lax.broadcasted_iota(jnp.int32, (1024, 64), 0), 4)
            == lax.broadcasted_iota(jnp.int32, (1024, 64), 1)
        ).astype(BF16)
        same_lane = (
            lax.bitwise_and(lax.broadcasted_iota(jnp.int32, (1024, 128), 0), 15)
            == lax.bitwise_and(lax.broadcasted_iota(jnp.int32, (1024, 128), 1), 15)
        )
        sel_f = jnp.where(same_lane, dot(spread, block_sel), 0.0)
        by_core = sel_f.astype(BF16).reshape(32, 2, 16, 128)
        for core in range(2):
            sel[core] = by_core[:, core].reshape(512, 128)

        @pl.when(c == 1)
        def _():
            for j in range(1, 8):
                z_copy(j).wait_send()
            pl.semaphore_signal(turn, inc=1, device_id=partner, device_id_type=MESH)

    for h in range(2):
        spot = 4 * y + x if h == 0 else 16 + 4 * x + y

        @pl.when(z != x + 4 * h)
        def _():
            remote(grid.at[c, spot], grid.at[c, spot], s_z.at[0], r_z.at[h], partner).wait_recv()

    def copy2(h, j, back_j=0):
        if h == 0:
            spot = 4 * y + lax.rem(x + back_j, 4)
            dev = x_peer(j)
        else:
            spot = 16 + 4 * x + lax.rem(y + back_j, 4)
            dev = y_peer(j)
        return remote(grid.at[c, spot], grid.at[c, spot], s_2.at[h, j - 1], r_2.at[h, j - 1], dev)

    def run4(h, off):
        return pl.ds(4 * lax.rem(y + off, 4), 4) if h == 0 else pl.ds(16 + 4 * lax.rem(x + off, 4), 4)

    def copy3(h, j, back_j=0):
        run = run4(h, back_j)
        dev = y_peer(j) if h == 0 else x_peer(j)
        return remote(grid.at[c, run], grid.at[c, run], s_3.at[h, j - 1], r_3.at[h, j - 1], dev)

    def copy_ex(h, j, kind):
        run = run4(h, (4 - j) % 4)
        return remote(grid.at[kind, run], grid.at[kind, run], s_ex.at[h, j], r_ex.at[h, j], partner)

    def spread_lines():
        for j in range(1, 4):
            copy2(0, j).start()
            copy2(1, j).start()

    def spread_planes(kind):
        for h in range(2):
            for j in range(1, 4):
                copy2(h, j, 4 - j).wait_recv()
            for j in range(1, 4):
                copy3(h, j).start()
        copy_ex(0, 0, kind).start()
        copy_ex(1, 0, kind).start()

    def hand_over(kind):
        for j in range(1, 4):
            for h in range(2):
                copy3(h, j, 4 - j).wait_recv()
                copy_ex(h, j, kind).start()

    def take_over(kind, js):
        for j in js:
            for h in range(2):
                copy_ex(h, j, kind).wait_recv()

    def assemble(kind, feats):
        for o in range(30):
            s, kp, f = SPOT_OF[o], o // 3, o % 3
            feats[128 * kp:128 * kp + 128, 128 * f:128 * f + 128] = grid[kind, s]

    @pl.when(c == 1)
    def _():
        spread_lines()
        spread_planes(1)
        hand_over(1)

    @pl.when(c == 0)
    def _():
        take_over(1, (0, 1))
        spread_lines()
        take_over(1, (2, 3))

    assemble(1, tea)

    for n in range(5):
        cols = slice(256 * n, 256 * n + 256)
        k_blk = jnp.exp(dot_nt(tw_t[...], tea[cols, :]) * (1.0 / TEACHER_TEMP))
        kt[:, cols] = k_blk
        part = k_blk[:, :128] + k_blk[:, 128:]
        csum[...] = part if n == 0 else csum[...] + part
    zero8 = jnp.zeros((8, ROWS), F32)

    def first_sweep(i, acc):
        rows = pl.ds(pl.multiple_of(i * BLK, BLK), BLK)
        col = 1.0 / jnp.sum(csum[rows, :], axis=1, keepdims=True)
        return acc + fold8(kt[rows, :] * col)

    def fold1(acc):
        return jnp.sum(acc, axis=0, keepdims=True)

    tot = fold1(lax.fori_loop(0, COLS // BLK, first_sweep, zero8))

    def ar_a_copy(k, j):
        dev, half = zc_peer(j)
        return remote(ar_v.at[k, half], ar_a.at[k, zc], s_ara.at[k], r_ara.at[k], dev)

    def ar_b_copy(k, j):
        ref = ar_b.at[k, c * 16 + xy]
        return remote(ref, ref, s_arb.at[k], r_arb.at[k], xyc_peer(j))

    def wait_bytes(ref, sem):
        pltpu.make_async_copy(ref, ref, sem).wait()

    def sum_start(k, v):
        ar_v[k, 0] = v[:, :640]
        ar_v[k, 1] = v[:, 640:]
        for j in range(1, 16):
            ar_a_copy(k, j).start()
        ar_a[k, zc] = ar_v[k, c]

    def sum_turn(k):
        wait_bytes(ar_a.at[k, pl.ds(0, 15)], r_ara.at[k])
        v = ar_a[k, 0]
        for i in range(1, 16):
            v = v + ar_a[k, i]
        ar_b[k, c * 16 + xy] = v
        for j in range(1, 32):
            ar_b_copy(k, j).start()

    def sum_end(k):
        wait_bytes(ar_b.at[k, pl.ds(0, 31)], r_arb.at[k])
        halves = []
        for half in range(2):
            v = ar_b[k, half * 16]
            for i in range(1, 16):
                v = v + ar_b[k, half * 16 + i]
            halves.append(v)
        return jnp.concatenate(halves, axis=1)

    def late_a_copy(k, j):
        half = lax.rem(xy * 2 + c + j, 2)
        return remote(
            ar_v.at[k, half], ar_b.at[k, xy * 2 + c], s_arb.at[k], r_arb.at[k], xyc_peer(j)
        )

    def late_b_copy(k, j):
        ref = ar_a.at[k, c * 8 + z]
        return remote(ref, ref, s_ara.at[k], r_ara.at[k], zc_peer(j)[0])

    def late_start(k, v):
        ar_v[k, 0] = v[:, :640]
        ar_v[k, 1] = v[:, 640:]
        for j in range(1, 32):
            late_a_copy(k, j).start()
        ar_b[k, xy * 2 + c] = ar_v[k, c]

    def late_turn(k):
        wait_bytes(ar_b.at[k, pl.ds(0, 31)], r_arb.at[k])
        v = ar_b[k, 0]
        for i in range(1, 32):
            v = v + ar_b[k, i]
        ar_a[k, c * 8 + z] = v
        for j in range(1, 16):
            late_b_copy(k, j).start()

    def late_end(k):
        wait_bytes(ar_a.at[k, pl.ds(0, 15)], r_ara.at[k])
        halves = []
        for half in range(2):
            v = ar_a[k, half * 8]
            for i in range(1, 8):
                v = v + ar_a[k, half * 8 + i]
            halves.append(v)
        return jnp.concatenate(halves, axis=1)

    def sum_sent(k):
        wait_bytes(ar_a.at[k, pl.ds(0, 15)], s_ara.at[k])
        wait_bytes(ar_b.at[k, pl.ds(0, 31)], s_arb.at[k])

    def core_piece(n):
        run = pl.ds(18 * n, 18 - 6 * n)
        return remote(pt.at[1 - c, run], core_in.at[run], s_core.at[n], r_core.at[n], partner)

    def copy_ra(h, j):
        run = run4(h, j)
        dst = (in_a0, in_a1)[h]
        dev = y_peer(j) if h == 0 else x_peer(j)
        return remote(summed.at[run], dst.at[j - 1], s_ra.at[h, j - 1], r_ra.at[h, j - 1], dev)

    def copy_rb(h, j):
        src = (half0, half1)[h]
        dst = (in_b0, in_b1)[h]
        dev = x_peer(j) if h == 0 else y_peer(j)
        spot = lax.rem((x if h == 0 else y) + j, 4)
        return remote(src.at[spot], dst.at[j - 1], s_rb.at[h, j - 1], r_rb.at[h, j - 1], dev)

    quarts, in_zs = (quart_p, quart_t), (in_zp, in_zt)

    def copy_rz(kind, h):
        away = lax.rem(x + 4 * h - z + 8, 8)
        slot = jnp.maximum(away - 1, 0)
        return remote(
            quarts[kind].at[h], in_zs[kind].at[slot], s_rz.at[h], r_rz.at[slot],
            at(x, y, x + 4 * h, c),
        )

    def core_sum():
        for s in (SPOT_OF[30], SPOT_OF[31]):
            summed[s] = jnp.zeros((128, 128), BF16)
        for n in range(2):
            core_piece(n).wait_recv()
            for o in range(18 * n, 18 + 12 * n):
                v = pt[c, o].astype(F32) + core_in[o].astype(F32)
                summed[SPOT_OF[o]] = v.astype(BF16)
        for j in range(1, 4):
            copy_ra(0, j).start()
            copy_ra(1, j).start()

    def line_sums():
        for h in range(2):
            for j in range(1, 4):
                copy_ra(h, j).wait_recv()
            own = run4(h, 0)
            got = (in_a0, in_a1)[h]
            v = summed[own].astype(F32)
            for j in range(3):
                v = v + got[j].astype(F32)
            (half0, half1)[h][...] = v.astype(BF16)
            for j in range(1, 4):
                copy_rb(h, j).start()

    def plane_sums(kind):
        for h in range(2):
            for j in range(1, 4):
                copy_rb(h, j).wait_recv()
            own = x if h == 0 else y
            got = (in_b0, in_b1)[h]
            v = (half0, half1)[h][own].astype(F32)
            for j in range(3):
                v = v + got[j].astype(F32)
            quarts[kind][h] = v.astype(quarts[kind].dtype)

            @pl.when(z != x + 4 * h)
            def _():
                copy_rz(kind, h).start()

    pair_copy = remote(whole.at[c], whole.at[c], s_pair, r_pair, partner)

    def finish_square(kind):
        src, got = quarts[kind], in_zs[kind]
        for j in range(1, 8):
            remote(src.at[0], got.at[j - 1], s_rz.at[0], r_rz.at[j - 1], partner).wait_recv()
        v = src[h_me].astype(F32)
        for j in range(7):
            v = v + got[j].astype(F32)
        whole[c] = v * scale[c, kp_me]
        pair_copy.start()

    parts = []

    def student(ns):
        for n in ns:
            cols = slice(256 * n, 256 * n + 256)
            l_blk = dot_nt(w_t[...], stu[cols, :]) * (1.0 / STUDENT_TEMP)
            lg[:, cols] = l_blk
            e_blk = jnp.exp(l_blk)
            ex[:, cols] = e_blk
            parts.append(jnp.sum(e_blk, axis=0, keepdims=True))

    def products(kind, src):
        for n in range(2):
            for half in range(3 * n, 3 + 2 * n):
                cols = slice(256 * half, 256 * half + 256)
                p_blk = dot(w_unit[...], src[:, cols].astype(BF16)).astype(BF16)
                for k in range(6):
                    lo, f = 128 * (k // 3), k % 3
                    pt[kind, 6 * half + k] = p_blk[128 * f:128 * f + 128, lo:lo + 128]

            @pl.when(c != kind)
            def _():
                core_piece(n).start()

    sum_start(0, tot)

    @pl.when(c == 0)
    def _():
        spread_planes(0)

    sum_turn(0)

    @pl.when(c == 0)
    def _():
        hand_over(0)

    @pl.when(c == 1)
    def _():
        take_over(0, range(4))

    assemble(0, stu)
    student(range(5))
    sum_start(3, jnp.concatenate(parts, axis=1))

    row = 1.0 / sum_end(0)

    def sweep(i, acc):
        rows = pl.ds(pl.multiple_of(i * BLK, BLK), BLK)
        k_blk = kt[rows, :]
        col = 1.0 / jnp.sum(k_blk * row, axis=1, keepdims=True)
        return acc + fold8(k_blk * col)

    tot = fold1(lax.fori_loop(0, COLS // BLK, sweep, zero8))
    late_start(1, tot)
    products(0, ex)
    late_turn(1)
    sum_turn(3)

    @pl.when(c == 0)
    def _():
        core_sum()

    row = 1.0 / late_end(1)

    def last_sweep(i, acc):
        rows = pl.ds(pl.multiple_of(i * BLK, BLK), BLK)
        k_blk = kt[rows, :]
        col = 1.0 / jnp.sum(k_blk * row, axis=1, keepdims=True)
        k_blk = k_blk * col
        kt[rows, :] = k_blk
        return acc[0] + fold8(k_blk), acc[1] + fold8(k_blk * lg[rows, :])

    acc_k, acc_l = lax.fori_loop(0, COLS // BLK, last_sweep, (zero8, zero8))

    products(1, kt)
    late_start(2, fold1(acc_k))

    @pl.when(c == 0)
    def _():
        line_sums()

    @pl.when(c == 1)
    def _():
        core_sum()

    late_turn(2)
    partition = sum_end(3)

    @pl.when(c == 0)
    def _():
        plane_sums(0)


    @pl.when(c == 1)
    def _():
        line_sums()

    row = 1.0 / late_end(2)
    row_w = jnp.concatenate([jnp.full((1, 128), w, F32) for w in ROW_W], axis=1)
    log_term = jnp.sum(row_w * jnp.log(partition), axis=1, keepdims=True)
    cross = jnp.sum(row_w * row * fold1(acc_l), axis=1, keepdims=True)
    ls_b[xy] = jnp.broadcast_to(cross, (1, 128))

    def ls_a_copy(j):
        return remote(ls_a.at[zc], ls_a.at[zc], s_lsa, r_lsa, zc_peer(j)[0])

    def ls_b_copy(j):
        return remote(ls_b.at[xy], ls_b.at[xy], s_lsb, r_lsb, xy_peer(j))

    for j in range(1, 16):
        ls_b_copy(j).start()
    lead = row_w * (ROWS / STUDENT_TEMP)
    scale_p = lead / partition
    scale_t = lead * row
    for kp in range(10):
        scale[0, kp] = scale_p[:, 128 * kp:128 * kp + 128]
        scale[1, kp] = -scale_t[:, 128 * kp:128 * kp + 128]
    scale[0, 10] = jnp.zeros((1, 128), F32)
    scale[1, 10] = jnp.zeros((1, 128), F32)

    @pl.loop(0, COLS // BLK)
    def _(i):
        rows = pl.ds(pl.multiple_of(i * BLK, BLK), BLK)
        gb[rows, :] = (ex[rows, :] * scale_p - kt[rows, :] * scale_t).astype(BF16)

    @pl.when(c == 1)
    def _():
        plane_sums(1)

    gu = dot(gb[...], stu[...]).T
    w_f = w_unit[...].astype(F32)
    gw_ref[...] = (
        1024.0 * (gu - w_f * jnp.sum(w_f * gu, axis=0, keepdims=True)) / w_norm[...]
    )
    wait_bytes(ls_b.at[pl.ds(0, 15)], r_lsb)
    v = ls_b[0]
    for i in range(1, 16):
        v = v + ls_b[i]
    ls_a[zc] = v
    for j in range(1, 16):
        ls_a_copy(j).start()

    sends_back = is_owner & (o_me < 30)

    def copy_back(i):
        return remote(
            tiles.at[i], back.at[k_me, f_me], s_back, r_back, (2 * i + c, b_me)
        )

    def stays(i):
        return (2 * i + c == img) & (b_me == y)

    @pl.when(is_owner & (c == 0))
    def _():
        finish_square(0)

    @pl.when(is_owner & (c == 1))
    def _():
        finish_square(1)

    @pl.when(is_owner)
    def _():
        remote(whole.at[1 - c], whole.at[1 - c], s_pair, r_pair, partner).wait_recv()

    @pl.when(sends_back)
    def _():
        v = whole[0] + whole[1]
        hi = v.astype(BF16)
        lo = (v - hi.astype(F32)).astype(BF16)
        for q in range(4):
            part_sel = sel[c, 128 * q:128 * q + 128]
            t = dot_nt(part_sel, hi) + dot_nt(part_sel, lo)
            tiles[8 * q:8 * q + 8] = t.reshape(8, 16, 128)
            for i in range(8 * q, 8 * q + 8):
                @pl.when(jnp.logical_not(stays(i)))
                def _():
                    copy_back(i).start()

                @pl.when(stays(i))
                def _():
                    pltpu.make_async_copy(tiles.at[i], back.at[k_me, f_me], r_back).start()

    wait_bytes(ls_a.at[pl.ds(0, 15)], r_lsa)
    v = ls_a[0]
    for i in range(1, 16):
        v = v + ls_a[i]
    loss_ref[...] = log_term - v[:, :1]
    store_loss = pltpu.make_async_copy(loss_ref, loss_hbm, s_loss)
    store_loss.start()

    each_owner(cnt_done, None)
    each_owner(tile_done, None, (0,))

    @pl.when(is_owner)
    def _():
        pair_copy.wait_send()

        @pl.when(c == 0)
        def _():
            for j in range(1, 8):
                z_copy(j).wait_send()

    for h in range(2):
        for j in range(1, 4):
            copy2(h, j).wait_send()
            copy3(h, j).wait_send()
            copy_ra(h, j).wait_send()
            copy_rb(h, j).wait_send()
        for j in range(4):
            copy_ex(h, j, c).wait_send()

        for kind in range(2):
            @pl.when((z != x + 4 * h) & (c == kind))
            def _():
                copy_rz(kind, h).wait_send()

    for k in range(4):
        sum_sent(k)
    wait_bytes(ls_a.at[pl.ds(0, 15)], s_lsa)
    wait_bytes(ls_b.at[pl.ds(0, 15)], s_lsb)
    for n in range(2):
        core_piece(n).wait_send()

    @pl.when(sends_back & (b_me == y))
    def _():
        wait_bytes(tiles.at[pl.ds(0, 31)], s_back)

    @pl.when(sends_back & (b_me != y))
    def _():
        wait_bytes(tiles, s_back)

    for b in range(4):
        @pl.when(y == b)
        def _():
            got = back.at[pl.ds(0, 4 - b)]
            pltpu.make_async_copy(got, got, r_back).wait()
            for k in range(4 - b, 4):
                back[k] = jnp.zeros((3, 16, 128), F32)

    cols = []
    for f in range(3):
        cols.append(back[0, f] + back[1, f] + back[2, f] + back[3, f])
    gx = jnp.concatenate(cols, axis=1)
    u = unit_f[y]
    gr_ref[...] = (gx - u * jnp.sum(u * gx, axis=1, keepdims=True)) / norm_f[y][:, :1]
    store_loss.wait()


def shards(student_feats, teacher_feats, student_weight, teacher_weight, patch_masks):
    vmem = pl.BlockSpec(memory_space=pltpu.VMEM)
    hbm = pl.BlockSpec(memory_space=pltpu.HBM)
    dma = pltpu.SemaphoreType.DMA

    scratch = [
        pltpu.VMEM((1, 128, E), BF16),
        pltpu.VMEM((1, 128, E), BF16),
        pltpu.VMEM((E, COLS), BF16),
        pltpu.VMEM((E, COLS), BF16),
        pltpu.VMEM((1, 128), jnp.int32),
        pltpu.VMEM((1, 1), F32),
        pltpu.VMEM((2, 4, 3, 16, 128), BF16),
        pltpu.VMEM((4, 16, E), F32),
        pltpu.VMEM((4, 16, 128), F32),
        pltpu.VMEM((1, 128), F32),
        pltpu.VMEM((64, 16, 128), BF16),
        pltpu.VMEM((64, 1, 128), F32),
        pltpu.VMEM((2, 512, 128), BF16),
        pltpu.VMEM((2, 32, 128, 128), BF16),
        pltpu.VMEM((ROWS, E), BF16),
        pltpu.VMEM((ROWS, E), BF16),
        pltpu.VMEM((E, COLS), BF16),
        pltpu.VMEM((COLS, E), BF16),
        pltpu.VMEM((COLS, E), BF16),
        pltpu.VMEM((1, COLS), F32),
        pltpu.VMEM((COLS, ROWS), F32),
        pltpu.VMEM((COLS, ROWS), F32),
        pltpu.VMEM((COLS, ROWS), F32),
        pltpu.VMEM((COLS, ROWS), BF16),
        pltpu.VMEM((COLS, 128), F32),
        pltpu.VMEM((4, 2, 1, 640), F32),
        pltpu.VMEM((4, 16, 1, 640), F32),
        pltpu.VMEM((4, 32, 1, 640), F32),
        pltpu.VMEM((16, 1, 128), F32),
        pltpu.VMEM((16, 1, 128), F32),
        pltpu.VMEM((2, 30, 128, 128), BF16),
        pltpu.VMEM((30, 128, 128), BF16),
        pltpu.VMEM((32, 128, 128), BF16),
        pltpu.VMEM((3, 4, 128, 128), BF16),
        pltpu.VMEM((3, 4, 128, 128), BF16),
        pltpu.VMEM((4, 128, 128), BF16),
        pltpu.VMEM((4, 128, 128), BF16),
        pltpu.VMEM((3, 128, 128), BF16),
        pltpu.VMEM((3, 128, 128), BF16),
        pltpu.VMEM((2, 128, 128), F32),
        pltpu.VMEM((2, 128, 128), BF16),
        pltpu.VMEM((7, 128, 128), F32),
        pltpu.VMEM((7, 128, 128), BF16),
        pltpu.VMEM((2, 11, 1, 128), F32),
        pltpu.VMEM((2, 128, 128), F32),
        pltpu.VMEM((32, 16, 128), F32),
        pltpu.VMEM((4, 3, 16, 128), F32),
        dma((16,)), dma((16,)), dma, dma,
        dma((7,)), dma((2,)),
        dma((2, 3)), dma((2, 3)), dma((2, 3)), dma((2, 3)), dma((2, 4)), dma((2, 4)),
        dma((4,)), dma((4,)), dma((4,)), dma((4,)), dma, dma, dma, dma,
        dma((2,)), dma((2,)),
        dma((2, 3)), dma((2, 3)), dma((2, 3)), dma((2, 3)), dma((2,)), dma((7,)),
        dma, dma,
        dma, dma,
        dma((5,)), dma,
        pltpu.SemaphoreType.REGULAR,
    ]
    loss, grad_weight, grad_rows = pl.pallas_call(
        kernel,
        out_shape=(
            jax.ShapeDtypeStruct((1, 1), F32),
            jax.ShapeDtypeStruct((E, COLS), F32),
            jax.ShapeDtypeStruct((16, E), F32),
        ),
        in_specs=[hbm] * 5,
        out_specs=(hbm, vmem, vmem),
        scratch_shapes=scratch,
        compiler_params=pltpu.CompilerParams(
            collective_id=0, has_side_effects=True, vmem_limit_bytes=40 * 2**20
        ),
    )(*(
        pltpu.with_memory_space_constraint(a, pltpu.HBM)
        for a in (student_feats, teacher_feats, student_weight, teacher_weight, patch_masks)
    ))
    return loss.reshape(()), grad_weight, grad_rows


def solution(mesh):
    placed = (
        P("img", None, None),
        P("img", None, None),
        P(None, ("img", "proto")),
        P(None, ("img", "proto")),
        P("img", None),
    )
    return jax.shard_map(
        shards,
        mesh=mesh,
        in_specs=placed,
        out_specs=(P(), P(None, ("img", "proto")), P(("img", "proto"), None)),
        check_vma=False,
    )
```

```python
import jax
import jax.numpy as jnp
from jax import lax
from jax.experimental import pallas as pl
from jax.experimental.pallas import tpu as pltpu
from jax.sharding import PartitionSpec as P

MESH = pl.DeviceIdType.MESH
F32, BF16 = jnp.float32, jnp.bfloat16
TEACHER_TEMP = 0.07
STUDENT_TEMP = 0.1
NORM_EPS = 1e-06
ROWS, COLS, E, ITERS = 1280, 512, 384, 3
BLK = 256
GROUPS = [(b, m) for b in range(4) for m in range(b + 1, 5)]
ROW_W = [1.0 / (16.0 * m * 32.0) for _, m in GROUPS]


def square_at(s):
    y, q = (s // 4, s % 4) if s < 16 else (s % 4, s // 4)
    if q == 7 and y >= 2:
        return 28 + y
    return q + (0, 12, 20, 8)[y] + (15 if y == 3 and q >= 4 else 0)


SPOT_OF = {square_at(s): s for s in range(32)}


def square_on(y, q):
    base = jnp.where(y == 0, 0, jnp.where(y == 1, 12, jnp.where(y == 2, 20, 8)))
    o = q + base + jnp.where((y == 3) & (q >= 4), 15, 0)
    return jnp.where((q == 7) & (y >= 2), 28 + y, o)


def split_square(o):
    kp = lax.div(o, 3)
    f = lax.rem(o, 3)
    b = lax.div(kp + 4, 8) + lax.div(kp + 1, 8) + lax.div(kp, 9)
    first = 4 * b - lax.div(b * (b - 1), 2)
    return kp, f, b, kp - first, kp - first + b + 1


def dot(a, b):
    return jnp.dot(a, b, preferred_element_type=F32)


def dot_nt(a, b):
    return lax.dot_general(a, b, (((1,), (1,)), ((), ())), preferred_element_type=F32)


def fold8(v):
    return jnp.sum(v.reshape(v.shape[0] // 8, 8, v.shape[1]), axis=0)


def kernel(
    sf_hbm, tf_hbm, sw_hbm, tw_hbm, mask_hbm,
    loss_hbm, gw_ref, gr_ref,
    sf, tf, sw, tw, mask, loss_ref,
    units, unit_f, norm_f, cnt, raw, rawc, sel, grid, tea, stu,
    w_unit, w_t, tw_t, w_norm, kt, lg, ex, gb, csum,
    ar_v, ar_a, ar_b, ls_a, ls_b,
    pt, core_in, summed, in_a0, in_a1, half0, half1, in_b0, in_b1, quart_p, quart_t, in_zp, in_zt,
    scale, whole, tiles, back,
    s_raw, s_cnt, r_raw, r_cnt, s_z, r_z, s_2, r_2, s_3, r_3, s_ex, r_ex,
    s_ara, r_ara, s_arb, r_arb, s_lsa, r_lsa, s_lsb, r_lsb, s_core, r_core, s_ra, r_ra, s_rb, r_rb, s_rz, r_rz, s_pair, r_pair, s_back, r_back, s_in, s_loss, turn,
):
    img = lax.axis_index("img")
    y = lax.axis_index("proto")
    c = lax.rem(img, 2)
    z = lax.rem(lax.div(img, 2), 8)
    x = lax.div(img, 16)
    is_owner = lax.rem(z, 4) == x
    h_me = lax.div(z, 4)
    o_me = square_on(y, 4 * h_me + x)
    s_me = jnp.where(h_me == 0, 4 * y + x, 16 + 4 * x + y)

    def at(px, py, pz, pc):
        return ((px * 8 + pz) * 2 + pc, py)

    def x_peer(j):
        return at(lax.rem(x + j, 4), y, z, c)

    def y_peer(j):
        return at(x, lax.rem(y + j, 4), z, c)

    def z_peer(j):
        return at(x, y, lax.rem(z + j, 8), c)

    zc, xy = z * 2 + c, x * 4 + y

    def zc_peer(j):
        g = lax.rem(zc + j, 16)
        return at(x, y, lax.div(g, 2), lax.rem(g, 2)), lax.rem(g, 2)

    def xyc_peer(j):
        g = lax.rem(xy * 2 + c + j, 32)
        return at(lax.div(g, 8), lax.rem(lax.div(g, 2), 4), z, lax.rem(g, 2))

    def xy_peer(j):
        g = lax.rem(xy + j, 16)
        return at(lax.div(g, 4), lax.rem(g, 4), z, c)

    partner = at(x, y, z, 1 - c)

    def remote(src, dst, s, r, dev):
        return pltpu.make_async_remote_copy(
            src_ref=src, dst_ref=dst, send_sem=s, recv_sem=r, device_id=dev, device_id_type=MESH
        )

    loads = [
        pltpu.make_async_copy(src, dst, s_in.at[n])
        for n, (src, dst) in enumerate(
            ((mask_hbm, mask), (tf_hbm, tf), (sf_hbm, sf), (tw_hbm, tw), (sw_hbm, sw))
        )
    ]
    for load in loads:
        load.start()

    bar = pltpu.get_barrier_semaphore()

    def greet(dev):
        pl.semaphore_signal(bar, inc=1, device_id=dev, device_id_type=MESH)

    def hops(n):
        px, pz = n // 16, n // 2 % 8
        return min(px, 4 - px) + min(pz, 8 - pz)

    @pl.when(is_owner)
    def _():
        for n in sorted(range(1, 64), key=hops, reverse=True):
            greet((lax.bitwise_and(img + n, 63), y))

    for j in range(1, 16):
        greet(zc_peer(j)[0])
    for j in range(1, 32):
        greet(xyc_peer(j))


    for load in loads[:3]:
        load.wait()
    mrow = mask[...].astype(F32)
    upper = (
        lax.broadcasted_iota(jnp.int32, (128, 128), 0) <= lax.broadcasted_iota(jnp.int32, (128, 128), 1)
    ).astype(BF16)
    mrow8 = jnp.broadcast_to(mrow, (8, 128))
    rank = dot(mrow8.astype(BF16), upper)
    cnt[...] = jnp.broadcast_to(jnp.sum(mrow, axis=1, keepdims=True), (1, 128))
    want = lax.broadcasted_iota(jnp.int32, (64, 128), 0).astype(F32)
    pick = jnp.where(
        (jnp.broadcast_to(rank[:1], (64, 128)) - 1.0 == want)
        & (jnp.broadcast_to(mrow, (64, 128)) > 0.5), 1.0, 0.0
    ).astype(BF16)

    def unit_rows(kind, feats):
        rows = dot(pick, feats[0])
        norm = jnp.sqrt(jnp.sum(rows * rows, axis=1, keepdims=True) + NORM_EPS)
        unit = (rows / norm).astype(BF16)
        for b in range(4):
            for f in range(3):
                units[kind, b, f] = unit[16 * b:16 * b + 16, 128 * f:128 * f + 128]
        return unit, norm

    s_unit, s_norm = unit_rows(0, sf)
    unit_rows(1, tf)
    for b in range(4):
        unit_f[b] = s_unit[16 * b:16 * b + 16].astype(F32)
        norm_f[b] = jnp.broadcast_to(s_norm[16 * b:16 * b + 16], (16, 128))

    @pl.when(is_owner)
    def _():
        pl.semaphore_wait(bar, 46 + 15)

    @pl.when(jnp.logical_not(is_owner))
    def _():
        pl.semaphore_wait(bar, 46 + 16)

    def each_owner(remote_fn, local_fn, cores=(1, 0)):
        for pc in cores:
            for h in range(2):
                for px in range(4):
                    t = (h * 4 + px) * 2 + pc
                    to = (px * 8 + px + 4 * h) * 2 + pc
                    _, f, b, _, _ = split_square(square_on(y, 4 * h + px))

                    @pl.when(img != to)
                    def _():
                        remote_fn(t, to, pc, b, f)

                    if local_fn is not None:
                        @pl.when(img == to)
                        def _():
                            local_fn(pc, b, f)

    def cnt_copy(t, to, pc, b, f):
        return remote(cnt, rawc.at[img], s_cnt.at[t], r_cnt, (to, y))

    def tile_copy(t, to, pc, b, f):
        return remote(units.at[pc, b, f], raw.at[img], s_raw.at[t], r_raw, (to, y))

    def cnt_start(*a):
        cnt_copy(*a).start()

    def tile_start(*a):
        tile_copy(*a).start()

    def cnt_done(*a):
        cnt_copy(*a).wait_send()

    def tile_done(*a):
        tile_copy(*a).wait_send()

    def cnt_local(pc, b, f):
        pltpu.make_async_copy(cnt, rawc.at[img], r_cnt).start()

    def tile_local(pc, b, f):
        pltpu.make_async_copy(units.at[pc, b, f], raw.at[img], r_raw).start()

    each_owner(cnt_start, cnt_local)
    each_owner(tile_start, tile_local, (1,))

    def unit_columns(w_ref):
        w = w_ref[...].astype(F32)
        norm = jnp.sqrt(jnp.sum(w * w, axis=0, keepdims=True) + NORM_EPS)
        return w / norm, norm

    loads[3].wait()
    tw_u, _ = unit_columns(tw)
    tw_t[...] = tw_u.T.astype(BF16)
    loads[4].wait()
    sw_u, sw_n = unit_columns(sw)
    w_norm[...] = sw_n
    w_unit[...] = sw_u.astype(BF16)
    w_t[...] = sw_u.T.astype(BF16)

    each_owner(tile_done, None, (1,))
    each_owner(tile_start, tile_local, (0,))

    kp_me, f_me, b_me, k_me, m_me = split_square(o_me)

    def z_copy(j):
        return remote(grid.at[c, s_me], grid.at[c, s_me], s_z.at[j - 1], r_z.at[h_me], z_peer(j))

    @pl.when(is_owner)
    def _():
        pltpu.make_async_copy(rawc, rawc, r_cnt).wait()
        counts = rawc[:, 0, :]
        match = jnp.where(counts == (16 * m_me).astype(F32), 1.0, 0.0)
        lower = (
            lax.broadcasted_iota(jnp.int32, (64, 64), 1) < lax.broadcasted_iota(jnp.int32, (64, 64), 0)
        ).astype(BF16)
        place = jnp.where(match > 0.5, dot(lower, match.astype(BF16)), -1.0)
        lane_image = lax.shift_right_logical(lax.broadcasted_iota(jnp.int32, (64, 1024), 1), 4)
        own_image = lane_image == lax.broadcasted_iota(jnp.int32, (64, 1024), 0)
        along = jnp.where(own_image, jnp.broadcast_to(place[:, :1], (64, 1024)), 0.0)
        place_row = dot(jnp.ones((8, 64), BF16), along.astype(BF16))
        sub = lax.broadcasted_iota(jnp.int32, (128, 1024), 0)
        same_row = lax.bitwise_and(sub, 15) == lax.bitwise_and(
            lax.broadcasted_iota(jnp.int32, (128, 1024), 1), 15
        )
        slot_block = lax.shift_right_logical(sub, 4).astype(F32)
        sel_t = jnp.where(
            same_row & (jnp.broadcast_to(place_row[:1], (128, 1024)) == slot_block), 1.0, 0.0
        ).astype(BF16)
        pltpu.make_async_copy(raw, raw, r_raw).wait()
        grid[c, s_me] = dot(sel_t, raw[...].reshape(1024, 128)).astype(BF16)

        @pl.when(c == 0)
        def _():
            pl.semaphore_wait(turn, 1)

        for j in range(1, 8):
            z_copy(j).start()

        lane_block = lax.shift_right_logical(lax.broadcasted_iota(jnp.int32, (64, 128), 1), 4)
        block_sel = jnp.where(place == lane_block.astype(F32), 1.0, 0.0).astype(BF16)
        spread = (
            lax.shift_right_logical(lax.broadcasted_iota(jnp.int32, (1024, 64), 0), 4)
            == lax.broadcasted_iota(jnp.int32, (1024, 64), 1)
        ).astype(BF16)
        same_lane = (
            lax.bitwise_and(lax.broadcasted_iota(jnp.int32, (1024, 128), 0), 15)
            == lax.bitwise_and(lax.broadcasted_iota(jnp.int32, (1024, 128), 1), 15)
        )
        sel_f = jnp.where(same_lane, dot(spread, block_sel), 0.0)
        by_core = sel_f.astype(BF16).reshape(32, 2, 16, 128)
        for core in range(2):
            sel[core] = by_core[:, core].reshape(512, 128)

        @pl.when(c == 1)
        def _():
            for j in range(1, 8):
                z_copy(j).wait_send()
            pl.semaphore_signal(turn, inc=1, device_id=partner, device_id_type=MESH)

    for h in range(2):
        spot = 4 * y + x if h == 0 else 16 + 4 * x + y

        @pl.when(z != x + 4 * h)
        def _():
            remote(grid.at[c, spot], grid.at[c, spot], s_z.at[0], r_z.at[h], partner).wait_recv()

    def copy2(h, j, back_j=0):
        if h == 0:
            spot = 4 * y + lax.rem(x + back_j, 4)
            dev = x_peer(j)
        else:
            spot = 16 + 4 * x + lax.rem(y + back_j, 4)
            dev = y_peer(j)
        return remote(grid.at[c, spot], grid.at[c, spot], s_2.at[h, j - 1], r_2.at[h, j - 1], dev)

    def run4(h, off):
        return pl.ds(4 * lax.rem(y + off, 4), 4) if h == 0 else pl.ds(16 + 4 * lax.rem(x + off, 4), 4)

    def copy3(h, j, back_j=0):
        run = run4(h, back_j)
        dev = y_peer(j) if h == 0 else x_peer(j)
        return remote(grid.at[c, run], grid.at[c, run], s_3.at[h, j - 1], r_3.at[h, j - 1], dev)

    def copy_ex(h, j, kind):
        run = run4(h, (4 - j) % 4)
        return remote(grid.at[kind, run], grid.at[kind, run], s_ex.at[h, j], r_ex.at[h, j], partner)

    def spread_lines():
        for j in range(1, 4):
            copy2(0, j).start()
            copy2(1, j).start()

    def spread_planes(kind):
        for h in range(2):
            for j in range(1, 4):
                copy2(h, j, 4 - j).wait_recv()
            for j in range(1, 4):
                copy3(h, j).start()
        copy_ex(0, 0, kind).start()
        copy_ex(1, 0, kind).start()

    def hand_over(kind):
        for j in range(1, 4):
            for h in range(2):
                copy3(h, j, 4 - j).wait_recv()
                copy_ex(h, j, kind).start()

    def take_over(kind, js):
        for j in js:
            for h in range(2):
                copy_ex(h, j, kind).wait_recv()

    def assemble(kind, feats):
        for o in range(30):
            s, kp, f = SPOT_OF[o], o // 3, o % 3
            feats[128 * kp:128 * kp + 128, 128 * f:128 * f + 128] = grid[kind, s]

    @pl.when(c == 1)
    def _():
        spread_lines()
        spread_planes(1)
        hand_over(1)

    @pl.when(c == 0)
    def _():
        take_over(1, (0, 1))
        spread_lines()
        take_over(1, (2, 3))

    assemble(1, tea)

    for n in range(5):
        cols = slice(256 * n, 256 * n + 256)
        k_blk = jnp.exp(dot_nt(tw_t[...], tea[cols, :]) * (1.0 / TEACHER_TEMP))
        kt[:, cols] = k_blk
        part = k_blk[:, :128] + k_blk[:, 128:]
        csum[...] = part if n == 0 else csum[...] + part
    zero8 = jnp.zeros((8, ROWS), F32)

    def first_sweep(i, acc):
        rows = pl.ds(pl.multiple_of(i * BLK, BLK), BLK)
        col = 1.0 / jnp.sum(csum[rows, :], axis=1, keepdims=True)
        return acc + fold8(kt[rows, :] * col)

    def fold1(acc):
        return jnp.sum(acc, axis=0, keepdims=True)

    tot = fold1(lax.fori_loop(0, COLS // BLK, first_sweep, zero8))

    def ar_a_copy(k, j):
        dev, half = zc_peer(j)
        return remote(ar_v.at[k, half], ar_a.at[k, zc], s_ara.at[k], r_ara.at[k], dev)

    def ar_b_copy(k, j):
        ref = ar_b.at[k, c * 16 + xy]
        return remote(ref, ref, s_arb.at[k], r_arb.at[k], xyc_peer(j))

    def wait_bytes(ref, sem):
        pltpu.make_async_copy(ref, ref, sem).wait()

    def sum_start(k, v):
        ar_v[k, 0] = v[:, :640]
        ar_v[k, 1] = v[:, 640:]
        for j in range(1, 16):
            ar_a_copy(k, j).start()
        ar_a[k, zc] = ar_v[k, c]

    def sum_turn(k):
        wait_bytes(ar_a.at[k, pl.ds(0, 15)], r_ara.at[k])
        v = ar_a[k, 0]
        for i in range(1, 16):
            v = v + ar_a[k, i]
        ar_b[k, c * 16 + xy] = v
        for j in range(1, 32):
            ar_b_copy(k, j).start()

    def sum_end(k):
        wait_bytes(ar_b.at[k, pl.ds(0, 31)], r_arb.at[k])
        halves = []
        for half in range(2):
            v = ar_b[k, half * 16]
            for i in range(1, 16):
                v = v + ar_b[k, half * 16 + i]
            halves.append(v)
        return jnp.concatenate(halves, axis=1)

    def late_a_copy(k, j):
        half = lax.rem(xy * 2 + c + j, 2)
        return remote(
            ar_v.at[k, half], ar_b.at[k, xy * 2 + c], s_arb.at[k], r_arb.at[k], xyc_peer(j)
        )

    def late_b_copy(k, j):
        ref = ar_a.at[k, c * 8 + z]
        return remote(ref, ref, s_ara.at[k], r_ara.at[k], zc_peer(j)[0])

    def late_start(k, v):
        ar_v[k, 0] = v[:, :640]
        ar_v[k, 1] = v[:, 640:]
        for j in range(1, 32):
            late_a_copy(k, j).start()
        ar_b[k, xy * 2 + c] = ar_v[k, c]

    def late_turn(k):
        wait_bytes(ar_b.at[k, pl.ds(0, 31)], r_arb.at[k])
        v = ar_b[k, 0]
        for i in range(1, 32):
            v = v + ar_b[k, i]
        ar_a[k, c * 8 + z] = v
        for j in range(1, 16):
            late_b_copy(k, j).start()

    def late_end(k):
        wait_bytes(ar_a.at[k, pl.ds(0, 15)], r_ara.at[k])
        halves = []
        for half in range(2):
            v = ar_a[k, half * 8]
            for i in range(1, 8):
                v = v + ar_a[k, half * 8 + i]
            halves.append(v)
        return jnp.concatenate(halves, axis=1)

    def sum_sent(k):
        wait_bytes(ar_a.at[k, pl.ds(0, 15)], s_ara.at[k])
        wait_bytes(ar_b.at[k, pl.ds(0, 31)], s_arb.at[k])

    def core_piece(n):
        run = pl.ds(18 * n, 18 - 6 * n)
        return remote(pt.at[1 - c, run], core_in.at[run], s_core.at[n], r_core.at[n], partner)

    def copy_ra(h, j):
        run = run4(h, j)
        dst = (in_a0, in_a1)[h]
        dev = y_peer(j) if h == 0 else x_peer(j)
        return remote(summed.at[run], dst.at[j - 1], s_ra.at[h, j - 1], r_ra.at[h, j - 1], dev)

    def copy_rb(h, j):
        src = (half0, half1)[h]
        dst = (in_b0, in_b1)[h]
        dev = x_peer(j) if h == 0 else y_peer(j)
        spot = lax.rem((x if h == 0 else y) + j, 4)
        return remote(src.at[spot], dst.at[j - 1], s_rb.at[h, j - 1], r_rb.at[h, j - 1], dev)

    quarts, in_zs = (quart_p, quart_t), (in_zp, in_zt)

    def copy_rz(kind, h):
        away = lax.rem(x + 4 * h - z + 8, 8)
        slot = jnp.maximum(away - 1, 0)
        return remote(
            quarts[kind].at[h], in_zs[kind].at[slot], s_rz.at[h], r_rz.at[slot],
            at(x, y, x + 4 * h, c),
        )

    def core_sum():
        for s in (SPOT_OF[30], SPOT_OF[31]):
            summed[s] = jnp.zeros((128, 128), BF16)
        for n in range(2):
            core_piece(n).wait_recv()
            for o in range(18 * n, 18 + 12 * n):
                v = pt[c, o].astype(F32) + core_in[o].astype(F32)
                summed[SPOT_OF[o]] = v.astype(BF16)
        for j in range(1, 4):
            copy_ra(0, j).start()
            copy_ra(1, j).start()

    def line_sums():
        for h in range(2):
            for j in range(1, 4):
                copy_ra(h, j).wait_recv()
            own = run4(h, 0)
            got = (in_a0, in_a1)[h]
            v = summed[own].astype(F32)
            for j in range(3):
                v = v + got[j].astype(F32)
            (half0, half1)[h][...] = v.astype(BF16)
            for j in range(1, 4):
                copy_rb(h, j).start()

    def plane_sums(kind):
        for h in range(2):
            for j in range(1, 4):
                copy_rb(h, j).wait_recv()
            own = x if h == 0 else y
            got = (in_b0, in_b1)[h]
            v = (half0, half1)[h][own].astype(F32)
            for j in range(3):
                v = v + got[j].astype(F32)
            quarts[kind][h] = v.astype(quarts[kind].dtype)

            @pl.when(z != x + 4 * h)
            def _():
                copy_rz(kind, h).start()

    pair_copy = remote(whole.at[c], whole.at[c], s_pair, r_pair, partner)

    def finish_square(kind):
        src, got = quarts[kind], in_zs[kind]
        for j in range(1, 8):
            remote(src.at[0], got.at[j - 1], s_rz.at[0], r_rz.at[j - 1], partner).wait_recv()
        v = src[h_me].astype(F32)
        for j in range(7):
            v = v + got[j].astype(F32)
        whole[c] = v * scale[c, kp_me]
        pair_copy.start()

    parts = []

    def student(ns):
        for n in ns:
            cols = slice(256 * n, 256 * n + 256)
            l_blk = dot_nt(w_t[...], stu[cols, :]) * (1.0 / STUDENT_TEMP)
            lg[:, cols] = l_blk
            e_blk = jnp.exp(l_blk)
            ex[:, cols] = e_blk
            parts.append(jnp.sum(e_blk, axis=0, keepdims=True))

    def products(kind, src):
        for n in range(2):
            for half in range(3 * n, 3 + 2 * n):
                cols = slice(256 * half, 256 * half + 256)
                p_blk = dot(w_unit[...], src[:, cols].astype(BF16)).astype(BF16)
                for k in range(6):
                    lo, f = 128 * (k // 3), k % 3
                    pt[kind, 6 * half + k] = p_blk[128 * f:128 * f + 128, lo:lo + 128]

            @pl.when(c != kind)
            def _():
                core_piece(n).start()

    sum_start(0, tot)

    @pl.when(c == 0)
    def _():
        spread_planes(0)

    sum_turn(0)

    @pl.when(c == 0)
    def _():
        hand_over(0)

    @pl.when(c == 1)
    def _():
        take_over(0, range(4))

    assemble(0, stu)
    student(range(5))
    sum_start(3, jnp.concatenate(parts, axis=1))

    row = 1.0 / sum_end(0)

    def sweep(i, acc):
        rows = pl.ds(pl.multiple_of(i * BLK, BLK), BLK)
        k_blk = kt[rows, :]
        col = 1.0 / jnp.sum(k_blk * row, axis=1, keepdims=True)
        return acc + fold8(k_blk * col)

    tot = fold1(lax.fori_loop(0, COLS // BLK, sweep, zero8))
    late_start(1, tot)
    products(0, ex)
    late_turn(1)
    sum_turn(3)

    @pl.when(c == 0)
    def _():
        core_sum()

    row = 1.0 / late_end(1)

    def last_sweep(i, acc):
        rows = pl.ds(pl.multiple_of(i * BLK, BLK), BLK)
        k_blk = kt[rows, :]
        col = 1.0 / jnp.sum(k_blk * row, axis=1, keepdims=True)
        k_blk = k_blk * col
        kt[rows, :] = k_blk
        return acc[0] + fold8(k_blk), acc[1] + fold8(k_blk * lg[rows, :])

    acc_k, acc_l = lax.fori_loop(0, COLS // BLK, last_sweep, (zero8, zero8))

    products(1, kt)
    late_start(2, fold1(acc_k))

    @pl.when(c == 0)
    def _():
        line_sums()

    @pl.when(c == 1)
    def _():
        core_sum()

    late_turn(2)
    partition = sum_end(3)

    @pl.when(c == 0)
    def _():
        plane_sums(0)


    @pl.when(c == 1)
    def _():
        line_sums()

    row = 1.0 / late_end(2)
    row_w = jnp.concatenate([jnp.full((1, 128), w, F32) for w in ROW_W], axis=1)
    log_term = jnp.sum(row_w * jnp.log(partition), axis=1, keepdims=True)
    cross = jnp.sum(row_w * row * fold1(acc_l), axis=1, keepdims=True)
    ls_b[xy] = jnp.broadcast_to(cross, (1, 128))

    def ls_a_copy(j):
        return remote(ls_a.at[zc], ls_a.at[zc], s_lsa, r_lsa, zc_peer(j)[0])

    def ls_b_copy(j):
        return remote(ls_b.at[xy], ls_b.at[xy], s_lsb, r_lsb, xy_peer(j))

    for j in range(1, 16):
        ls_b_copy(j).start()
    lead = row_w * (ROWS / STUDENT_TEMP)
    scale_p = lead / partition
    scale_t = lead * row
    for kp in range(10):
        scale[0, kp] = scale_p[:, 128 * kp:128 * kp + 128]
        scale[1, kp] = -scale_t[:, 128 * kp:128 * kp + 128]
    scale[0, 10] = jnp.zeros((1, 128), F32)
    scale[1, 10] = jnp.zeros((1, 128), F32)

    @pl.loop(0, COLS // BLK)
    def _(i):
        rows = pl.ds(pl.multiple_of(i * BLK, BLK), BLK)
        gb[rows, :] = (ex[rows, :] * scale_p - kt[rows, :] * scale_t).astype(BF16)

    @pl.when(c == 1)
    def _():
        plane_sums(1)

    gu = dot(gb[...], stu[...]).T
    w_f = w_unit[...].astype(F32)
    gw_ref[...] = (
        1024.0 * (gu - w_f * jnp.sum(w_f * gu, axis=0, keepdims=True)) / w_norm[...]
    )
    wait_bytes(ls_b.at[pl.ds(0, 15)], r_lsb)
    v = ls_b[0]
    for i in range(1, 16):
        v = v + ls_b[i]
    ls_a[zc] = v
    for j in range(1, 16):
        ls_a_copy(j).start()

    sends_back = is_owner & (o_me < 30)

    def copy_back(i):
        return remote(
            tiles.at[i], back.at[k_me, f_me], s_back, r_back, (2 * i + c, b_me)
        )

    def stays(i):
        return (2 * i + c == img) & (b_me == y)

    @pl.when(is_owner & (c == 0))
    def _():
        finish_square(0)

    @pl.when(is_owner & (c == 1))
    def _():
        finish_square(1)

    @pl.when(is_owner)
    def _():
        remote(whole.at[1 - c], whole.at[1 - c], s_pair, r_pair, partner).wait_recv()

    @pl.when(sends_back)
    def _():
        v = whole[0] + whole[1]
        hi = v.astype(BF16)
        lo = (v - hi.astype(F32)).astype(BF16)
        for q in range(4):
            part_sel = sel[c, 128 * q:128 * q + 128]
            t = dot_nt(part_sel, hi) + dot_nt(part_sel, lo)
            tiles[8 * q:8 * q + 8] = t.reshape(8, 16, 128)
            for i in range(8 * q, 8 * q + 8):
                @pl.when(jnp.logical_not(stays(i)))
                def _():
                    copy_back(i).start()

                @pl.when(stays(i))
                def _():
                    pltpu.make_async_copy(tiles.at[i], back.at[k_me, f_me], r_back).start()

    wait_bytes(ls_a.at[pl.ds(0, 15)], r_lsa)
    v = ls_a[0]
    for i in range(1, 16):
        v = v + ls_a[i]
    loss_ref[...] = log_term - v[:, :1]
    store_loss = pltpu.make_async_copy(loss_ref, loss_hbm, s_loss)
    store_loss.start()

    each_owner(cnt_done, None)
    each_owner(tile_done, None, (0,))

    @pl.when(is_owner)
    def _():
        pair_copy.wait_send()

        @pl.when(c == 0)
        def _():
            for j in range(1, 8):
                z_copy(j).wait_send()

    for h in range(2):
        for j in range(1, 4):
            copy2(h, j).wait_send()
            copy3(h, j).wait_send()
            copy_ra(h, j).wait_send()
            copy_rb(h, j).wait_send()
        for j in range(4):
            copy_ex(h, j, c).wait_send()

        for kind in range(2):
            @pl.when((z != x + 4 * h) & (c == kind))
            def _():
                copy_rz(kind, h).wait_send()

    for k in range(4):
        sum_sent(k)
    wait_bytes(ls_a.at[pl.ds(0, 15)], s_lsa)
    wait_bytes(ls_b.at[pl.ds(0, 15)], s_lsb)
    for n in range(2):
        core_piece(n).wait_send()

    @pl.when(sends_back & (b_me == y))
    def _():
        wait_bytes(tiles.at[pl.ds(0, 31)], s_back)

    @pl.when(sends_back & (b_me != y))
    def _():
        wait_bytes(tiles, s_back)

    for b in range(4):
        @pl.when(y == b)
        def _():
            got = back.at[pl.ds(0, 4 - b)]
            pltpu.make_async_copy(got, got, r_back).wait()
            for k in range(4 - b, 4):
                back[k] = jnp.zeros((3, 16, 128), F32)

    cols = []
    for f in range(3):
        cols.append(back[0, f] + back[1, f] + back[2, f] + back[3, f])
    gx = jnp.concatenate(cols, axis=1)
    u = unit_f[y]
    gr_ref[...] = (gx - u * jnp.sum(u * gx, axis=1, keepdims=True)) / norm_f[y][:, :1]
    store_loss.wait()


def shards(student_feats, teacher_feats, student_weight, teacher_weight, patch_masks):
    vmem = pl.BlockSpec(memory_space=pltpu.VMEM)
    hbm = pl.BlockSpec(memory_space=pltpu.HBM)
    dma = pltpu.SemaphoreType.DMA

    scratch = [
        pltpu.VMEM((1, 128, E), BF16),
        pltpu.VMEM((1, 128, E), BF16),
        pltpu.VMEM((E, COLS), BF16),
        pltpu.VMEM((E, COLS), BF16),
        pltpu.VMEM((1, 128), jnp.int32),
        pltpu.VMEM((1, 1), F32),
        pltpu.VMEM((2, 4, 3, 16, 128), BF16),
        pltpu.VMEM((4, 16, E), F32),
        pltpu.VMEM((4, 16, 128), F32),
        pltpu.VMEM((1, 128), F32),
        pltpu.VMEM((64, 16, 128), BF16),
        pltpu.VMEM((64, 1, 128), F32),
        pltpu.VMEM((2, 512, 128), BF16),
        pltpu.VMEM((2, 32, 128, 128), BF16),
        pltpu.VMEM((ROWS, E), BF16),
        pltpu.VMEM((ROWS, E), BF16),
        pltpu.VMEM((E, COLS), BF16),
        pltpu.VMEM((COLS, E), BF16),
        pltpu.VMEM((COLS, E), BF16),
        pltpu.VMEM((1, COLS), F32),
        pltpu.VMEM((COLS, ROWS), F32),
        pltpu.VMEM((COLS, ROWS), F32),
        pltpu.VMEM((COLS, ROWS), F32),
        pltpu.VMEM((COLS, ROWS), BF16),
        pltpu.VMEM((COLS, 128), F32),
        pltpu.VMEM((4, 2, 1, 640), F32),
        pltpu.VMEM((4, 16, 1, 640), F32),
        pltpu.VMEM((4, 32, 1, 640), F32),
        pltpu.VMEM((16, 1, 128), F32),
        pltpu.VMEM((16, 1, 128), F32),
        pltpu.VMEM((2, 30, 128, 128), BF16),
        pltpu.VMEM((30, 128, 128), BF16),
        pltpu.VMEM((32, 128, 128), BF16),
        pltpu.VMEM((3, 4, 128, 128), BF16),
        pltpu.VMEM((3, 4, 128, 128), BF16),
        pltpu.VMEM((4, 128, 128), BF16),
        pltpu.VMEM((4, 128, 128), BF16),
        pltpu.VMEM((3, 128, 128), BF16),
        pltpu.VMEM((3, 128, 128), BF16),
        pltpu.VMEM((2, 128, 128), F32),
        pltpu.VMEM((2, 128, 128), BF16),
        pltpu.VMEM((7, 128, 128), F32),
        pltpu.VMEM((7, 128, 128), BF16),
        pltpu.VMEM((2, 11, 1, 128), F32),
        pltpu.VMEM((2, 128, 128), F32),
        pltpu.VMEM((32, 16, 128), F32),
        pltpu.VMEM((4, 3, 16, 128), F32),
        dma((16,)), dma((16,)), dma, dma,
        dma((7,)), dma((2,)),
        dma((2, 3)), dma((2, 3)), dma((2, 3)), dma((2, 3)), dma((2, 4)), dma((2, 4)),
        dma((4,)), dma((4,)), dma((4,)), dma((4,)), dma, dma, dma, dma,
        dma((2,)), dma((2,)),
        dma((2, 3)), dma((2, 3)), dma((2, 3)), dma((2, 3)), dma((2,)), dma((7,)),
        dma, dma,
        dma, dma,
        dma((5,)), dma,
        pltpu.SemaphoreType.REGULAR,
    ]
    loss, grad_weight, grad_rows = pl.pallas_call(
        kernel,
        out_shape=(
            jax.ShapeDtypeStruct((1, 1), F32),
            jax.ShapeDtypeStruct((E, COLS), F32),
            jax.ShapeDtypeStruct((16, E), F32),
        ),
        in_specs=[hbm] * 5,
        out_specs=(hbm, vmem, vmem),
        scratch_shapes=scratch,
        compiler_params=pltpu.CompilerParams(
            collective_id=0, has_side_effects=True, vmem_limit_bytes=40 * 2**20
        ),
    )(*(
        pltpu.with_memory_space_constraint(a, pltpu.HBM)
        for a in (student_feats, teacher_feats, student_weight, teacher_weight, patch_masks)
    ))
    return loss.reshape(()), grad_weight, grad_rows


def solution(mesh):
    placed = (
        P("img", None, None),
        P("img", None, None),
        P(None, ("img", "proto")),
        P(None, ("img", "proto")),
        P("img", None),
    )
    return jax.shard_map(
        shards,
        mesh=mesh,
        in_specs=placed,
        out_specs=(P(), P(None, ("img", "proto")), P(("img", "proto"), None)),
        check_vma=False,
    )
```
